32 devices in a mesh: batch: 8 (over z, y), head: 4 (over x, core).
Axes of the slice: x: 2, y: 2, z: 4, core: 2. Of those that a mesh axis runs over, the one named last changes fastest.
Arguments:
- tokens: bfloat16 [16384, 768], P(('batch', 'head')), may hold values from -6 to 6
- cotangent: bfloat16 [16384, 768], P(('batch', 'head')), may hold values from -6 to 6
- lengths: int32 [32], P('batch'), may hold values from 16 to 512, as said below
- labels: int32 [32], P('batch'), may hold values from 0 to 2
- w_qkv: bfloat16 [768, 2304], replicated, may hold values from -0.21875 to 0.21875
- w_out: bfloat16 [768, 768], replicated, may hold values from -0.875 to 0.875
- w_up: bfloat16 [768, 3072], replicated, may hold values from -0.21875 to 0.21875
- w_down: bfloat16 [3072, 768], replicated, may hold values from -0.109375 to 0.109375
- w_pool: bfloat16 [768, 768], replicated, may hold values from -0.21875 to 0.21875
- w_class: bfloat16 [3, 768], replicated, may hold values from -0.625 to 0.625
- biases: float32 [7, 768], replicated, may hold values from -3 to 3
- norm_gains: float32 [2, 768], replicated, may hold values from 0.25 to 1.75
- bias_up: float32 [3072], replicated, may hold values from -3 to 3
Outputs:
- out: bfloat16 [16384, 768], P(('batch', 'head'))
- grad_tokens: bfloat16 [16384, 768], P(('batch', 'head'))
- losses: float32 [32], P(('batch', 'head'))
- g_qkv: float32 [768, 2304], P(None, ('batch', 'head'))
- g_out: float32 [768, 768], P(None, ('batch', 'head'))
- g_up: float32 [768, 3072], P(None, ('batch', 'head'))
- g_down: float32 [3072, 768], P(None, ('batch', 'head'))
- g_pool: float32 [768, 768], P(None, ('batch', 'head'))
- g_class: float32 [3, 768], P(None, ('batch', 'head'))
- g_biases: float32 [6, 768], P(None, ('batch', 'head'))
- g_gains: float32 [2, 768], P(None, ('batch', 'head'))
- g_bias_up: float32 [3072], P(('batch', 'head'))
- g_pool_bias: float32 [768], P(('batch', 'head'))
The draws below stay inside these ranges and needn't reach their ends.
Inputs may be any that keep to these rules, and one draw needn't show every extreme that they name: `lengths`: some sequence has exactly 512 and some exactly 16 positions.
All inputs are finite; a program needn't handle non-finite values.
Results may differ from the reference program's by a relative error of at most 0.014.
Values may be sent and summed in bfloat16 or wider, within the bound.
A program may use at most 192 MiB of HBM per device.

```python
import jax
import jax.numpy as jnp
from jax import lax

D = 768
HEADS = 12
HEAD_DIM = 64
FF = 3072
CLASSES = 3
SLOT = 512
LEN_MIN = 16
SEQ_DEV = 1
SEQS = 32
TOKENS = 16384
N_HEAD = 4


def draw_lengths(key, part):
    drawn = jax.random.randint(key, (SEQS,), LEN_MIN, SLOT + 1).astype(jnp.int32)
    return drawn.at[0].set(SLOT).at[1].set(LEN_MIN)


def set_ends(values, own_key, low, high):
    spot = [jax.random.randint(jax.random.fold_in(own_key, axis), (), 0, length) for axis, length in enumerate(values.shape)]
    widest = values.shape.index(max(values.shape))
    next_to = spot[:widest] + [(spot[widest] + 1) % values.shape[widest]] + spot[widest + 1:]
    return values.at[tuple(spot)].set(low).at[tuple(next_to)].set(high)


def spiked(values, own_key, source, target, parts, factor):
    def block_of(axis_at):
        return (jnp.arange(values.shape[axis_at]) // (values.shape[axis_at] // parts)).reshape((-1,) + (1,) * (values.ndim - 1 - axis_at))

    one_side = jax.random.permutation(own_key, parts)[block_of(target)]
    second = (block_of(target) + parts // 2) % parts
    return jnp.where((block_of(source) == one_side) | (block_of(source) == second), factor * values, values)


def block_levels(own_key, extent, split, least, high):
    loudness, own = 1.0, jax.random.fold_in(own_key, 6)
    for position, blocks in split:
        steps = jnp.exp(jax.random.uniform(jax.random.fold_in(own, position), (blocks,), jnp.float32, least / len(split), high / len(split)))
        loudness = loudness * jnp.repeat(steps, extent[position] // blocks).reshape([-1 if axis == position else 1 for axis in range(len(extent))])
    return loudness


def centred(rng, extent, width, limit, shards=(), dtype=jnp.bfloat16):
    array = jax.random.normal(rng, extent, jnp.float32) * width
    if len(shards) > 0:
        array = block_levels(rng, extent, shards, -0.22, 0.18) * array
    return jnp.clip(array, min=-limit, max=limit).astype(dtype)


def bell_draw_with(own_key, shape, width, bound, shards, heavy, kind=jnp.bfloat16):
    result = width * jax.random.normal(own_key, shape, jnp.float32)
    if shards:
        result = result * block_levels(own_key, shape, shards, -0.22, 0.18)
    return jnp.clip(spiked(result, jax.random.fold_in(own_key, 3), *heavy), -bound, bound).astype(kind)


def setup_inputs(seed: int = 0) -> dict:
    splits = jax.random.split(jax.random.key(seed), 14)
    return {
        "tokens": centred(splits[0], (TOKENS, D), 1.0, 6.0, ((0, 32),)),
        "cotangent": bell_draw_with(splits[1], (TOKENS, D), 1.0, 6.0, ((0, 32),), (0, 1, 32, 2.75)),
        "lengths": draw_lengths(jax.random.fold_in(splits[13], 71), 0),
        "labels": set_ends(jax.random.randint(splits[3], (SEQS,), 0, CLASSES), jax.random.fold_in(splits[3], 1), 0, CLASSES - 1).astype(jnp.int32),
        "w_qkv": centred(splits[4], (D, 3 * D), D ** -0.5, 0.21875),
        "w_out": centred(splits[5], (D, D), (D // 16) ** -0.5, 0.875),
        "w_up": centred(splits[6], (D, FF), D ** -0.5, 0.21875),
        "w_down": centred(splits[7], (FF, D), FF ** -0.5, 0.109375),
        "w_pool": centred(splits[8], (D, D), D ** -0.5, 0.21875),
        "w_class": centred(splits[9], (CLASSES, D), (D // 8) ** -0.5, 0.625),
        "biases": centred(splits[10], (7, D), 0.5, 3.0, (), jnp.float32),
        "norm_gains": jnp.clip(1.0 + 0.15 * jax.random.normal(splits[11], (2, D), jnp.float32), 0.25, 1.75),
        "bias_up": centred(splits[12], (FF,), 0.5, 3.0, (), jnp.float32),
    }


@jax.custom_vjp
def low(v):
    return lax.optimization_barrier(v.astype(jnp.bfloat16)).astype(jnp.float32)

@jax.custom_vjp
def low_back(v):
    return v

def low_keep(v):
    return (low(v), None)

def low_pass(kept, grad):
    return (grad,)

def back_keep(v):
    return (v, None)

def back_low(kept, grad):
    return (low(grad),)
low.defvjp(low_keep, low_pass)
low_back.defvjp(back_keep, back_low)

def matmul(left, right):
    return jnp.dot(left, right, precision=lax.Precision.HIGHEST, preferred_element_type=jnp.float32)

def layer_norm(hidden, gain, shift):
    center = hidden - lax.optimization_barrier(jnp.mean(hidden, axis=-1, keepdims=True))
    spread = lax.optimization_barrier(jnp.mean(center * center, axis=-1, keepdims=True))
    return center * lax.rsqrt(spread + 1e-12) * gain + shift

def attend_one(group_item):
    packed, length = group_item
    queries = packed[:, 0]
    keys_all = packed[:, 1]
    values = packed[:, 2]
    scores = jnp.einsum('qhd,khd->hqk', queries, keys_all, precision=lax.Precision.HIGHEST) * HEAD_DIM ** (-0.5)
    scores = low_back(scores)
    allowed = jnp.arange(SLOT) < length
    scores = jnp.where(allowed[None, None, :], scores, -1e+30)
    weights = jax.nn.softmax(scores, axis=-1)
    return jnp.einsum('hqk,khd->qhd', low(weights), values, precision=lax.Precision.HIGHEST)

def group_forward(params, inputs, seq_lengths, seq_labels):
    w_qkv, w_out, w_up, w_down, w_pool, w_class, biases, norm_gains, bias_up = params
    seq_count = inputs.shape[0] // SLOT
    zeros_key = jnp.zeros((D,), jnp.float32)
    packed = matmul(inputs, w_qkv) + jnp.concatenate([biases[0], zeros_key, biases[1]])
    packed = low(low_back(packed)).reshape(seq_count, SLOT, 3, HEADS, HEAD_DIM)
    context = lax.map(jax.checkpoint(attend_one), (packed, seq_lengths))
    context = low(low_back(context.reshape(seq_count * SLOT, D)))
    attn = low_back(matmul(context, w_out) + biases[2])
    norm_one = layer_norm(inputs + attn, norm_gains[0], biases[3])
    hidden_up = low_back(matmul(low(norm_one), w_up) + bias_up)
    activated = low(jax.nn.gelu(hidden_up, approximate=False))
    branch = low_back(matmul(activated, w_down) + biases[4])
    outputs = layer_norm(norm_one + branch, norm_gains[1], biases[5])
    leading = low(outputs.reshape(seq_count, SLOT, D)[:, 0])
    pooled = jnp.tanh(matmul(leading, w_pool) + biases[6])
    logits = matmul(low(pooled), w_class.T)
    chosen = lax.optimization_barrier(jnp.sum(jnp.where(jnp.arange(CLASSES)[None, :] == seq_labels[:, None], logits, 0.0), axis=-1))
    losses = jax.nn.logsumexp(logits, axis=-1) - chosen
    return (outputs, losses)

def reference(tokens, cotangent, lengths, labels, w_qkv, w_out, w_up, w_down, w_pool, w_class, biases, norm_gains, bias_up):
    params = tuple((weight.astype(jnp.float32) for weight in (w_qkv, w_out, w_up, w_down, w_pool, w_class, biases, norm_gains, bias_up)))
    group_seqs = SEQ_DEV * N_HEAD
    group_rows = group_seqs * SLOT
    group_count = lengths.shape[0] // group_seqs
    scan_items = (tokens.reshape(group_count, group_rows, D), cotangent.reshape(group_count, group_rows, D), lengths.reshape(group_count, group_seqs), labels.reshape(group_count, group_seqs))

    def advance(running, group_item):
        token_grp, cot_grp, len_grp, lab_grp = group_item
        inputs = token_grp.astype(jnp.float32)
        slot_live = (jnp.arange(SLOT)[None, :] < len_grp[:, None]).reshape(group_rows)
        seed_grad = cot_grp.astype(jnp.float32) * slot_live[:, None].astype(jnp.float32)

        def forward(param_set, values):
            return group_forward(param_set, values, len_grp, lab_grp)
        (outputs, losses), pullback = jax.vjp(forward, params, inputs)
        grad_params, grad_inputs = pullback((seed_grad, jnp.ones_like(losses)))
        running = jax.tree.map(jnp.add, running, grad_params)
        return (running, (outputs.astype(jnp.bfloat16), grad_inputs.astype(jnp.bfloat16), losses.astype(jnp.float32)))
    zero_grads = jax.tree.map(jnp.zeros_like, params)
    totals, (outs_all, grads_all, loss_all) = lax.scan(advance, zero_grads, scan_items)
    return (outs_all.reshape(-1, D), grads_all.reshape(-1, D), loss_all.reshape(-1), totals[0], totals[1], totals[2], totals[3], totals[4], totals[5], totals[6][:6], totals[7], totals[8], totals[6][6])
```

```python
import functools

import jax
import jax.numpy as jnp
from jax import lax
from jax.experimental import pallas as pl
from jax.experimental.pallas import tpu as pltpu
from jax.sharding import PartitionSpec as P

D = 768
HEADS = 12
HEAD_DIM = 64
FF = 3072
CLASSES = 3
SLOT = 512
MESH = pl.DeviceIdType.MESH
LOW = jnp.bfloat16
F32 = jnp.float32


def layer_norm(hidden, gain, shift):
    center = hidden - jnp.mean(hidden, axis=-1, keepdims=True)
    spread = jnp.mean(center * center, axis=-1, keepdims=True)
    return center * lax.rsqrt(spread + 1e-12) * gain + shift


def exact_gelu(hidden):
    return jax.nn.gelu(hidden, approximate=False)


def inner(left, right):
    return lax.dot_general(
        left, right, (((0,), (0,)), ((), ())), preferred_element_type=jnp.float32
    )


def against(left, right):
    return lax.dot_general(
        left, right, (((1,), (1,)), ((), ())), preferred_element_type=jnp.float32
    )


def exact(left, right):
    return jnp.dot(left, right, precision=lax.Precision.HIGHEST, preferred_element_type=jnp.float32)


class Place:
    def __init__(self, rest):
        batch = lax.axis_index("batch")
        head = lax.axis_index("head")
        self.rest = rest
        self.z = batch // 2
        self.y = lax.rem(batch, 2)
        self.x = head // 2
        self.c = lax.rem(head, 2)

    def device(self, z, y, x, c):
        return (z * 2 + y, x * 2 + c)

    def core_peer(self):
        return self.device(self.z, self.y, self.x, 1 - self.c)

    def x_peer(self):
        return self.device(self.z, self.y, 1 - self.x, self.c)

    def y_peer(self):
        return self.device(self.z, 1 - self.y, self.x, self.c)

    def z_at(self, offset):
        return lax.rem(self.z + offset, self.rest)

    def z_peer(self, offset):
        return self.device(self.z_at(offset), self.y, self.x, self.c)

    def barrier(self):
        sem = pltpu.get_barrier_semaphore()
        for peer in (self.core_peer(), self.x_peer(), self.y_peer()):
            pl.semaphore_signal(sem, inc=1, device_id=peer, device_id_type=MESH)
        for offset in range(1, self.rest):
            pl.semaphore_signal(sem, inc=1, device_id=self.z_peer(offset), device_id_type=MESH)
        pl.semaphore_wait(sem, 3 + self.rest - 1)


def remote(src, dst, send, recv, peer):
    return pltpu.make_async_remote_copy(
        src_ref=src, dst_ref=dst, send_sem=send, recv_sem=recv, device_id=peer, device_id_type=MESH
    )


class Reduce:
    def __init__(self, place, part, bufs, sems, x_first):
        self.place, self.part, self.x_first = place, part, x_first
        self.r1, self.r2, self.r3, self.r4 = bufs
        send, recv, zsend, zrecv = sems
        p = place
        if x_first:
            far, near, second_far, second_near = (1 - p.x, p.x, 1 - p.y, p.y)
            peers = (p.x_peer(), p.y_peer())
            src2 = self.r1.at[far]
        else:
            far, near, second_far, second_near = (1 - p.y, p.y, 1 - p.x, p.x)
            peers = (p.y_peer(), p.x_peer())
            src2 = self.r1.at[:, far]
        self.near, self.second_near = near, second_near
        self.copies = [
            remote(part.at[1 - p.c], self.r1, send.at[0], recv.at[0], p.core_peer()),
            remote(src2, self.r2, send.at[1], recv.at[1], peers[0]),
            remote(self.r2.at[second_far], self.r3, send.at[2], recv.at[2], peers[1]),
        ]
        self.last = [
            remote(self.r3.at[p.z_at(k)], self.r4.at[k - 1], zsend.at[k - 1], zrecv.at[k - 1], p.z_peer(k))
            for k in range(1, p.rest)
        ]

    def start(self):
        self.copies[0].start()

    def step1(self):
        p = self.place
        self.copies[0].wait()
        for i in range(2):
            for j in range(2):
                def add(k, carry, i=i, j=j):
                    self.r1[i, j, k] = self.r1[i, j, k] + self.part[p.c, i, j, k]
                    return carry
                lax.fori_loop(0, p.rest, add, 0)
        self.copies[1].start()

    def step2(self):
        p = self.place
        self.copies[1].wait()
        for i in range(2):
            def add(k, carry, i=i):
                own = self.r1[self.near, i, k] if self.x_first else self.r1[i, self.near, k]
                self.r2[i, k] = self.r2[i, k] + own
                return carry
            lax.fori_loop(0, p.rest, add, 0)
        self.copies[2].start()

    def step3(self):
        p = self.place
        self.copies[2].wait()

        def add(k, carry):
            self.r3[k] = self.r3[k] + self.r2[self.second_near, k]
            return carry
        lax.fori_loop(0, p.rest, add, 0)
        for copy in self.last:
            copy.start()

    def total(self):
        p = self.place
        for copy in self.last:
            copy.wait()
        result = self.r3[p.z].astype(F32)
        for k in range(1, p.rest):
            result = result + self.r4[k - 1].astype(F32)
        return result


def chunk_scratch(rest, rows, width):
    return [
        pltpu.VMEM((2, 2, rest, rows, width), LOW),
        pltpu.VMEM((2, rest, rows, width), LOW),
        pltpu.VMEM((rest, rows, width), LOW),
        pltpu.VMEM((rest - 1, rows, width), LOW),
        pltpu.SemaphoreType.DMA((3,)),
        pltpu.SemaphoreType.DMA((3,)),
        pltpu.SemaphoreType.DMA((rest - 1,)),
        pltpu.SemaphoreType.DMA((rest - 1,)),
    ]


class Small:
    def __init__(self, place, small, lead, everyone, bufs):
        got, gotz, send, recv, zsend, zrecv, gsend, grecv, gzsend, gzrecv = bufs
        p = place
        self.place, self.small, self.got, self.gotz = p, small, got, gotz
        self.lead, self.everyone = lead, everyone
        peers = (p.core_peer(), p.x_peer(), p.y_peer())
        blocks = (
            everyone.at[p.z, p.y, p.x, p.c], everyone.at[p.z, p.y, p.x], everyone.at[p.z, p.y],
        )
        self.sums = [remote(small, got.at[i], send.at[i], recv.at[i], peers[i]) for i in range(3)]
        self.sum_last = [
            remote(small, gotz.at[k - 1], zsend.at[k - 1], zrecv.at[k - 1], p.z_peer(k)) for k in range(1, p.rest)
        ]
        self.gathers = [remote(blocks[i], blocks[i], gsend.at[i], grecv.at[i], peers[i]) for i in range(3)]
        self.gather_last = [
            remote(everyone.at[p.z], everyone.at[p.z], gzsend.at[k - 1], gzrecv.at[k - 1], p.z_peer(k))
            for k in range(1, p.rest)
        ]

    def gather_start(self):
        p = self.place
        self.everyone[p.z, p.y, p.x, p.c] = self.lead[...]
        self.gathers[0].start()

    def gather_step(self, i):
        self.gathers[i].wait()
        if i < 2:
            self.gathers[i + 1].start()
        else:
            for copy in self.gather_last:
                copy.start()

    def gather_end(self):
        for copy in self.gather_last:
            copy.wait()

    def sum_start(self):
        self.sums[0].start()

    def sum_step(self, i):
        self.sums[i].wait()
        self.small[...] = self.small[...] + self.got[i]
        if i < 2:
            self.sums[i + 1].start()
        else:
            for copy in self.sum_last:
                copy.start()

    def sum_end(self):
        for copy in self.sum_last:
            copy.wait()
        total = self.small[...]
        for k in range(1, self.place.rest):
            total = total + self.gotz[k - 1]
        return total


def small_scratch(rest):
    return [
        pltpu.VMEM((3, 16, D), F32),
        pltpu.VMEM((rest - 1, 16, D), F32),
    ] + [pltpu.SemaphoreType.DMA((3,)), pltpu.SemaphoreType.DMA((3,)),
         pltpu.SemaphoreType.DMA((rest - 1,)), pltpu.SemaphoreType.DMA((rest - 1,))] * 2


def reduce_kernel(rest, n_chunks, *refs):
    parts = refs[:n_chunks]
    small_in, lead = refs[n_chunks : n_chunks + 2]
    outs = refs[n_chunks + 2 : 2 * n_chunks + 2]
    small_out, everyone = refs[2 * n_chunks + 2 : 2 * n_chunks + 4]
    scratch = refs[2 * n_chunks + 4 :]
    place = Place(rest)
    chunks = []
    for i in range(n_chunks):
        own = scratch[8 * i : 8 * i + 8]
        chunks.append(Reduce(place, parts[i], own[:4], own[4:], i % 2 == 0))
    rest_scratch = scratch[8 * n_chunks :]
    small = Small(place, rest_scratch[0], lead, everyone, rest_scratch[1:])
    rest_scratch[0][...] = small_in[...]
    place.barrier()
    small.gather_start()
    small.sum_start()
    steps = [[c.step1, c.step2, c.step3] for c in chunks]
    for chunk in chunks:
        chunk.start()
    for i in range(3):
        small.gather_step(i)
        small.sum_step(i)
    for phase in range(n_chunks + 4):
        for i in range(n_chunks):
            k = phase - i
            if i % 2 == 1:
                k = phase - i + 1
            if 0 <= k < 3:
                steps[i][k]()
            if k == 3:
                outs[i][...] = chunks[i].total()
    small.gather_end()
    small_out[...] = small.sum_end()


def reduce_gradients(rest, parts, small, lead):
    vmem = pl.BlockSpec(memory_space=pltpu.VMEM)
    scratch = []
    for part in parts:
        scratch += chunk_scratch(rest, *part.shape[4:])
    scratch += [pltpu.VMEM((16, D), F32)] + small_scratch(rest)
    outs = [jax.ShapeDtypeStruct(part.shape[4:], F32) for part in parts]
    outs += [
        jax.ShapeDtypeStruct((16, D), F32),
        jax.ShapeDtypeStruct((rest, 2, 2, 2, 2, D), F32),
    ]
    return pl.pallas_call(
        functools.partial(reduce_kernel, rest, len(parts)),
        out_shape=tuple(outs),
        in_specs=[vmem] * (len(parts) + 2),
        out_specs=tuple([vmem] * len(outs)),
        scratch_shapes=scratch,
        compiler_params=pltpu.CompilerParams(
            collective_id=0, has_side_effects=True, vmem_limit_bytes=60 << 20
        ),
    )(*parts, small, lead)


def owner_blocks(grad_t, rest, width):
    rows = grad_t.shape[0] // (8 * rest)
    view = grad_t.astype(LOW).reshape(rest, 2, 2, 2, rows, width)
    return view.transpose(3, 2, 1, 0, 4, 5)


def attention(packed, length):
    heads = packed.reshape(SLOT, 3, HEADS, HEAD_DIM)
    queries, keys_all, values = heads[:, 0], heads[:, 1], heads[:, 2]
    scores = jnp.einsum("qhd,khd->hqk", queries, keys_all, preferred_element_type=F32) * HEAD_DIM ** (-0.5)
    scores = jnp.where((jnp.arange(SLOT) < length)[None, None, :], scores, -1e30)
    row_max = jnp.max(scores, axis=-1, keepdims=True)
    weights = jnp.exp(scores - row_max)
    weights = weights / jnp.sum(weights, axis=-1, keepdims=True)
    low = weights.astype(LOW)
    context = jnp.einsum("hqk,khd->qhd", low, values, preferred_element_type=F32)
    return context.astype(LOW).reshape(SLOT, D), low


def attention_back(packed, low, d_context):
    heads = packed.reshape(SLOT, 3, HEADS, HEAD_DIM)
    queries, keys_all, values = heads[:, 0], heads[:, 1], heads[:, 2]
    d_heads = d_context.reshape(SLOT, HEADS, HEAD_DIM)
    weights = low.astype(F32)
    d_weights = jnp.einsum("qhd,khd->hqk", d_heads, values, preferred_element_type=F32)
    d_values = jnp.einsum("hqk,qhd->khd", low, d_heads, preferred_element_type=F32)
    row_dot = jnp.sum(weights * d_weights, axis=-1, keepdims=True)
    d_scores = (weights * (d_weights - row_dot)).astype(LOW)
    scale = HEAD_DIM ** (-0.5)
    d_queries = jnp.einsum("hqk,khd->qhd", d_scores, keys_all, preferred_element_type=F32) * scale
    d_keys = jnp.einsum("hqk,qhd->khd", d_scores, queries, preferred_element_type=F32) * scale
    return jnp.stack([d_queries, d_keys, d_values], axis=1).astype(LOW).reshape(SLOT, 3 * D)


def per_device(
    tokens,
    cotangent,
    lengths,
    labels,
    w_qkv,
    w_out,
    w_up,
    w_down,
    w_pool,
    w_class,
    biases,
    norm_gains,
    bias_up,
):
    rest = lax.axis_size("batch") // 2
    head_rank = lax.axis_index("head")
    rank = lax.axis_index("batch") * 4 + head_rank
    length = lax.dynamic_index_in_dim(lengths, head_rank, keepdims=False)
    label = lax.dynamic_index_in_dim(labels, head_rank, keepdims=False)
    slot_live = (jnp.arange(SLOT) < length).astype(F32)
    zeros_key = jnp.zeros((D,), F32)
    packed = jnp.dot(tokens, w_qkv, preferred_element_type=F32) + jnp.concatenate(
        [biases[0], zeros_key, biases[1]]
    )
    packed = packed.astype(LOW)
    context, probs = attention(packed, length)
    attn = jnp.dot(context, w_out, preferred_element_type=F32) + biases[2]
    first_sum = tokens.astype(F32) + attn
    norm_one, first_pull = jax.vjp(layer_norm, first_sum, norm_gains[0], biases[3])
    norm_low = norm_one.astype(LOW)
    hidden_up = jnp.dot(norm_low, w_up, preferred_element_type=F32) + bias_up
    activated_full, gelu_pull = jax.vjp(exact_gelu, hidden_up)
    activated = activated_full.astype(LOW)
    branch = jnp.dot(activated, w_down, preferred_element_type=F32) + biases[4]
    out_full, second_pull = jax.vjp(layer_norm, norm_one + branch, norm_gains[1], biases[5])
    leading = out_full[:1].astype(LOW)
    pooled = jnp.tanh(jnp.dot(leading, w_pool, preferred_element_type=F32) + biases[6])
    pooled_low = pooled.astype(LOW)
    logits = against(pooled_low, w_class)
    onehot = (jnp.arange(CLASSES)[None, :] == label).astype(F32)
    losses = jax.nn.logsumexp(logits, axis=-1) - jnp.sum(onehot * logits, axis=-1)
    d_logits = jax.nn.softmax(logits, axis=-1) - onehot
    g_class = exact(d_logits.T, pooled_low.astype(F32))
    d_pre = exact(d_logits, w_class.astype(F32)) * (1.0 - pooled * pooled)
    d_leading = exact(d_pre, w_pool.astype(F32).T)
    d_out = cotangent.astype(F32) * slot_live[:, None]
    d_out = d_out.at[0].add(d_leading[0])
    d_h2, g_gain_two, g_shift_two = second_pull(d_out)
    d_branch = d_h2.astype(LOW)
    g_bias_down = jnp.sum(d_branch.astype(F32), axis=0)
    g_down_t = inner(d_branch, activated)
    d_activated = against(d_branch, w_down)
    d_up = gelu_pull(d_activated)[0].astype(LOW)
    g_bias_up = jnp.sum(d_up.astype(F32), axis=0)
    g_up_t = inner(d_up, norm_low)
    d_norm_one = d_h2 + against(d_up, w_up)
    d_h1, g_gain_one, g_shift_one = first_pull(d_norm_one)
    d_attn = d_h1.astype(LOW)
    g_bias_out = jnp.sum(d_attn.astype(F32), axis=0)
    g_out_t = inner(d_attn, context)
    d_context = against(d_attn, w_out).astype(LOW)
    d_packed = attention_back(packed, probs, d_context)
    g_qkv_t = inner(d_packed, tokens)
    column_sums = jnp.sum(d_packed.astype(F32), axis=0)
    grad_tokens = (d_h1 + against(d_packed, w_qkv)).astype(LOW)
    small = jnp.concatenate(
        [
            g_class,
            jnp.stack([column_sums[:D], column_sums[2 * D :], g_bias_out, g_shift_one, g_bias_down, g_shift_two]),
            jnp.stack([g_gain_one, g_gain_two]),
            g_bias_up.reshape(FF // D, D),
            d_pre,
        ]
    )
    lead = jnp.concatenate([leading.astype(F32), d_pre])
    down = owner_blocks(g_down_t, rest, FF)
    up = owner_blocks(g_up_t, rest, D)
    last = jnp.concatenate([owner_blocks(g_qkv_t, rest, D), owner_blocks(g_out_t, rest, D)], axis=4)
    half = up.shape[4] // 2
    parts = [
        down[..., : FF // 2], down[..., FF // 2 :],
        up[..., :half, :], up[..., half:, :],
        last[..., :half, :], last[..., half:, :],
    ]
    *sums, small, everyone = reduce_gradients(rest, parts, small, lead)
    g_down = jnp.concatenate(sums[0:2], axis=1).T
    g_up = jnp.concatenate(sums[2:4], axis=0).T
    g_last = jnp.concatenate(sums[4:6], axis=0).T
    own_qkv = 3 * D // (8 * rest)
    own = D // (8 * rest)
    everyone = everyone.reshape(8 * rest, 2, D)
    window = lax.dynamic_slice_in_dim(small, rank * own, own, axis=1)
    pre_window = lax.dynamic_slice_in_dim(everyone[:, 1], rank * own, own, axis=1)
    g_pool = lax.dot_general(
        everyone[:, 0], pre_window, (((0,), (0,)), ((), ())),
        precision=lax.Precision.HIGHEST, preferred_element_type=F32,
    )
    own_up = FF // (8 * rest)
    g_bias_up = lax.dynamic_slice_in_dim(small[11:15].reshape(FF), rank * own_up, own_up)
    return (
        out_full.astype(LOW),
        grad_tokens,
        losses,
        g_last[:, :own_qkv],
        g_last[:, own_qkv:],
        g_up,
        g_down,
        g_pool,
        window[:3],
        window[3:9],
        window[9:11],
        g_bias_up,
        window[15],
    )


def solution(mesh):
    return jax.shard_map(
        per_device,
        mesh=mesh,
        in_specs=(
            P(("batch", "head"), None),
            P(("batch", "head"), None),
            P("batch"),
            P("batch"),
            P(),
            P(),
            P(),
            P(),
            P(),
            P(),
            P(),
            P(),
            P(),
        ),
        out_specs=(
            P(("batch", "head"), None),
            P(("batch", "head"), None),
            P(("batch", "head")),
            P(None, ("batch", "head")),
            P(None, ("batch", "head")),
            P(None, ("batch", "head")),
            P(None, ("batch", "head")),
            P(None, ("batch", "head")),
            P(None, ("batch", "head")),
            P(None, ("batch", "head")),
            P(None, ("batch", "head")),
            P(("batch", "head")),
            P(("batch", "head")),
        ),
        check_vma=False,
    )
```

```python
import functools

import jax
import jax.numpy as jnp
from jax import lax
from jax.experimental import pallas as pl
from jax.experimental.pallas import tpu as pltpu
from jax.sharding import PartitionSpec as P

D = 768
HEADS = 12
HEAD_DIM = 64
FF = 3072
CLASSES = 3
SLOT = 512
MESH = pl.DeviceIdType.MESH
LOW = jnp.bfloat16
F32 = jnp.float32


def layer_norm(hidden, gain, shift):
    center = hidden - jnp.mean(hidden, axis=-1, keepdims=True)
    spread = jnp.mean(center * center, axis=-1, keepdims=True)
    return center * lax.rsqrt(spread + 1e-12) * gain + shift


def exact_gelu(hidden):
    return jax.nn.gelu(hidden, approximate=False)


def inner(left, right):
    return lax.dot_general(
        left, right, (((0,), (0,)), ((), ())), preferred_element_type=jnp.float32
    )


def against(left, right):
    return lax.dot_general(
        left, right, (((1,), (1,)), ((), ())), preferred_element_type=jnp.float32
    )


def exact(left, right):
    return jnp.dot(left, right, precision=lax.Precision.HIGHEST, preferred_element_type=jnp.float32)


class Place:
    def __init__(self, rest):
        batch = lax.axis_index("batch")
        head = lax.axis_index("head")
        self.rest = rest
        self.z = batch // 2
        self.y = lax.rem(batch, 2)
        self.x = head // 2
        self.c = lax.rem(head, 2)

    def device(self, z, y, x, c):
        return (z * 2 + y, x * 2 + c)

    def core_peer(self):
        return self.device(self.z, self.y, self.x, 1 - self.c)

    def x_peer(self):
        return self.device(self.z, self.y, 1 - self.x, self.c)

    def y_peer(self):
        return self.device(self.z, 1 - self.y, self.x, self.c)

    def z_at(self, offset):
        return lax.rem(self.z + offset, self.rest)

    def z_peer(self, offset):
        return self.device(self.z_at(offset), self.y, self.x, self.c)

    def barrier(self):
        sem = pltpu.get_barrier_semaphore()
        for peer in (self.core_peer(), self.x_peer(), self.y_peer()):
            pl.semaphore_signal(sem, inc=1, device_id=peer, device_id_type=MESH)
        for offset in range(1, self.rest):
            pl.semaphore_signal(sem, inc=1, device_id=self.z_peer(offset), device_id_type=MESH)
        pl.semaphore_wait(sem, 3 + self.rest - 1)


def remote(src, dst, send, recv, peer):
    return pltpu.make_async_remote_copy(
        src_ref=src, dst_ref=dst, send_sem=send, recv_sem=recv, device_id=peer, device_id_type=MESH
    )


class Reduce:
    def __init__(self, place, part, bufs, sems, x_first):
        self.place, self.part, self.x_first = place, part, x_first
        self.r1, self.r2, self.r3, self.r4 = bufs
        send, recv, zsend, zrecv = sems
        p = place
        if x_first:
            far, near, second_far, second_near = (1 - p.x, p.x, 1 - p.y, p.y)
            peers = (p.x_peer(), p.y_peer())
            src2 = self.r1.at[far]
        else:
            far, near, second_far, second_near = (1 - p.y, p.y, 1 - p.x, p.x)
            peers = (p.y_peer(), p.x_peer())
            src2 = self.r1.at[:, far]
        self.near, self.second_near = near, second_near
        self.copies = [
            remote(part.at[1 - p.c], self.r1, send.at[0], recv.at[0], p.core_peer()),
            remote(src2, self.r2, send.at[1], recv.at[1], peers[0]),
            remote(self.r2.at[second_far], self.r3, send.at[2], recv.at[2], peers[1]),
        ]
        self.last = [
            remote(self.r3.at[p.z_at(k)], self.r4.at[k - 1], zsend.at[k - 1], zrecv.at[k - 1], p.z_peer(k))
            for k in range(1, p.rest)
        ]

    def start(self):
        self.copies[0].start()

    def step1(self):
        p = self.place
        self.copies[0].wait()
        for i in range(2):
            for j in range(2):
                def add(k, carry, i=i, j=j):
                    self.r1[i, j, k] = self.r1[i, j, k] + self.part[p.c, i, j, k]
                    return carry
                lax.fori_loop(0, p.rest, add, 0)
        self.copies[1].start()

    def step2(self):
        p = self.place
        self.copies[1].wait()
        for i in range(2):
            def add(k, carry, i=i):
                own = self.r1[self.near, i, k] if self.x_first else self.r1[i, self.near, k]
                self.r2[i, k] = self.r2[i, k] + own
                return carry
            lax.fori_loop(0, p.rest, add, 0)
        self.copies[2].start()

    def step3(self):
        p = self.place
        self.copies[2].wait()

        def add(k, carry):
            self.r3[k] = self.r3[k] + self.r2[self.second_near, k]
            return carry
        lax.fori_loop(0, p.rest, add, 0)
        for copy in self.last:
            copy.start()

    def total(self):
        p = self.place
        for copy in self.last:
            copy.wait()
        result = self.r3[p.z].astype(F32)
        for k in range(1, p.rest):
            result = result + self.r4[k - 1].astype(F32)
        return result


def chunk_scratch(rest, rows, width):
    return [
        pltpu.VMEM((2, 2, rest, rows, width), LOW),
        pltpu.VMEM((2, rest, rows, width), LOW),
        pltpu.VMEM((rest, rows, width), LOW),
        pltpu.VMEM((rest - 1, rows, width), LOW),
        pltpu.SemaphoreType.DMA((3,)),
        pltpu.SemaphoreType.DMA((3,)),
        pltpu.SemaphoreType.DMA((rest - 1,)),
        pltpu.SemaphoreType.DMA((rest - 1,)),
    ]


class Small:
    def __init__(self, place, small, lead, everyone, bufs):
        got, gotz, send, recv, zsend, zrecv, gsend, grecv, gzsend, gzrecv = bufs
        p = place
        self.place, self.small, self.got, self.gotz = p, small, got, gotz
        self.lead, self.everyone = lead, everyone
        peers = (p.core_peer(), p.x_peer(), p.y_peer())
        blocks = (
            everyone.at[p.z, p.y, p.x, p.c], everyone.at[p.z, p.y, p.x], everyone.at[p.z, p.y],
        )
        self.sums = [remote(small, got.at[i], send.at[i], recv.at[i], peers[i]) for i in range(3)]
        self.sum_last = [
            remote(small, gotz.at[k - 1], zsend.at[k - 1], zrecv.at[k - 1], p.z_peer(k)) for k in range(1, p.rest)
        ]
        self.gathers = [remote(blocks[i], blocks[i], gsend.at[i], grecv.at[i], peers[i]) for i in range(3)]
        self.gather_last = [
            remote(everyone.at[p.z], everyone.at[p.z], gzsend.at[k - 1], gzrecv.at[k - 1], p.z_peer(k))
            for k in range(1, p.rest)
        ]

    def gather_start(self):
        p = self.place
        self.everyone[p.z, p.y, p.x, p.c] = self.lead[...]
        self.gathers[0].start()

    def gather_step(self, i):
        self.gathers[i].wait()
        if i < 2:
            self.gathers[i + 1].start()
        else:
            for copy in self.gather_last:
                copy.start()

    def gather_end(self):
        for copy in self.gather_last:
            copy.wait()

    def sum_start(self):
        self.sums[0].start()

    def sum_step(self, i):
        self.sums[i].wait()
        self.small[...] = self.small[...] + self.got[i]
        if i < 2:
            self.sums[i + 1].start()
        else:
            for copy in self.sum_last:
                copy.start()

    def sum_end(self):
        for copy in self.sum_last:
            copy.wait()
        total = self.small[...]
        for k in range(1, self.place.rest):
            total = total + self.gotz[k - 1]
        return total


def small_scratch(rest):
    return [
        pltpu.VMEM((3, 16, D), F32),
        pltpu.VMEM((rest - 1, 16, D), F32),
    ] + [pltpu.SemaphoreType.DMA((3,)), pltpu.SemaphoreType.DMA((3,)),
         pltpu.SemaphoreType.DMA((rest - 1,)), pltpu.SemaphoreType.DMA((rest - 1,))] * 2


def reduce_kernel(rest, n_chunks, *refs):
    parts = refs[:n_chunks]
    small_in, lead = refs[n_chunks : n_chunks + 2]
    outs = refs[n_chunks + 2 : 2 * n_chunks + 2]
    small_out, everyone = refs[2 * n_chunks + 2 : 2 * n_chunks + 4]
    scratch = refs[2 * n_chunks + 4 :]
    place = Place(rest)
    chunks = []
    for i in range(n_chunks):
        own = scratch[8 * i : 8 * i + 8]
        chunks.append(Reduce(place, parts[i], own[:4], own[4:], i % 2 == 0))
    rest_scratch = scratch[8 * n_chunks :]
    small = Small(place, rest_scratch[0], lead, everyone, rest_scratch[1:])
    rest_scratch[0][...] = small_in[...]
    place.barrier()
    small.gather_start()
    small.sum_start()
    steps = [[c.step1, c.step2, c.step3] for c in chunks]
    for chunk in chunks:
        chunk.start()
    for i in range(3):
        small.gather_step(i)
        small.sum_step(i)
    for phase in range(n_chunks + 4):
        for i in range(n_chunks):
            k = phase - i
            if i % 2 == 1:
                k = phase - i + 1
            if 0 <= k < 3:
                steps[i][k]()
            if k == 3:
                outs[i][...] = chunks[i].total()
    small.gather_end()
    small_out[...] = small.sum_end()


def reduce_gradients(rest, parts, small, lead):
    vmem = pl.BlockSpec(memory_space=pltpu.VMEM)
    scratch = []
    for part in parts:
        scratch += chunk_scratch(rest, *part.shape[4:])
    scratch += [pltpu.VMEM((16, D), F32)] + small_scratch(rest)
    outs = [jax.ShapeDtypeStruct(part.shape[4:], F32) for part in parts]
    outs += [
        jax.ShapeDtypeStruct((16, D), F32),
        jax.ShapeDtypeStruct((rest, 2, 2, 2, 2, D), F32),
    ]
    return pl.pallas_call(
        functools.partial(reduce_kernel, rest, len(parts)),
        out_shape=tuple(outs),
        in_specs=[vmem] * (len(parts) + 2),
        out_specs=tuple([vmem] * len(outs)),
        scratch_shapes=scratch,
        compiler_params=pltpu.CompilerParams(
            collective_id=0, has_side_effects=True, vmem_limit_bytes=60 << 20
        ),
    )(*parts, small, lead)


def owner_blocks(grad_t, rest, width):
    rows = grad_t.shape[0] // (8 * rest)
    view = grad_t.astype(LOW).reshape(rest, 2, 2, 2, rows, width)
    return view.transpose(3, 2, 1, 0, 4, 5)


def attention(packed, length):
    heads = packed.reshape(SLOT, 3, HEADS, HEAD_DIM)
    queries, keys_all, values = heads[:, 0], heads[:, 1], heads[:, 2]
    scores = jnp.einsum("qhd,khd->hqk", queries, keys_all, preferred_element_type=F32) * HEAD_DIM ** (-0.5)
    scores = jnp.where((jnp.arange(SLOT) < length)[None, None, :], scores, -1e30)
    row_max = jnp.max(scores, axis=-1, keepdims=True)
    weights = jnp.exp(scores - row_max)
    weights = weights / jnp.sum(weights, axis=-1, keepdims=True)
    low = weights.astype(LOW)
    context = jnp.einsum("hqk,khd->qhd", low, values, preferred_element_type=F32)
    return context.astype(LOW).reshape(SLOT, D), low


def attention_back(packed, low, d_context):
    heads = packed.reshape(SLOT, 3, HEADS, HEAD_DIM)
    queries, keys_all, values = heads[:, 0], heads[:, 1], heads[:, 2]
    d_heads = d_context.reshape(SLOT, HEADS, HEAD_DIM)
    weights = low.astype(F32)
    d_weights = jnp.einsum("qhd,khd->hqk", d_heads, values, preferred_element_type=F32)
    d_values = jnp.einsum("hqk,qhd->khd", low, d_heads, preferred_element_type=F32)
    row_dot = jnp.sum(weights * d_weights, axis=-1, keepdims=True)
    d_scores = (weights * (d_weights - row_dot)).astype(LOW)
    scale = HEAD_DIM ** (-0.5)
    d_queries = jnp.einsum("hqk,khd->qhd", d_scores, keys_all, preferred_element_type=F32) * scale
    d_keys = jnp.einsum("hqk,qhd->khd", d_scores, queries, preferred_element_type=F32) * scale
    return jnp.stack([d_queries, d_keys, d_values], axis=1).astype(LOW).reshape(SLOT, 3 * D)


def nn(left, right):
    return jnp.dot(left, right, preferred_element_type=F32)


def aligned(index, step):
    return pl.ds(pl.multiple_of(index * step, step), step)


def column_sum(ones, array):
    return nn(ones, array)[0:1]


def normalized(hidden):
    center = hidden - jnp.mean(hidden, axis=-1, keepdims=True)
    spread = jnp.mean(center * center, axis=-1, keepdims=True)
    scale = lax.rsqrt(spread + 1e-12)
    return center * scale, scale


def normalized_back(normed, scale, d_normed):
    first = jnp.mean(d_normed, axis=-1, keepdims=True)
    second = jnp.mean(d_normed * normed, axis=-1, keepdims=True)
    return scale * (d_normed - first - normed * second)


class Staged:
    def __init__(self, place, order, part, bufs, send, recv, zsend, zrecv):
        p = self.place = place
        self.part, self.bufs = part, bufs
        sizes = {"x": 2, "y": 2, "z": p.rest}
        mine = {"x": p.x, "y": p.y, "z": p.z}
        peers = {"x": p.x_peer, "y": p.y_peer}
        self.count = 4 * p.rest
        self.stages = [[remote(part.at[pl.ds((1 - p.c) * self.count, self.count)], bufs[0], send.at[0], recv.at[0], p.core_peer())]]
        self.own = [lambda: part[pl.ds(p.c * self.count, self.count)]]
        self.got = [(bufs[0], 1, self.count)]
        blocks = self.count
        held = bufs[0]
        for i, axis in enumerate(order):
            blocks = blocks // sizes[axis]
            buf = bufs[i + 1]
            at = mine[axis]
            if axis == "z":
                copies = [
                    remote(
                        held.at[pl.ds(p.z_at(k) * blocks, blocks)], buf.at[pl.ds((k - 1) * blocks, blocks)],
                        zsend.at[k - 1], zrecv.at[k - 1], p.z_peer(k),
                    )
                    for k in range(1, p.rest)
                ]
                self.got.append((buf, p.rest - 1, blocks))
            else:
                copies = [
                    remote(held.at[pl.ds((1 - at) * blocks, blocks)], buf, send.at[i + 1], recv.at[i + 1], peers[axis]())
                ]
                self.got.append((buf, 1, blocks))
            self.stages.append(copies)
            self.own.append(lambda held=held, at=at, blocks=blocks: held[pl.ds(at * blocks, blocks)])
            held = buf

    def start(self, i):
        for copy in self.stages[i]:
            copy.start()

    def take(self, i):
        for copy in self.stages[i]:
            copy.wait()
        buf, pieces, blocks = self.got[i]
        if pieces == 1:
            buf[...] = buf[...] + self.own[i]()
        else:
            buf[0:blocks] = self.sum(i).astype(LOW)

    def sum(self, i):
        buf, pieces, blocks = self.got[i]
        total = self.own[i]().astype(F32)
        for k in range(pieces):
            total = total + buf[k * blocks : (k + 1) * blocks].astype(F32)
        return total

    def step(self, i):
        self.take(i)
        self.start(i + 1)

    def finish(self):
        i = len(self.stages) - 1
        for copy in self.stages[i]:
            copy.wait()
        return self.sum(i)[0]


def block_index(order, rest, z, y, x, c):
    sizes = {"x": 2, "y": 2, "z": rest}
    at = {"x": x, "y": y, "z": z}
    index = c
    for axis in order:
        index = index * sizes[axis] + at[axis]
    return index


def owners(rest):
    return [(z, y, x, c) for z in range(rest) for y in range(2) for x in range(2) for c in range(2)]


def staged_scratch(rest, order, rows, width):
    sizes = {"x": 2, "y": 2, "z": rest}
    blocks = 4 * rest
    bufs = [pltpu.VMEM((blocks, rows, width), LOW)]
    for axis in order:
        blocks = blocks // sizes[axis]
        copies = rest - 1 if axis == "z" else 1
        bufs.append(pltpu.VMEM((copies * blocks, rows, width), LOW))
    return bufs


ORDERS = ("xyz", "yxz", "xyz", "yxz", "xzy", "yzx")
N_IN = 13
N_OUT = 11


def layer_kernel(rest, *refs):
    (lengths, labels, biases, gains, bias_up, w_class, tokens_h, cot_h, wqkv_h, wout_h, wup_h, wdown_h, wpool_h) = refs[:N_IN]
    out_h, gtok_h, *sums = refs[N_IN : N_IN + 8]
    small_out, everyone, loss_out = refs[N_IN + 8 : N_IN + N_OUT]
    scratch = list(refs[N_IN + N_OUT :])
    (
        tokens, w_qkv, w_out, w_up, shared, packed, weights, inverse, context, normed_one, norm_low,
        activated, slope, d_hidden, d_low, d_packed, part_down, scale_one, small, lead, in_sem, out_sem,
    ) = scratch[:22]
    cot = d_low
    d_context = norm_low
    wide = SLOT
    pool_wide = d_packed.at[0:D]
    pool_rest = d_packed.at[D : 2 * D, 0 : D - wide]
    out_wide = d_packed.at[2 * D : 2 * D + SLOT]
    out_rest = d_packed.at[D : D + SLOT, wide // 2 : wide // 2 + D - wide]
    place = Place(rest)
    small_bufs = scratch[22:32]
    chunk_bufs = scratch[32:]
    head_rank = lax.axis_index("head")
    length = lengths[head_rank]
    label = labels[head_rank]
    loads = [
        pltpu.make_async_copy(src, dst, in_sem.at[i])
        for i, (src, dst) in enumerate(
            [(tokens_h, tokens), (wqkv_h, w_qkv), (wout_h, w_out), (wup_h, w_up),
             (wdown_h, shared), (cot_h, cot), (wpool_h.at[:, 0:wide], pool_wide), (wpool_h.at[:, wide:D], pool_rest)]
        )
    ]
    for load in loads:
        load.start()
    sem = pltpu.get_barrier_semaphore()
    for peer in (place.core_peer(), place.x_peer(), place.y_peer()):
        pl.semaphore_signal(sem, inc=1, device_id=peer, device_id_type=MESH)
    for offset in range(1, rest):
        pl.semaphore_signal(sem, inc=1, device_id=place.z_peer(offset), device_id_type=MESH)

    half = FF // 2
    per = 8 * rest
    chunk_parts = [part_down.at[0:per], part_down.at[per : 2 * per]]
    rows_up = FF // per // 2
    shared_blocks = shared.reshape(2 * per, rows_up, D)
    chunk_parts += [shared_blocks.at[0:per], shared_blocks.at[per : 2 * per]] * 2
    chunks = []
    for i in range(6):
        own = chunk_bufs[8 * i : 8 * i + 8]
        chunks.append(Staged(place, ORDERS[i], chunk_parts[i], own[:4], *own[4:]))
    tiny = Small(place, small, lead, everyone, small_bufs)

    loads[0].wait()
    loads[1].wait()
    ones = jnp.ones((8, SLOT), LOW)
    for part in range(3):
        columns = slice(part * D, part * D + D)
        result = nn(tokens[...], w_qkv[:, columns])
        if part == 0:
            result = (result + biases[0:1]).astype(LOW) * jnp.asarray(HEAD_DIM ** (-0.5), LOW)
        elif part == 2:
            result = (result + biases[1:2]).astype(LOW)
        else:
            result = result.astype(LOW)
        packed[:, columns] = result

    key_live = lax.broadcasted_iota(jnp.int32, (SLOT, 1), 0) < length
    lane = lax.broadcasted_iota(jnp.int32, (1, 2 * HEAD_DIM), 1)
    lane_of = [lane < HEAD_DIM, lane >= HEAD_DIM]

    def attend(pair, carry):
        at = pl.multiple_of(pair * 2 * HEAD_DIM, 2 * HEAD_DIM)
        queries = packed[:, pl.ds(at, 2 * HEAD_DIM)]
        keys_all = packed[:, pl.ds(at + D, 2 * HEAD_DIM)]
        values_t = packed[:, pl.ds(at + 2 * D, 2 * HEAD_DIM)].T
        got = []
        for k in range(2):
            own_keys = jnp.where(lane_of[k], keys_all, jnp.zeros_like(keys_all))
            scores = jnp.where(key_live, against(own_keys, queries), -1e30)
            powers = jnp.exp(scores - jnp.max(scores, axis=0, keepdims=True))
            inv = 1.0 / jnp.sum(powers, axis=0, keepdims=True)
            powers = powers.astype(LOW)
            weights[2 * pair + k] = powers
            inverse[pair, k : k + 1] = inv
            got.append(nn(values_t[k * HEAD_DIM : (k + 1) * HEAD_DIM], powers) * inv)
        context[:, pl.ds(at, 2 * HEAD_DIM)] = jnp.concatenate(got, axis=0).T.astype(LOW)
        return carry

    lax.fori_loop(0, HEADS // 2, attend, 0)

    blocks = [slice(0, SLOT // 2), slice(SLOT // 2, SLOT)]
    loads[2].wait()
    for rows in blocks:
        hidden = nn(context[rows], w_out[...]) + biases[2:3] + tokens[rows].astype(F32)
        normed, scale = normalized(hidden)
        normed_one[rows] = normed
        scale_one[rows] = scale
        norm_low[rows] = (normed * gains[0:1] + biases[3:4]).astype(LOW)

    loads[3].wait()

    def feed(tile, carry):
        columns = aligned(tile, D)
        hidden = nn(norm_low[...], w_up[:, columns]) + bias_up[0:1, columns]
        share = 0.5 + 0.5 * lax.erf(hidden * 0.7071067811865476)
        activated[:, columns] = (hidden * share).astype(LOW)
        slope[:, columns] = (share + hidden * (jnp.exp(-0.5 * hidden * hidden) * 0.3989422804014327)).astype(LOW)
        return carry

    lax.fori_loop(0, FF // D, feed, 0)

    w_down = shared
    for i in (4, 5, 6, 7):
        loads[i].wait()
    row = lax.broadcasted_iota(jnp.int32, (SLOT // 2, 1), 0)
    kept = []
    for k, rows in enumerate(blocks):
        hidden = nn(activated[rows], w_down[...]) + biases[4:5] + (normed_one[rows] * gains[0:1] + biases[3:4])
        normed, scale = normalized(hidden)
        result = normed * gains[1:2] + biases[5:6]
        low = result.astype(LOW)
        out_wide[rows] = low[:, 0:wide]
        out_rest[rows] = low[:, wide:D]
        d_hidden[rows] = normed
        kept.append(scale)
        if k == 0:
            leading = low[0:8]
    out_copies = [
        pltpu.make_async_copy(out_wide, out_h.at[:, 0:wide], out_sem.at[0]),
        pltpu.make_async_copy(out_rest, out_h.at[:, wide:D], out_sem.at[2]),
    ]
    for copy in out_copies:
        copy.start()

    pooled = jnp.concatenate([nn(leading, pool_wide[...]), nn(leading, pool_rest[...])], axis=1)
    pooled = jnp.tanh(pooled + biases[6:7])[0:1]
    pooled_low = pooled.astype(LOW).astype(F32)
    classes = w_class[...].astype(F32)
    logits = jnp.sum(pooled_low * classes, axis=-1, keepdims=True)
    top = jnp.max(logits, axis=0, keepdims=True)
    powers = jnp.exp(logits - top)
    total = jnp.sum(powers, axis=0, keepdims=True)
    onehot = (lax.broadcasted_iota(jnp.int32, (CLASSES, 1), 0) == label).astype(F32)
    loss_out[...] = jnp.broadcast_to(
        jnp.log(total) + top - jnp.sum(onehot * logits, axis=0, keepdims=True), loss_out.shape
    )
    d_logits = powers / total - onehot
    d_pre = jnp.sum(d_logits * classes, axis=0, keepdims=True) * (1.0 - pooled * pooled)
    high = d_pre.astype(LOW).astype(F32)
    middle = (d_pre - high).astype(LOW).astype(F32)
    low = d_pre - high - middle
    eight = lax.broadcasted_iota(jnp.int32, (8, 1), 0)
    split = jnp.where(eight == 0, high, jnp.where(eight == 1, middle, jnp.where(eight == 2, low, 0.0)))
    split = split.astype(LOW)
    d_leading = against(split[:, 0:wide], pool_wide[...]) + against(split[:, wide:D], pool_rest[...])
    d_leading = jnp.sum(d_leading, axis=0, keepdims=True)
    small[0:3] = d_logits * pooled_low
    small[15:16] = d_pre
    lead[0:1] = leading[0:1].astype(F32)
    lead[1:2] = d_pre

    shift_two = jnp.zeros((1, D), F32)
    gain_two = jnp.zeros((1, D), F32)
    for k in (1, 0):
        rows = blocks[k]
        normed, scale = d_hidden[rows], kept[k]
        d_out = jnp.where(row + k * (SLOT // 2) < length, cot[rows].astype(F32), 0.0)
        if k == 0:
            d_out = d_out + jnp.where(row == 0, d_leading, 0.0)
        shift_two = shift_two + jnp.sum(d_out, axis=0, keepdims=True)
        gain_two = gain_two + jnp.sum(d_out * normed, axis=0, keepdims=True)
        d_two = normalized_back(normed, scale, d_out * gains[1:2])
        d_hidden[rows] = d_two
        d_low[rows] = d_two.astype(LOW)
    small[8:9] = shift_two
    small[10:11] = gain_two
    small[7:8] = column_sum(ones, d_low[...])

    for copy in out_copies:
        copy.wait()
    pl.semaphore_wait(sem, 3 + rest - 1)
    tiny.gather_start()
    d_branch_t = d_low[...].T
    rows_down = D // per
    for chunk in range(2):
        for tile in range(4):
            columns = slice(tile * D // 2, (tile + 1) * D // 2)
            result = nn(d_branch_t, activated[:, chunk * half + columns.start : chunk * half + columns.stop])
            for d, owner in enumerate(owners(rest)):
                part_down[chunk * per + block_index(ORDERS[chunk], rest, *owner), :, columns] = (
                    result[d * rows_down : (d + 1) * rows_down].astype(LOW)
                )
        chunks[chunk].start(0)

    def feed_back(tile, carry):
        columns = aligned(tile, D)
        d_up = (against(d_low[...], w_down[columns]) * slope[:, columns].astype(F32)).astype(LOW)
        slope[:, columns] = d_up
        small[pl.ds(11 + tile, 1)] = column_sum(ones, d_up)
        return carry

    lax.fori_loop(0, FF // D, feed_back, 0)
    d_up = slope
    tiny.gather_step(0)
    chunks[0].step(0)
    chunks[1].step(0)

    for tile in range(FF // D):
        for columns in (slice(0, D // 2), slice(D // 2, D)):
            result = inner(d_up[:, tile * D : (tile + 1) * D], norm_low[:, columns])
            for d in range(per * D // FF):
                owner = owners(rest)[tile * (per * D // FF) + d]
                for chunk in (2, 3):
                    first = d * 2 * rows_up + (chunk - 2) * rows_up
                    shared_blocks[(chunk - 2) * per + block_index(ORDERS[chunk], rest, *owner), :, columns] = (
                        result[first : first + rows_up].astype(LOW)
                    )
    chunks[2].start(0)
    chunks[3].start(0)
    tiny.gather_step(1)

    shift_one = jnp.zeros((1, D), F32)
    gain_one = jnp.zeros((1, D), F32)
    for rows in blocks:
        d_norm = d_hidden[rows] + against(d_up[rows], w_up[...])
        normed = normed_one[rows]
        shift_one = shift_one + jnp.sum(d_norm, axis=0, keepdims=True)
        gain_one = gain_one + jnp.sum(d_norm * normed, axis=0, keepdims=True)
        d_one = normalized_back(normed, scale_one[rows], d_norm * gains[0:1])
        d_hidden[rows] = d_one
        d_low[rows] = d_one.astype(LOW)
    small[6:7] = shift_one
    small[9:10] = gain_one
    small[5:6] = column_sum(ones, d_low[...])
    chunks[2].step(0)
    chunks[3].step(0)
    tiny.gather_step(2)

    d_context[...] = against(d_low[...], w_out[...]).astype(LOW)
    result_out = inner(d_low[...], context[...])
    own_qkv = 3 * D // per
    own_out = D // per
    first_rows = rows_up - (own_qkv - rows_up)
    for d, owner in enumerate(owners(rest)):
        shared_blocks[per + block_index(ORDERS[5], rest, *owner), own_qkv - rows_up :] = (
            result_out[d * own_out : (d + 1) * own_out].astype(LOW)
        )

    def attend_back(pair, carry):
        at = pl.multiple_of(pair * 2 * HEAD_DIM, 2 * HEAD_DIM)
        queries_t = packed[:, pl.ds(at, 2 * HEAD_DIM)].T
        keys_t = packed[:, pl.ds(at + D, 2 * HEAD_DIM)].T
        values = packed[:, pl.ds(at + 2 * D, 2 * HEAD_DIM)]
        context_t = context[:, pl.ds(at, 2 * HEAD_DIM)].T
        d_context_t = d_context[:, pl.ds(at, 2 * HEAD_DIM)].T
        scaled = []
        dots = []
        for k in range(2):
            rows = slice(k * HEAD_DIM, (k + 1) * HEAD_DIM)
            own = d_context_t[rows].astype(F32) * inverse[pair, k : k + 1]
            dots.append(jnp.sum(own * context_t[rows].astype(F32), axis=0, keepdims=True))
            scaled.append(own.astype(LOW))
        both = jnp.concatenate(scaled, axis=0).T
        for k in range(2):
            rows = slice(k * HEAD_DIM, (k + 1) * HEAD_DIM)
            own_values = jnp.where(lane_of[k], values, jnp.zeros_like(values))
            powers = weights[2 * pair + k]
            d_scores = (powers.astype(F32) * (against(own_values, both) - dots[k])).astype(LOW)
            put = pl.multiple_of(at + k * HEAD_DIM, HEAD_DIM)
            d_packed[pl.ds(put, HEAD_DIM)] = (nn(keys_t[rows], d_scores) * HEAD_DIM ** (-0.5)).astype(LOW)
            d_packed[pl.ds(put + D, HEAD_DIM)] = against(queries_t[rows], d_scores).astype(LOW)
            d_packed[pl.ds(put + 2 * D, HEAD_DIM)] = against(scaled[k], powers).astype(LOW)
        return carry

    lax.fori_loop(0, 3, attend_back, 0)
    chunks[0].step(1)
    chunks[1].step(1)
    lax.fori_loop(3, HEADS // 2, attend_back, 0)

    for tile in range(rest):
        size = 8 * own_qkv
        result = nn(d_packed[tile * size : (tile + 1) * size], tokens[...])
        for d in range(8):
            owner = owners(rest)[tile * 8 + d]
            first = d * own_qkv
            shared_blocks[block_index(ORDERS[4], rest, *owner)] = result[first : first + rows_up].astype(LOW)
            shared_blocks[per + block_index(ORDERS[5], rest, *owner), : own_qkv - rows_up] = (
                result[first + rows_up : first + own_qkv].astype(LOW)
            )
    chunks[4].start(0)
    chunks[5].start(0)
    small[3:4] = against(ones, d_packed[0:D])[0:1]
    small[4:5] = against(ones, d_packed[2 * D : 3 * D])[0:1]
    tiny.sum_start()
    chunks[0].step(2)
    chunks[1].step(2)

    chunks[4].step(0)
    chunks[5].step(0)
    for k, rows in enumerate(blocks):
        d_tokens = nn(w_qkv[...], d_packed[:, rows]).T + d_hidden[rows]
        d_low[rows] = d_tokens.astype(LOW)
    token_copy = pltpu.make_async_copy(d_low, gtok_h, out_sem.at[1])
    token_copy.start()
    tiny.sum_step(0)
    chunks[2].step(1)
    chunks[3].step(1)
    sums[0][...] = chunks[0].finish()
    sums[1][...] = chunks[1].finish()
    tiny.sum_step(1)
    chunks[2].step(2)
    chunks[3].step(2)
    tiny.sum_step(2)
    chunks[4].step(1)
    chunks[5].step(1)
    sums[2][...] = chunks[2].finish()
    sums[3][...] = chunks[3].finish()
    small_out[...] = tiny.sum_end()
    tiny.gather_end()
    chunks[4].step(2)
    chunks[5].step(2)
    sums[4][...] = chunks[4].finish()
    sums[5][...] = chunks[5].finish()
    token_copy.wait()


def layer(rest, tokens, cotangent, lengths, labels, w_qkv, w_out, w_up, w_down, w_pool, w_class, biases, norm_gains, bias_up):
    per = 8 * rest
    rows_up = FF // per // 2
    rows_down = D // per
    vmem = pl.BlockSpec(memory_space=pltpu.VMEM)
    smem = pl.BlockSpec(memory_space=pltpu.SMEM)
    anywhere = pl.BlockSpec(memory_space=pl.ANY)
    dma = pltpu.SemaphoreType.DMA
    shapes = [(rows_down, FF // 2)] * 2 + [(rows_up, D)] * 4
    scratch = [
        pltpu.VMEM((SLOT, D), LOW),
        pltpu.VMEM((D, 3 * D), LOW),
        pltpu.VMEM((D, D), LOW),
        pltpu.VMEM((D, FF), LOW),
        pltpu.VMEM((FF, D), LOW),
        pltpu.VMEM((SLOT, 3 * D), LOW),
        pltpu.VMEM((HEADS, SLOT, SLOT), LOW),
        pltpu.VMEM((HEADS // 2, 2, SLOT), F32),
        pltpu.VMEM((SLOT, D), LOW),
        pltpu.VMEM((SLOT, D), F32),
        pltpu.VMEM((SLOT, D), LOW),
        pltpu.VMEM((SLOT, FF), LOW),
        pltpu.VMEM((SLOT, FF), LOW),
        pltpu.VMEM((SLOT, D), F32),
        pltpu.VMEM((SLOT, D), LOW),
        pltpu.VMEM((3 * D, SLOT), LOW),
        pltpu.VMEM((2 * per, rows_down, FF // 2), LOW),
        pltpu.VMEM((SLOT, 1), F32),
        pltpu.VMEM((16, D), F32),
        pltpu.VMEM((2, D), F32),
        dma((8,)),
        dma((3,)),
    ] + small_scratch(rest)
    for order, (rows, width) in zip(ORDERS, shapes):
        scratch += staged_scratch(rest, order, rows, width) + [dma((4,)), dma((4,)), dma((rest - 1,)), dma((rest - 1,))]
    outs = [jax.ShapeDtypeStruct((SLOT, D), LOW)] * 2 + [jax.ShapeDtypeStruct(shape, F32) for shape in shapes] + [
        jax.ShapeDtypeStruct((16, D), F32),
        jax.ShapeDtypeStruct((rest, 2, 2, 2, 2, D), F32),
        jax.ShapeDtypeStruct((1, 128), F32),
    ]
    return pl.pallas_call(
        functools.partial(layer_kernel, rest),
        out_shape=tuple(outs),
        in_specs=[smem, smem] + [vmem] * 4 + [anywhere] * 7,
        out_specs=tuple([anywhere] * 2 + [vmem] * 9),
        scratch_shapes=scratch,
        compiler_params=pltpu.CompilerParams(
            collective_id=0, has_side_effects=True, vmem_limit_bytes=61 << 20
        ),
    )(lengths, labels, biases, norm_gains, bias_up.reshape(1, FF), w_class, tokens, cotangent, w_qkv, w_out, w_up, w_down, w_pool)


def finish_kernel(rest, *refs):
    out_in, gtok_in, down1, down2, up1, up2, last1, last2, small, everyone, loss = refs[:11]
    (out, gtok, losses, g_qkv, g_out, g_up, g_down, g_pool, g_class, g_biases, g_gains, g_bias_up, g_pool_bias) = refs[11:24]
    sem = refs[24]
    copies = [pltpu.make_async_copy(out_in, out, sem.at[0]), pltpu.make_async_copy(gtok_in, gtok, sem.at[1])]
    for copy in copies:
        copy.start()
    per = 8 * rest
    rank = lax.axis_index("batch") * 4 + lax.axis_index("head")
    own = D // per
    own_qkv = 3 * own
    own_up = FF // per
    rows_up = own_up // 2
    losses[...] = loss[0:1, 0:1]
    g_down[0 : FF // 2] = down1[...].T
    g_down[FF // 2 : FF] = down2[...].T
    g_up[...] = jnp.concatenate([up1[...], up2[...]], axis=0).T
    last = jnp.concatenate([last1[...], last2[...]], axis=0).T
    g_qkv[...] = last[:, :own_qkv]
    g_out[...] = last[:, own_qkv:]

    def window(array, start, size):
        at = lax.broadcasted_iota(jnp.int32, (D, size), 0)
        want = lax.broadcasted_iota(jnp.int32, (D, size), 1)
        return exact(array, (at == want + start).astype(F32))

    picked = window(small[...], rank * own, own)
    g_class[...] = picked[0:3]
    g_biases[...] = picked[3:9]
    g_gains[...] = picked[9:11]
    g_pool_bias[...] = picked[15:16]
    flat = rank * own_up
    part = flat // D
    rows = small[11:15]
    pick = lax.broadcasted_iota(jnp.int32, (4, 1), 0) == part
    chosen = jnp.sum(jnp.where(pick, rows, 0.0), axis=0, keepdims=True)
    g_bias_up[...] = window(jnp.broadcast_to(chosen, (8, D)), flat - part * D, own_up)[0:1]
    leading = everyone[:, 0]
    d_pre = window(everyone[:, 1], rank * own, own)
    g_pool[...] = lax.dot_general(
        leading, d_pre, (((0,), (0,)), ((), ())), precision=lax.Precision.HIGHEST, preferred_element_type=F32
    )
    for copy in copies:
        copy.wait()


def finish(rest, results):
    per = 8 * rest
    own = D // per
    vmem = pl.BlockSpec(memory_space=pltpu.VMEM)
    anywhere = pl.BlockSpec(memory_space=pl.ANY)
    shape = lambda *s: jax.ShapeDtypeStruct(s, F32)
    results = list(results)
    results[9] = results[9].reshape(per, 2, D)
    outs = [jax.ShapeDtypeStruct((SLOT, D), LOW)] * 2 + [
        shape(1, 1), shape(D, 3 * own), shape(D, own), shape(D, 4 * own), shape(FF, own), shape(D, own),
        shape(3, own), shape(6, own), shape(2, own), shape(1, 4 * own), shape(1, own),
    ]
    out = list(pl.pallas_call(
        functools.partial(finish_kernel, rest),
        out_shape=tuple(outs),
        in_specs=[anywhere] * 2 + [vmem] * 9,
        out_specs=tuple([anywhere] * 2 + [vmem] * 11),
        scratch_shapes=[pltpu.SemaphoreType.DMA((2,))],
        compiler_params=pltpu.CompilerParams(vmem_limit_bytes=32 << 20),
    )(*results))
    for i in (2, 11, 12):
        out[i] = out[i].reshape(-1)
    return tuple(out)


def per_device(
    tokens,
    cotangent,
    lengths,
    labels,
    w_qkv,
    w_out,
    w_up,
    w_down,
    w_pool,
    w_class,
    biases,
    norm_gains,
    bias_up,
):
    rest = lax.axis_size("batch") // 2
    if D // (8 * rest) % 8 == 0:
        return finish(rest, layer(
            rest, tokens, cotangent, lengths, labels, w_qkv, w_out, w_up, w_down, w_pool, w_class, biases, norm_gains,
            bias_up,
        ))
    head_rank = lax.axis_index("head")
    rank = lax.axis_index("batch") * 4 + head_rank
    length = lax.dynamic_index_in_dim(lengths, head_rank, keepdims=False)
    label = lax.dynamic_index_in_dim(labels, head_rank, keepdims=False)
    slot_live = (jnp.arange(SLOT) < length).astype(F32)
    zeros_key = jnp.zeros((D,), F32)
    packed = jnp.dot(tokens, w_qkv, preferred_element_type=F32) + jnp.concatenate(
        [biases[0], zeros_key, biases[1]]
    )
    packed = packed.astype(LOW)
    context, probs = attention(packed, length)
    attn = jnp.dot(context, w_out, preferred_element_type=F32) + biases[2]
    first_sum = tokens.astype(F32) + attn
    norm_one, first_pull = jax.vjp(layer_norm, first_sum, norm_gains[0], biases[3])
    norm_low = norm_one.astype(LOW)
    hidden_up = jnp.dot(norm_low, w_up, preferred_element_type=F32) + bias_up
    activated_full, gelu_pull = jax.vjp(exact_gelu, hidden_up)
    activated = activated_full.astype(LOW)
    branch = jnp.dot(activated, w_down, preferred_element_type=F32) + biases[4]
    out_full, second_pull = jax.vjp(layer_norm, norm_one + branch, norm_gains[1], biases[5])
    leading = out_full[:1].astype(LOW)
    pooled = jnp.tanh(jnp.dot(leading, w_pool, preferred_element_type=F32) + biases[6])
    pooled_low = pooled.astype(LOW)
    logits = against(pooled_low, w_class)
    onehot = (jnp.arange(CLASSES)[None, :] == label).astype(F32)
    losses = jax.nn.logsumexp(logits, axis=-1) - jnp.sum(onehot * logits, axis=-1)
    d_logits = jax.nn.softmax(logits, axis=-1) - onehot
    g_class = exact(d_logits.T, pooled_low.astype(F32))
    d_pre = exact(d_logits, w_class.astype(F32)) * (1.0 - pooled * pooled)
    d_leading = exact(d_pre, w_pool.astype(F32).T)
    d_out = cotangent.astype(F32) * slot_live[:, None]
    d_out = d_out.at[0].add(d_leading[0])
    d_h2, g_gain_two, g_shift_two = second_pull(d_out)
    d_branch = d_h2.astype(LOW)
    g_bias_down = jnp.sum(d_branch.astype(F32), axis=0)
    g_down_t = inner(d_branch, activated)
    d_activated = against(d_branch, w_down)
    d_up = gelu_pull(d_activated)[0].astype(LOW)
    g_bias_up = jnp.sum(d_up.astype(F32), axis=0)
    g_up_t = inner(d_up, norm_low)
    d_norm_one = d_h2 + against(d_up, w_up)
    d_h1, g_gain_one, g_shift_one = first_pull(d_norm_one)
    d_attn = d_h1.astype(LOW)
    g_bias_out = jnp.sum(d_attn.astype(F32), axis=0)
    g_out_t = inner(d_attn, context)
    d_context = against(d_attn, w_out).astype(LOW)
    d_packed = attention_back(packed, probs, d_context)
    g_qkv_t = inner(d_packed, tokens)
    column_sums = jnp.sum(d_packed.astype(F32), axis=0)
    grad_tokens = (d_h1 + against(d_packed, w_qkv)).astype(LOW)
    small = jnp.concatenate(
        [
            g_class,
            jnp.stack([column_sums[:D], column_sums[2 * D :], g_bias_out, g_shift_one, g_bias_down, g_shift_two]),
            jnp.stack([g_gain_one, g_gain_two]),
            g_bias_up.reshape(FF // D, D),
            d_pre,
        ]
    )
    lead = jnp.concatenate([leading.astype(F32), d_pre])
    down = owner_blocks(g_down_t, rest, FF)
    up = owner_blocks(g_up_t, rest, D)
    last = jnp.concatenate([owner_blocks(g_qkv_t, rest, D), owner_blocks(g_out_t, rest, D)], axis=4)
    half = up.shape[4] // 2
    parts = [
        down[..., : FF // 2], down[..., FF // 2 :],
        up[..., :half, :], up[..., half:, :],
        last[..., :half, :], last[..., half:, :],
    ]
    *sums, small, everyone = reduce_gradients(rest, parts, small, lead)
    g_down = jnp.concatenate(sums[0:2], axis=1).T
    g_up = jnp.concatenate(sums[2:4], axis=0).T
    g_last = jnp.concatenate(sums[4:6], axis=0).T
    own_qkv = 3 * D // (8 * rest)
    own = D // (8 * rest)
    everyone = everyone.reshape(8 * rest, 2, D)
    window = lax.dynamic_slice_in_dim(small, rank * own, own, axis=1)
    pre_window = lax.dynamic_slice_in_dim(everyone[:, 1], rank * own, own, axis=1)
    g_pool = lax.dot_general(
        everyone[:, 0], pre_window, (((0,), (0,)), ((), ())),
        precision=lax.Precision.HIGHEST, preferred_element_type=F32,
    )
    own_up = FF // (8 * rest)
    g_bias_up = lax.dynamic_slice_in_dim(small[11:15].reshape(FF), rank * own_up, own_up)
    return (
        out_full.astype(LOW),
        grad_tokens,
        losses,
        g_last[:, :own_qkv],
        g_last[:, own_qkv:],
        g_up,
        g_down,
        g_pool,
        window[:3],
        window[3:9],
        window[9:11],
        g_bias_up,
        window[15],
    )


def solution(mesh):
    return jax.shard_map(
        per_device,
        mesh=mesh,
        in_specs=(
            P(("batch", "head"), None),
            P(("batch", "head"), None),
            P("batch"),
            P("batch"),
            P(),
            P(),
            P(),
            P(),
            P(),
            P(),
            P(),
            P(),
            P(),
        ),
        out_specs=(
            P(("batch", "head"), None),
            P(("batch", "head"), None),
            P(("batch", "head")),
            P(None, ("batch", "head")),
            P(None, ("batch", "head")),
            P(None, ("batch", "head")),
            P(None, ("batch", "head")),
            P(None, ("batch", "head")),
            P(None, ("batch", "head")),
            P(None, ("batch", "head")),
            P(None, ("batch", "head")),
            P(("batch", "head")),
            P(("batch", "head")),
        ),
        check_vma=False,
    )
```

```python
import functools

import jax
import jax.numpy as jnp
from jax import lax
from jax.experimental import pallas as pl
from jax.experimental.pallas import tpu as pltpu
from jax.sharding import PartitionSpec as P

D = 768
HEADS = 12
HEAD_DIM = 64
FF = 3072
CLASSES = 3
SLOT = 512
MESH = pl.DeviceIdType.MESH
LOW = jnp.bfloat16
F32 = jnp.float32


def layer_norm(hidden, gain, shift):
    center = hidden - jnp.mean(hidden, axis=-1, keepdims=True)
    spread = jnp.mean(center * center, axis=-1, keepdims=True)
    return center * lax.rsqrt(spread + 1e-12) * gain + shift


def exact_gelu(hidden):
    return jax.nn.gelu(hidden, approximate=False)


def inner(left, right):
    return lax.dot_general(
        left, right, (((0,), (0,)), ((), ())), preferred_element_type=jnp.float32
    )


def against(left, right):
    return lax.dot_general(
        left, right, (((1,), (1,)), ((), ())), preferred_element_type=jnp.float32
    )


def exact(left, right):
    return jnp.dot(left, right, precision=lax.Precision.HIGHEST, preferred_element_type=jnp.float32)


class Place:
    def __init__(self, rest):
        batch = lax.axis_index("batch")
        head = lax.axis_index("head")
        self.rest = rest
        self.z = batch // 2
        self.y = lax.rem(batch, 2)
        self.x = head // 2
        self.c = lax.rem(head, 2)

    def device(self, z, y, x, c):
        return (z * 2 + y, x * 2 + c)

    def core_peer(self):
        return self.device(self.z, self.y, self.x, 1 - self.c)

    def x_peer(self):
        return self.device(self.z, self.y, 1 - self.x, self.c)

    def y_peer(self):
        return self.device(self.z, 1 - self.y, self.x, self.c)

    def z_at(self, offset):
        return lax.rem(self.z + offset, self.rest)

    def z_peer(self, offset):
        return self.device(self.z_at(offset), self.y, self.x, self.c)

    def barrier(self):
        sem = pltpu.get_barrier_semaphore()
        for peer in (self.core_peer(), self.x_peer(), self.y_peer()):
            pl.semaphore_signal(sem, inc=1, device_id=peer, device_id_type=MESH)
        for offset in range(1, self.rest):
            pl.semaphore_signal(sem, inc=1, device_id=self.z_peer(offset), device_id_type=MESH)
        pl.semaphore_wait(sem, 3 + self.rest - 1)


def remote(src, dst, send, recv, peer):
    return pltpu.make_async_remote_copy(
        src_ref=src, dst_ref=dst, send_sem=send, recv_sem=recv, device_id=peer, device_id_type=MESH
    )


class Reduce:
    def __init__(self, place, part, bufs, sems, x_first):
        self.place, self.part, self.x_first = place, part, x_first
        self.r1, self.r2, self.r3, self.r4 = bufs
        send, recv, zsend, zrecv = sems
        p = place
        if x_first:
            far, near, second_far, second_near = (1 - p.x, p.x, 1 - p.y, p.y)
            peers = (p.x_peer(), p.y_peer())
            src2 = self.r1.at[far]
        else:
            far, near, second_far, second_near = (1 - p.y, p.y, 1 - p.x, p.x)
            peers = (p.y_peer(), p.x_peer())
            src2 = self.r1.at[:, far]
        self.near, self.second_near = near, second_near
        self.copies = [
            remote(part.at[1 - p.c], self.r1, send.at[0], recv.at[0], p.core_peer()),
            remote(src2, self.r2, send.at[1], recv.at[1], peers[0]),
            remote(self.r2.at[second_far], self.r3, send.at[2], recv.at[2], peers[1]),
        ]
        self.last = [
            remote(self.r3.at[p.z_at(k)], self.r4.at[k - 1], zsend.at[k - 1], zrecv.at[k - 1], p.z_peer(k))
            for k in range(1, p.rest)
        ]

    def start(self):
        self.copies[0].start()

    def step1(self):
        p = self.place
        self.copies[0].wait()
        for i in range(2):
            for j in range(2):
                def add(k, carry, i=i, j=j):
                    self.r1[i, j, k] = self.r1[i, j, k] + self.part[p.c, i, j, k]
                    return carry
                lax.fori_loop(0, p.rest, add, 0)
        self.copies[1].start()

    def step2(self):
        p = self.place
        self.copies[1].wait()
        for i in range(2):
            def add(k, carry, i=i):
                own = self.r1[self.near, i, k] if self.x_first else self.r1[i, self.near, k]
                self.r2[i, k] = self.r2[i, k] + own
                return carry
            lax.fori_loop(0, p.rest, add, 0)
        self.copies[2].start()

    def step3(self):
        p = self.place
        self.copies[2].wait()

        def add(k, carry):
            self.r3[k] = self.r3[k] + self.r2[self.second_near, k]
            return carry
        lax.fori_loop(0, p.rest, add, 0)
        for copy in self.last:
            copy.start()

    def total(self):
        p = self.place
        for copy in self.last:
            copy.wait()
        result = self.r3[p.z].astype(F32)
        for k in range(1, p.rest):
            result = result + self.r4[k - 1].astype(F32)
        return result


def chunk_scratch(rest, rows, width):
    return [
        pltpu.VMEM((2, 2, rest, rows, width), LOW),
        pltpu.VMEM((2, rest, rows, width), LOW),
        pltpu.VMEM((rest, rows, width), LOW),
        pltpu.VMEM((rest - 1, rows, width), LOW),
        pltpu.SemaphoreType.DMA((3,)),
        pltpu.SemaphoreType.DMA((3,)),
        pltpu.SemaphoreType.DMA((rest - 1,)),
        pltpu.SemaphoreType.DMA((rest - 1,)),
    ]


class Small:
    def __init__(self, place, small, lead, everyone, bufs):
        got, gotz, send, recv, zsend, zrecv, gsend, grecv, gzsend, gzrecv = bufs
        p = place
        self.place, self.small, self.got, self.gotz = p, small, got, gotz
        self.lead, self.everyone = lead, everyone
        peers = (p.core_peer(), p.x_peer(), p.y_peer())
        blocks = (
            everyone.at[p.z, p.y, p.x, p.c], everyone.at[p.z, p.y, p.x], everyone.at[p.z, p.y],
        )
        self.sums = [remote(small, got.at[i], send.at[i], recv.at[i], peers[i]) for i in range(3)]
        self.sum_last = [
            remote(small, gotz.at[k - 1], zsend.at[k - 1], zrecv.at[k - 1], p.z_peer(k)) for k in range(1, p.rest)
        ]
        self.gathers = [remote(blocks[i], blocks[i], gsend.at[i], grecv.at[i], peers[i]) for i in range(3)]
        self.gather_last = [
            remote(everyone.at[p.z], everyone.at[p.z], gzsend.at[k - 1], gzrecv.at[k - 1], p.z_peer(k))
            for k in range(1, p.rest)
        ]

    def gather_start(self):
        p = self.place
        self.everyone[p.z, p.y, p.x, p.c] = self.lead[...]
        self.gathers[0].start()

    def gather_step(self, i):
        self.gathers[i].wait()
        if i < 2:
            self.gathers[i + 1].start()
        else:
            for copy in self.gather_last:
                copy.start()

    def gather_end(self):
        for copy in self.gather_last:
            copy.wait()

    def sum_start(self):
        self.sums[0].start()

    def sum_step(self, i):
        self.sums[i].wait()
        self.small[...] = self.small[...] + self.got[i]
        if i < 2:
            self.sums[i + 1].start()
        else:
            for copy in self.sum_last:
                copy.start()

    def sum_end(self):
        for copy in self.sum_last:
            copy.wait()
        total = self.small[...]
        for k in range(1, self.place.rest):
            total = total + self.gotz[k - 1]
        return total


def small_scratch(rest):
    return [
        pltpu.VMEM((3, 16, D), F32),
        pltpu.VMEM((rest - 1, 16, D), F32),
    ] + [pltpu.SemaphoreType.DMA((3,)), pltpu.SemaphoreType.DMA((3,)),
         pltpu.SemaphoreType.DMA((rest - 1,)), pltpu.SemaphoreType.DMA((rest - 1,))] * 2


def reduce_kernel(rest, n_chunks, *refs):
    parts = refs[:n_chunks]
    small_in, lead = refs[n_chunks : n_chunks + 2]
    outs = refs[n_chunks + 2 : 2 * n_chunks + 2]
    small_out, everyone = refs[2 * n_chunks + 2 : 2 * n_chunks + 4]
    scratch = refs[2 * n_chunks + 4 :]
    place = Place(rest)
    chunks = []
    for i in range(n_chunks):
        own = scratch[8 * i : 8 * i + 8]
        chunks.append(Reduce(place, parts[i], own[:4], own[4:], i % 2 == 0))
    rest_scratch = scratch[8 * n_chunks :]
    small = Small(place, rest_scratch[0], lead, everyone, rest_scratch[1:])
    rest_scratch[0][...] = small_in[...]
    place.barrier()
    small.gather_start()
    small.sum_start()
    steps = [[c.step1, c.step2, c.step3] for c in chunks]
    for chunk in chunks:
        chunk.start()
    for i in range(3):
        small.gather_step(i)
        small.sum_step(i)
    for phase in range(n_chunks + 4):
        for i in range(n_chunks):
            k = phase - i
            if i % 2 == 1:
                k = phase - i + 1
            if 0 <= k < 3:
                steps[i][k]()
            if k == 3:
                outs[i][...] = chunks[i].total()
    small.gather_end()
    small_out[...] = small.sum_end()


def reduce_gradients(rest, parts, small, lead):
    vmem = pl.BlockSpec(memory_space=pltpu.VMEM)
    scratch = []
    for part in parts:
        scratch += chunk_scratch(rest, *part.shape[4:])
    scratch += [pltpu.VMEM((16, D), F32)] + small_scratch(rest)
    outs = [jax.ShapeDtypeStruct(part.shape[4:], F32) for part in parts]
    outs += [
        jax.ShapeDtypeStruct((16, D), F32),
        jax.ShapeDtypeStruct((rest, 2, 2, 2, 2, D), F32),
    ]
    return pl.pallas_call(
        functools.partial(reduce_kernel, rest, len(parts)),
        out_shape=tuple(outs),
        in_specs=[vmem] * (len(parts) + 2),
        out_specs=tuple([vmem] * len(outs)),
        scratch_shapes=scratch,
        compiler_params=pltpu.CompilerParams(
            collective_id=0, has_side_effects=True, vmem_limit_bytes=60 << 20
        ),
    )(*parts, small, lead)


def owner_blocks(grad_t, rest, width):
    rows = grad_t.shape[0] // (8 * rest)
    view = grad_t.astype(LOW).reshape(rest, 2, 2, 2, rows, width)
    return view.transpose(3, 2, 1, 0, 4, 5)


def attention(packed, length):
    heads = packed.reshape(SLOT, 3, HEADS, HEAD_DIM)
    queries, keys_all, values = heads[:, 0], heads[:, 1], heads[:, 2]
    scores = jnp.einsum("qhd,khd->hqk", queries, keys_all, preferred_element_type=F32) * HEAD_DIM ** (-0.5)
    scores = jnp.where((jnp.arange(SLOT) < length)[None, None, :], scores, -1e30)
    row_max = jnp.max(scores, axis=-1, keepdims=True)
    weights = jnp.exp(scores - row_max)
    weights = weights / jnp.sum(weights, axis=-1, keepdims=True)
    low = weights.astype(LOW)
    context = jnp.einsum("hqk,khd->qhd", low, values, preferred_element_type=F32)
    return context.astype(LOW).reshape(SLOT, D), low


def attention_back(packed, low, d_context):
    heads = packed.reshape(SLOT, 3, HEADS, HEAD_DIM)
    queries, keys_all, values = heads[:, 0], heads[:, 1], heads[:, 2]
    d_heads = d_context.reshape(SLOT, HEADS, HEAD_DIM)
    weights = low.astype(F32)
    d_weights = jnp.einsum("qhd,khd->hqk", d_heads, values, preferred_element_type=F32)
    d_values = jnp.einsum("hqk,qhd->khd", low, d_heads, preferred_element_type=F32)
    row_dot = jnp.sum(weights * d_weights, axis=-1, keepdims=True)
    d_scores = (weights * (d_weights - row_dot)).astype(LOW)
    scale = HEAD_DIM ** (-0.5)
    d_queries = jnp.einsum("hqk,khd->qhd", d_scores, keys_all, preferred_element_type=F32) * scale
    d_keys = jnp.einsum("hqk,qhd->khd", d_scores, queries, preferred_element_type=F32) * scale
    return jnp.stack([d_queries, d_keys, d_values], axis=1).astype(LOW).reshape(SLOT, 3 * D)


def nn(left, right):
    return jnp.dot(left, right, preferred_element_type=F32)


def aligned(index, step):
    return pl.ds(pl.multiple_of(index * step, step), step)


def column_sum(ones, array):
    return nn(ones, array)[0:1]


def normalized(hidden):
    center = hidden - jnp.mean(hidden, axis=-1, keepdims=True)
    spread = jnp.mean(center * center, axis=-1, keepdims=True)
    scale = lax.rsqrt(spread + 1e-12)
    return center * scale, scale


def normalized_back(normed, scale, d_normed):
    first = jnp.mean(d_normed, axis=-1, keepdims=True)
    second = jnp.mean(d_normed * normed, axis=-1, keepdims=True)
    return scale * (d_normed - first - normed * second)


class Unit:
    def __init__(self, place, order, part, bufs, send, recv, put):
        p = self.place = place
        self.put = put
        self.at = 0
        self.legs = []
        bufs = list(bufs)
        count = part.shape[0] // 2
        held = bufs.pop(0)
        copy = remote(part.at[pl.ds((1 - p.c) * count, count)], held, send.at[0], recv.at[0], p.core_peer())
        self.legs.append((copy.start, self.pair_end(copy, held, part, p.c * count, count, False)))
        base = 0
        slot = 1
        for i, axis in enumerate(order):
            last = i == len(order) - 1
            if axis == "z":
                count = count // 4
                self.line(held, base, count, bufs.pop(0), bufs.pop(0), send, recv, slot, last)
                base = base + p.z * count
                slot += 3
            else:
                count = count // 2
                mine, peer = (p.x, p.x_peer()) if axis == "x" else (p.y, p.y_peer())
                got = bufs.pop(0)
                copy = remote(held.at[pl.ds(base + (1 - mine) * count, count)], got, send.at[slot], recv.at[slot], peer)
                self.legs.append((copy.start, self.pair_end(copy, got, held, base + mine * count, count, last)))
                held, base = got, 0
                slot += 1

    def pair_end(self, copy, got, own, start, count, last):
        def end():
            copy.wait()
            if last:
                self.put(got[0].astype(F32) + own[start].astype(F32))
            else:
                got[...] = got[...] + own[pl.ds(start, count)]
        return end

    def line(self, held, base, n, wide, single, send, recv, slot, last):
        p = self.place
        z = p.z
        outer = jnp.logical_or(z == 0, z == 3)
        inner = jnp.logical_not(outer)
        low = z < 2
        near = jnp.where(low, 1 - z, 5 - z)
        far = jnp.where(low, z + 2, z - 2)
        middle = 3 - z

        def at(block, count=n):
            return held.at[pl.ds(base + block * n, count)]

        def device(block):
            return p.device(block, p.y, p.x, p.c)

        outward = remote(at(jnp.where(z == 0, 1, 0), 3 * n), wide, send.at[slot], recv.at[slot], device(near))
        back = remote(at(near), wide.at[0:n], send.at[slot], recv.at[slot], device(near))
        across = remote(at(middle), single, send.at[slot + 1], recv.at[slot + 1], device(middle))
        beyond = remote(at(far), wide.at[n : 2 * n], send.at[slot + 2], recv.at[slot + 2], device(far))

        def begin_first():
            @pl.when(outer)
            def _():
                outward.start()

            @pl.when(inner)
            def _():
                back.start()

        def end_first():
            @pl.when(outer)
            def _():
                outward.wait_send()
                back.wait_recv()

            @pl.when(inner)
            def _():
                back.wait_send()
                outward.wait_recv()
                start = base + jnp.where(z == 1, n, 0)
                held[pl.ds(start, 3 * n)] = held[pl.ds(start, 3 * n)] + wide[...]

        def begin_second():
            @pl.when(inner)
            def _():
                across.start()
                beyond.start()

        def end_second():
            @pl.when(outer)
            def _():
                beyond.wait_recv()
                total = held[pl.ds(base + z * n, n)].astype(F32) + wide[0:n].astype(F32) + wide[n : 2 * n].astype(F32)
                if last:
                    self.put(total[0])
                else:
                    held[pl.ds(base + z * n, n)] = total.astype(LOW)

            @pl.when(inner)
            def _():
                across.wait()
                beyond.wait_send()
                total = held[pl.ds(base + z * n, n)].astype(F32) + single[...].astype(F32)
                if last:
                    self.put(total[0])
                else:
                    held[pl.ds(base + z * n, n)] = total.astype(LOW)

        self.legs.append((begin_first, end_first))
        self.legs.append((begin_second, end_second))

    def step(self):
        if self.at > 0:
            self.legs[self.at - 1][1]()
        if self.at < len(self.legs):
            self.legs[self.at][0]()
        self.at += 1


class Gather:
    def __init__(self, tiny):
        self.steps = [tiny.gather_start] + [functools.partial(tiny.gather_step, i) for i in range(3)] + [tiny.gather_end]

    def step(self):
        self.steps.pop(0)()


class Total:
    def __init__(self, tiny, put):
        self.steps = [tiny.sum_start] + [functools.partial(tiny.sum_step, i) for i in range(3)]
        self.steps.append(lambda: put(tiny.sum_end()))

    def step(self):
        self.steps.pop(0)()


def block_index(order, rest, z, y, x, c):
    sizes = {"x": 2, "y": 2, "z": rest}
    at = {"x": x, "y": y, "z": z}
    index = c
    for axis in order:
        index = index * sizes[axis] + at[axis]
    return index


def owners(rest):
    return [(z, y, x, c) for z in range(rest) for y in range(2) for x in range(2) for c in range(2)]


def unit_scratch(order, rows, width):
    blocks = 16
    bufs = [pltpu.VMEM((blocks, rows, width), LOW)]
    for axis in order:
        if axis == "z":
            blocks = blocks // 4
            bufs += [pltpu.VMEM((3 * blocks, rows, width), LOW), pltpu.VMEM((blocks, rows, width), LOW)]
        else:
            blocks = blocks // 2
            bufs.append(pltpu.VMEM((blocks, rows, width), LOW))
    return bufs + [pltpu.SemaphoreType.DMA((6,)), pltpu.SemaphoreType.DMA((6,))]


ORDERS = ("xyz", "xyz", "zxy", "yzx", "yzx", "zxy", "xzy", "yxz", "xzy", "yxz", "xzy", "yxz")
UNIT_PART = (0, 1, 2, 3, 0, 1, 2, 3, 0, 1, 2, 3)
PLAN = (
    (),
    (),
    (),
    (),
    (),
    (0, 12),
    (1, 2, 3),
    (),
    (),
    (12,),
    (),
    (),
    (),
    (3, 4, 5, 6, 7, 0, 2, 12),
    (1,),
    (),
    (8,),
    (),
    (3, 6, 2),
    (),
    (12,),
    (3, 0, 2),
    (8, 1, 5, 3),
    (),
    (9, 13, 10, 11, 2, 4, 7, 6, 0, 5, 1, 13, 7, 0, 6, 1, 5, 10, 8, 9, 6, 13, 4, 11, 5, 7, 8, 9, 10, 11, 8, 13, 7, 4, 9, 4, 11, 10, 9, 10, 11),
)
N_IN = 13
N_OUT = 9


def layer_kernel(rest, *refs):
    (lengths, labels, biases, gains, bias_up, w_class, tokens_h, cot_h, wqkv_h, wout_h, wup_h, wdown_h, wpool_h) = refs[:N_IN]
    out_h, gtok_h, down_out, up_out, qkv_out, attn_out, small_out, everyone, loss_out = refs[N_IN : N_IN + N_OUT]
    scratch = list(refs[N_IN + N_OUT :])
    (
        tokens, w_qkv, w_out, w_up, w_down, packed, weights, inverse, context, normed_one, norm_low,
        activated, slope, d_hidden, d_low, d_packed, part0, part1, part2, part3, scale_one, small, lead, in_sem, out_sem,
    ) = scratch[:25]
    parts = [part0, part1, part2, part3]
    cot = d_low
    d_context = norm_low
    wide = SLOT
    pool_wide = d_packed.at[0:D]
    pool_rest = d_packed.at[D : 2 * D, 0 : D - wide]
    out_wide = d_packed.at[2 * D : 2 * D + SLOT]
    out_rest = d_packed.at[D : D + SLOT, wide // 2 : wide // 2 + D - wide]
    place = Place(rest)
    small_bufs = scratch[25:35]
    unit_bufs = scratch[35:]
    head_rank = lax.axis_index("head")
    length = lengths[head_rank]
    label = labels[head_rank]
    loads = [
        pltpu.make_async_copy(src, dst, in_sem.at[i])
        for i, (src, dst) in enumerate(
            [(tokens_h, tokens), (wqkv_h, w_qkv), (wout_h, w_out), (wup_h, w_up),
             (wdown_h, w_down), (cot_h, cot), (wpool_h.at[:, 0:wide], pool_wide), (wpool_h.at[:, wide:D], pool_rest)]
        )
    ]
    loads[0].start()
    loads[1].start()
    sem = pltpu.get_barrier_semaphore()
    for peer in (place.core_peer(), place.x_peer(), place.y_peer()):
        pl.semaphore_signal(sem, inc=1, device_id=peer, device_id_type=MESH)
    for offset in range(1, rest):
        pl.semaphore_signal(sem, inc=1, device_id=place.z_peer(offset), device_id_type=MESH)

    height = D // 32
    order_of = owners(rest)

    def put_down(i):
        return lambda total: down_out.__setitem__((slice(None), slice(i * D, (i + 1) * D)), total)

    def put_rows(ref, i):
        return lambda total: ref.__setitem__(slice(i * height, (i + 1) * height), total)

    tiny = Small(place, small, lead, everyone, small_bufs)
    puts = [put_down(i) for i in range(4)] + [put_rows(up_out, i) for i in range(4)] + [put_rows(attn_out, 0)]
    puts += [put_rows(qkv_out, i) for i in range(3)]
    units = []
    at = 0
    for i, order in enumerate(ORDERS):
        size = len(unit_scratch(order, height, D))
        own = unit_bufs[at : at + size]
        at += size
        units.append(Unit(place, order, parts[UNIT_PART[i]], own[:-2], own[-2], own[-1], puts[i]))
    units.append(Gather(tiny))
    units.append(Total(tiny, lambda total: small_out.__setitem__(Ellipsis, total)))
    plan = list(PLAN)

    def steps():
        for i in plan.pop(0):
            units[i].step()

    loads[0].wait()
    loads[1].wait()
    for load in loads[2:]:
        load.start()
    ones = jnp.ones((8, SLOT), LOW)
    for part in range(3):
        columns = slice(part * D, part * D + D)
        result = nn(tokens[...], w_qkv[:, columns])
        if part == 0:
            result = (result + biases[0:1]).astype(LOW) * jnp.asarray(HEAD_DIM ** (-0.5), LOW)
        elif part == 2:
            result = (result + biases[1:2]).astype(LOW)
        else:
            result = result.astype(LOW)
        packed[:, columns] = result

    key_live = lax.broadcasted_iota(jnp.int32, (SLOT, 1), 0) < length
    lane = lax.broadcasted_iota(jnp.int32, (1, 2 * HEAD_DIM), 1)
    lane_of = [lane < HEAD_DIM, lane >= HEAD_DIM]

    def attend(pair, carry):
        at = pl.multiple_of(pair * 2 * HEAD_DIM, 2 * HEAD_DIM)
        queries = packed[:, pl.ds(at, 2 * HEAD_DIM)]
        keys_all = packed[:, pl.ds(at + D, 2 * HEAD_DIM)]
        values_t = packed[:, pl.ds(at + 2 * D, 2 * HEAD_DIM)].T
        got = []
        for k in range(2):
            own_keys = jnp.where(lane_of[k], keys_all, jnp.zeros_like(keys_all))
            scores = jnp.where(key_live, against(own_keys, queries), -1e30)
            powers = jnp.exp(scores - jnp.max(scores, axis=0, keepdims=True))
            inv = 1.0 / jnp.sum(powers, axis=0, keepdims=True)
            powers = powers.astype(LOW)
            weights[2 * pair + k] = powers
            inverse[pair, k : k + 1] = inv
            got.append(nn(values_t[k * HEAD_DIM : (k + 1) * HEAD_DIM], powers) * inv)
        context[:, pl.ds(at, 2 * HEAD_DIM)] = jnp.concatenate(got, axis=0).T.astype(LOW)
        return carry

    lax.fori_loop(0, HEADS // 2, attend, 0)

    blocks = [slice(0, SLOT // 2), slice(SLOT // 2, SLOT)]
    loads[2].wait()
    for rows in blocks:
        hidden = nn(context[rows], w_out[...]) + biases[2:3] + tokens[rows].astype(F32)
        normed, scale = normalized(hidden)
        normed_one[rows] = normed
        scale_one[rows] = scale
        norm_low[rows] = (normed * gains[0:1] + biases[3:4]).astype(LOW)

    loads[3].wait()

    def feed(tile, carry):
        columns = aligned(tile, D)
        hidden = nn(norm_low[...], w_up[:, columns]) + bias_up[0:1, columns]
        share = 0.5 + 0.5 * lax.erf(hidden * 0.7071067811865476)
        activated[:, columns] = (hidden * share).astype(LOW)
        slope[:, columns] = (share + hidden * (jnp.exp(-0.5 * hidden * hidden) * 0.3989422804014327)).astype(LOW)
        return carry

    lax.fori_loop(0, FF // D, feed, 0)

    for i in (4, 5, 6, 7):
        loads[i].wait()
    row = lax.broadcasted_iota(jnp.int32, (SLOT // 2, 1), 0)
    kept = []
    for k, rows in enumerate(blocks):
        hidden = nn(activated[rows], w_down[...]) + biases[4:5] + (normed_one[rows] * gains[0:1] + biases[3:4])
        normed, scale = normalized(hidden)
        result = normed * gains[1:2] + biases[5:6]
        low = result.astype(LOW)
        out_wide[rows] = low[:, 0:wide]
        out_rest[rows] = low[:, wide:D]
        d_hidden[rows] = normed
        kept.append(scale)
        if k == 0:
            leading = low[0:8]
    out_copies = [
        pltpu.make_async_copy(out_wide, out_h.at[:, 0:wide], out_sem.at[0]),
        pltpu.make_async_copy(out_rest, out_h.at[:, wide:D], out_sem.at[2]),
    ]
    for copy in out_copies:
        copy.start()

    pooled = jnp.concatenate([nn(leading, pool_wide[...]), nn(leading, pool_rest[...])], axis=1)
    pooled = jnp.tanh(pooled + biases[6:7])[0:1]
    pooled_low = pooled.astype(LOW).astype(F32)
    classes = w_class[...].astype(F32)
    logits = jnp.sum(pooled_low * classes, axis=-1, keepdims=True)
    top = jnp.max(logits, axis=0, keepdims=True)
    powers = jnp.exp(logits - top)
    total = jnp.sum(powers, axis=0, keepdims=True)
    onehot = (lax.broadcasted_iota(jnp.int32, (CLASSES, 1), 0) == label).astype(F32)
    loss_out[...] = jnp.broadcast_to(
        jnp.log(total) + top - jnp.sum(onehot * logits, axis=0, keepdims=True), loss_out.shape
    )
    d_logits = powers / total - onehot
    d_pre = jnp.sum(d_logits * classes, axis=0, keepdims=True) * (1.0 - pooled * pooled)
    high = d_pre.astype(LOW).astype(F32)
    middle = (d_pre - high).astype(LOW).astype(F32)
    low = d_pre - high - middle
    eight = lax.broadcasted_iota(jnp.int32, (8, 1), 0)
    split = jnp.where(eight == 0, high, jnp.where(eight == 1, middle, jnp.where(eight == 2, low, 0.0)))
    split = split.astype(LOW)
    d_leading = against(split[:, 0:wide], pool_wide[...]) + against(split[:, wide:D], pool_rest[...])
    d_leading = jnp.sum(d_leading, axis=0, keepdims=True)
    small[0:3] = d_logits * pooled_low
    small[15:16] = d_pre
    lead[0:1] = leading[0:1].astype(F32)
    lead[1:2] = d_pre

    shift_two = jnp.zeros((1, D), F32)
    gain_two = jnp.zeros((1, D), F32)
    for k in (1, 0):
        rows = blocks[k]
        normed, scale = d_hidden[rows], kept[k]
        d_out = jnp.where(row + k * (SLOT // 2) < length, cot[rows].astype(F32), 0.0)
        if k == 0:
            d_out = d_out + jnp.where(row == 0, d_leading, 0.0)
        shift_two = shift_two + jnp.sum(d_out, axis=0, keepdims=True)
        gain_two = gain_two + jnp.sum(d_out * normed, axis=0, keepdims=True)
        d_two = normalized_back(normed, scale, d_out * gains[1:2])
        d_hidden[rows] = d_two
        d_low[rows] = d_two.astype(LOW)
    small[8:9] = shift_two
    small[10:11] = gain_two
    small[7:8] = column_sum(ones, d_low[...])

    rows = height
    for copy in out_copies:
        copy.wait()
    pl.semaphore_wait(sem, 3 + rest - 1)
    units[12].step()
    d_branch_t = d_low[...].T
    for i in range(4):
        for columns in (slice(0, D // 2), slice(D // 2, D)):
            result = nn(d_branch_t, activated[:, i * D + columns.start : i * D + columns.stop])
            for d, owner in enumerate(order_of):
                parts[i][block_index(ORDERS[i], rest, *owner), :, columns] = result[d * rows : (d + 1) * rows].astype(LOW)
        units[i].step()
        steps()

    for tile in range(FF // D):
        columns = slice(tile * D, (tile + 1) * D)
        d_up = (against(d_low[...], w_down[columns]) * slope[:, columns].astype(F32)).astype(LOW)
        slope[:, columns] = d_up
        small[11 + tile : 12 + tile] = column_sum(ones, d_up)
        steps()
    d_up = slope

    for tile in range(FF // D):
        for columns in (slice(0, D // 2), slice(D // 2, D)):
            result = inner(d_up[:, tile * D : (tile + 1) * D], norm_low[:, columns])
            for d in range(8):
                owner = order_of[tile * 8 + d]
                for i in range(4):
                    first = (d * 4 + i) * rows
                    parts[i][block_index(ORDERS[4 + i], rest, *owner), :, columns] = result[first : first + rows].astype(LOW)
        if tile == 3:
            for i in range(4, 8):
                units[i].step()
        steps()

    shift_one = jnp.zeros((1, D), F32)
    gain_one = jnp.zeros((1, D), F32)
    for block in blocks:
        d_norm = d_hidden[block] + against(d_up[block], w_up[...])
        normed = normed_one[block]
        shift_one = shift_one + jnp.sum(d_norm, axis=0, keepdims=True)
        gain_one = gain_one + jnp.sum(d_norm * normed, axis=0, keepdims=True)
        d_one = normalized_back(normed, scale_one[block], d_norm * gains[0:1])
        d_hidden[block] = d_one
        d_low[block] = d_one.astype(LOW)
        steps()
    small[6:7] = shift_one
    small[9:10] = gain_one
    small[5:6] = column_sum(ones, d_low[...])

    result = inner(d_low[...], context[...])
    for d, owner in enumerate(order_of):
        parts[UNIT_PART[8]][block_index(ORDERS[8], rest, *owner)] = result[d * rows : (d + 1) * rows].astype(LOW)
    units[8].step()
    d_context[...] = against(d_low[...], w_out[...]).astype(LOW)
    steps()

    def attend_back(pair):
        at = pair * 2 * HEAD_DIM
        queries_t = packed[:, at : at + 2 * HEAD_DIM].T
        keys_t = packed[:, at + D : at + D + 2 * HEAD_DIM].T
        values = packed[:, at + 2 * D : at + 2 * D + 2 * HEAD_DIM]
        context_t = context[:, at : at + 2 * HEAD_DIM].T
        d_context_t = d_context[:, at : at + 2 * HEAD_DIM].T
        scaled = []
        dots = []
        for k in range(2):
            own_rows = slice(k * HEAD_DIM, (k + 1) * HEAD_DIM)
            own = d_context_t[own_rows].astype(F32) * inverse[pair, k : k + 1]
            dots.append(jnp.sum(own * context_t[own_rows].astype(F32), axis=0, keepdims=True))
            scaled.append(own.astype(LOW))
        both = jnp.concatenate(scaled, axis=0).T
        for k in range(2):
            own_rows = slice(k * HEAD_DIM, (k + 1) * HEAD_DIM)
            own_values = jnp.where(lane_of[k], values, jnp.zeros_like(values))
            powers = weights[2 * pair + k]
            d_scores = (powers.astype(F32) * (against(own_values, both) - dots[k])).astype(LOW)
            put = at + k * HEAD_DIM
            d_packed[put : put + HEAD_DIM] = (nn(keys_t[own_rows], d_scores) * HEAD_DIM ** (-0.5)).astype(LOW)
            d_packed[put + D : put + D + HEAD_DIM] = against(queries_t[own_rows], d_scores).astype(LOW)
            d_packed[put + 2 * D : put + 2 * D + HEAD_DIM] = against(scaled[k], powers).astype(LOW)

    for pair in range(HEADS // 2):
        attend_back(pair)
        steps()

    small[3:4] = against(ones, d_packed[0:D])[0:1]
    small[4:5] = against(ones, d_packed[2 * D : 3 * D])[0:1]
    units[13].step()
    for tile in range(rest):
        result = nn(d_packed[tile * 24 * rows : (tile + 1) * 24 * rows], tokens[...])
        for d in range(8):
            owner = order_of[tile * 8 + d]
            for i in range(3):
                first = (d * 3 + i) * rows
                parts[UNIT_PART[9 + i]][block_index(ORDERS[9 + i], rest, *owner)] = result[first : first + rows].astype(LOW)
    for i in range(9, 12):
        units[i].step()
    steps()

    for block in blocks:
        d_tokens = nn(w_qkv[...], d_packed[:, block]).T + d_hidden[block]
        d_low[block] = d_tokens.astype(LOW)
        steps()
    token_copy = pltpu.make_async_copy(d_low, gtok_h, out_sem.at[1])
    token_copy.start()
    steps()
    token_copy.wait()


def layer(rest, tokens, cotangent, lengths, labels, w_qkv, w_out, w_up, w_down, w_pool, w_class, biases, norm_gains, bias_up):
    rows = D // 32
    vmem = pl.BlockSpec(memory_space=pltpu.VMEM)
    smem = pl.BlockSpec(memory_space=pltpu.SMEM)
    anywhere = pl.BlockSpec(memory_space=pl.ANY)
    dma = pltpu.SemaphoreType.DMA
    scratch = [
        pltpu.VMEM((SLOT, D), LOW),
        pltpu.VMEM((D, 3 * D), LOW),
        pltpu.VMEM((D, D), LOW),
        pltpu.VMEM((D, FF), LOW),
        pltpu.VMEM((FF, D), LOW),
        pltpu.VMEM((SLOT, 3 * D), LOW),
        pltpu.VMEM((HEADS, SLOT, SLOT), LOW),
        pltpu.VMEM((HEADS // 2, 2, SLOT), F32),
        pltpu.VMEM((SLOT, D), LOW),
        pltpu.VMEM((SLOT, D), F32),
        pltpu.VMEM((SLOT, D), LOW),
        pltpu.VMEM((SLOT, FF), LOW),
        pltpu.VMEM((SLOT, FF), LOW),
        pltpu.VMEM((SLOT, D), F32),
        pltpu.VMEM((SLOT, D), LOW),
        pltpu.VMEM((3 * D, SLOT), LOW),
    ] + [pltpu.VMEM((32, rows, D), LOW)] * 4 + [
        pltpu.VMEM((SLOT, 1), F32),
        pltpu.VMEM((16, D), F32),
        pltpu.VMEM((2, D), F32),
        dma((8,)),
        dma((3,)),
    ] + small_scratch(rest)
    for order in ORDERS:
        scratch += unit_scratch(order, rows, D)
    outs = [jax.ShapeDtypeStruct((SLOT, D), LOW)] * 2 + [
        jax.ShapeDtypeStruct((rows, FF), F32),
        jax.ShapeDtypeStruct((4 * rows, D), F32),
        jax.ShapeDtypeStruct((3 * rows, D), F32),
        jax.ShapeDtypeStruct((rows, D), F32),
        jax.ShapeDtypeStruct((16, D), F32),
        jax.ShapeDtypeStruct((rest, 2, 2, 2, 2, D), F32),
        jax.ShapeDtypeStruct((1, 128), F32),
    ]
    return pl.pallas_call(
        functools.partial(layer_kernel, rest),
        out_shape=tuple(outs),
        in_specs=[smem, smem] + [vmem] * 4 + [anywhere] * 7,
        out_specs=tuple([anywhere] * 2 + [vmem] * 7),
        scratch_shapes=scratch,
        compiler_params=pltpu.CompilerParams(
            collective_id=0, has_side_effects=True, vmem_limit_bytes=61 << 20
        ),
    )(lengths, labels, biases, norm_gains, bias_up.reshape(1, FF), w_class, tokens, cotangent, w_qkv, w_out, w_up, w_down, w_pool)


def finish_kernel(rest, *refs):
    *moved, small, everyone, loss = refs[:9]
    targets = refs[9:15]
    losses, g_pool, g_class, g_biases, g_gains, g_bias_up, g_pool_bias = refs[15:22]
    *stages, sem_in, sem_out = refs[22:]
    arrive = [pltpu.make_async_copy(src, mid, sem_in.at[i]) for i, (src, mid) in enumerate(zip(moved, stages))]
    leave = [pltpu.make_async_copy(mid, dst, sem_out.at[i]) for i, (mid, dst) in enumerate(zip(stages, targets))]
    for copy in arrive:
        copy.start()
    for before, after in zip(arrive, leave):
        before.wait()
        after.start()
    rank = lax.axis_index("batch") * 4 + lax.axis_index("head")
    own = D // (8 * rest)
    own_up = 4 * own
    losses[...] = loss[0:1, 0:1]

    def window(array, start, size):
        at = lax.broadcasted_iota(jnp.int32, (D, size), 0)
        want = lax.broadcasted_iota(jnp.int32, (D, size), 1)
        return exact(array, (at == want + start).astype(F32))

    picked = window(small[...], rank * own, own)
    g_class[...] = picked[0:3]
    g_biases[...] = picked[3:9]
    g_gains[...] = picked[9:11]
    g_pool_bias[...] = picked[15:16]
    flat = rank * own_up
    part = flat // D
    pick = lax.broadcasted_iota(jnp.int32, (4, 1), 0) == part
    chosen = jnp.sum(jnp.where(pick, small[11:15], 0.0), axis=0, keepdims=True)
    g_bias_up[...] = window(jnp.broadcast_to(chosen, (8, D)), flat - part * D, own_up)[0:1]
    d_pre = window(everyone[:, 1], rank * own, own)
    g_pool[...] = lax.dot_general(
        d_pre, everyone[:, 0], (((0,), (0,)), ((), ())), precision=lax.Precision.HIGHEST, preferred_element_type=F32
    )
    for copy in leave:
        copy.wait()


def finish(rest, results):
    own = D // (8 * rest)
    vmem = pl.BlockSpec(memory_space=pltpu.VMEM)
    anywhere = pl.BlockSpec(memory_space=pl.ANY)
    shape = lambda *s: jax.ShapeDtypeStruct(s, F32)
    results = list(results)
    results[7] = results[7].reshape(8 * rest, 2, D)
    outs = [jax.ShapeDtypeStruct((SLOT, D), LOW)] * 2 + [
        shape(own, FF), shape(4 * own, D), shape(3 * own, D), shape(own, D),
        shape(1, 1), shape(own, D), shape(3, own), shape(6, own), shape(2, own), shape(1, 4 * own), shape(1, own),
    ]
    (out, gtok, down, up, qkv, attn, losses, pool, g_class, g_biases, g_gains, g_bias_up, g_pool_bias) = pl.pallas_call(
        functools.partial(finish_kernel, rest),
        out_shape=tuple(outs),
        in_specs=[anywhere] * 6 + [vmem] * 3,
        out_specs=tuple([anywhere] * 6 + [vmem] * 7),
        scratch_shapes=[pltpu.VMEM(o.shape, o.dtype) for o in outs[:6]] + [pltpu.SemaphoreType.DMA((6,))] * 2,
        compiler_params=pltpu.CompilerParams(vmem_limit_bytes=60 << 20),
    )(*results)
    return (
        out, gtok, losses.reshape(-1), qkv.T, attn.T, up.T, down.T, pool.T, g_class, g_biases, g_gains,
        g_bias_up.reshape(-1), g_pool_bias.reshape(-1),
    )


def per_device(
    tokens,
    cotangent,
    lengths,
    labels,
    w_qkv,
    w_out,
    w_up,
    w_down,
    w_pool,
    w_class,
    biases,
    norm_gains,
    bias_up,
):
    rest = lax.axis_size("batch") // 2
    if rest == 4:
        return finish(rest, layer(
            rest, tokens, cotangent, lengths, labels, w_qkv, w_out, w_up, w_down, w_pool, w_class, biases, norm_gains,
            bias_up,
        ))
    head_rank = lax.axis_index("head")
    rank = lax.axis_index("batch") * 4 + head_rank
    length = lax.dynamic_index_in_dim(lengths, head_rank, keepdims=False)
    label = lax.dynamic_index_in_dim(labels, head_rank, keepdims=False)
    slot_live = (jnp.arange(SLOT) < length).astype(F32)
    zeros_key = jnp.zeros((D,), F32)
    packed = jnp.dot(tokens, w_qkv, preferred_element_type=F32) + jnp.concatenate(
        [biases[0], zeros_key, biases[1]]
    )
    packed = packed.astype(LOW)
    context, probs = attention(packed, length)
    attn = jnp.dot(context, w_out, preferred_element_type=F32) + biases[2]
    first_sum = tokens.astype(F32) + attn
    norm_one, first_pull = jax.vjp(layer_norm, first_sum, norm_gains[0], biases[3])
    norm_low = norm_one.astype(LOW)
    hidden_up = jnp.dot(norm_low, w_up, preferred_element_type=F32) + bias_up
    activated_full, gelu_pull = jax.vjp(exact_gelu, hidden_up)
    activated = activated_full.astype(LOW)
    branch = jnp.dot(activated, w_down, preferred_element_type=F32) + biases[4]
    out_full, second_pull = jax.vjp(layer_norm, norm_one + branch, norm_gains[1], biases[5])
    leading = out_full[:1].astype(LOW)
    pooled = jnp.tanh(jnp.dot(leading, w_pool, preferred_element_type=F32) + biases[6])
    pooled_low = pooled.astype(LOW)
    logits = against(pooled_low, w_class)
    onehot = (jnp.arange(CLASSES)[None, :] == label).astype(F32)
    losses = jax.nn.logsumexp(logits, axis=-1) - jnp.sum(onehot * logits, axis=-1)
    d_logits = jax.nn.softmax(logits, axis=-1) - onehot
    g_class = exact(d_logits.T, pooled_low.astype(F32))
    d_pre = exact(d_logits, w_class.astype(F32)) * (1.0 - pooled * pooled)
    d_leading = exact(d_pre, w_pool.astype(F32).T)
    d_out = cotangent.astype(F32) * slot_live[:, None]
    d_out = d_out.at[0].add(d_leading[0])
    d_h2, g_gain_two, g_shift_two = second_pull(d_out)
    d_branch = d_h2.astype(LOW)
    g_bias_down = jnp.sum(d_branch.astype(F32), axis=0)
    g_down_t = inner(d_branch, activated)
    d_activated = against(d_branch, w_down)
    d_up = gelu_pull(d_activated)[0].astype(LOW)
    g_bias_up = jnp.sum(d_up.astype(F32), axis=0)
    g_up_t = inner(d_up, norm_low)
    d_norm_one = d_h2 + against(d_up, w_up)
    d_h1, g_gain_one, g_shift_one = first_pull(d_norm_one)
    d_attn = d_h1.astype(LOW)
    g_bias_out = jnp.sum(d_attn.astype(F32), axis=0)
    g_out_t = inner(d_attn, context)
    d_context = against(d_attn, w_out).astype(LOW)
    d_packed = attention_back(packed, probs, d_context)
    g_qkv_t = inner(d_packed, tokens)
    column_sums = jnp.sum(d_packed.astype(F32), axis=0)
    grad_tokens = (d_h1 + against(d_packed, w_qkv)).astype(LOW)
    small = jnp.concatenate(
        [
            g_class,
            jnp.stack([column_sums[:D], column_sums[2 * D :], g_bias_out, g_shift_one, g_bias_down, g_shift_two]),
            jnp.stack([g_gain_one, g_gain_two]),
            g_bias_up.reshape(FF // D, D),
            d_pre,
        ]
    )
    lead = jnp.concatenate([leading.astype(F32), d_pre])
    down = owner_blocks(g_down_t, rest, FF)
    up = owner_blocks(g_up_t, rest, D)
    last = jnp.concatenate([owner_blocks(g_qkv_t, rest, D), owner_blocks(g_out_t, rest, D)], axis=4)
    half = up.shape[4] // 2
    parts = [
        down[..., : FF // 2], down[..., FF // 2 :],
        up[..., :half, :], up[..., half:, :],
        last[..., :half, :], last[..., half:, :],
    ]
    *sums, small, everyone = reduce_gradients(rest, parts, small, lead)
    g_down = jnp.concatenate(sums[0:2], axis=1).T
    g_up = jnp.concatenate(sums[2:4], axis=0).T
    g_last = jnp.concatenate(sums[4:6], axis=0).T
    own_qkv = 3 * D // (8 * rest)
    own = D // (8 * rest)
    everyone = everyone.reshape(8 * rest, 2, D)
    window = lax.dynamic_slice_in_dim(small, rank * own, own, axis=1)
    pre_window = lax.dynamic_slice_in_dim(everyone[:, 1], rank * own, own, axis=1)
    g_pool = lax.dot_general(
        everyone[:, 0], pre_window, (((0,), (0,)), ((), ())),
        precision=lax.Precision.HIGHEST, preferred_element_type=F32,
    )
    own_up = FF // (8 * rest)
    g_bias_up = lax.dynamic_slice_in_dim(small[11:15].reshape(FF), rank * own_up, own_up)
    return (
        out_full.astype(LOW),
        grad_tokens,
        losses,
        g_last[:, :own_qkv],
        g_last[:, own_qkv:],
        g_up,
        g_down,
        g_pool,
        window[:3],
        window[3:9],
        window[9:11],
        g_bias_up,
        window[15],
    )


def solution(mesh):
    return jax.shard_map(
        per_device,
        mesh=mesh,
        in_specs=(
            P(("batch", "head"), None),
            P(("batch", "head"), None),
            P("batch"),
            P("batch"),
            P(),
            P(),
            P(),
            P(),
            P(),
            P(),
            P(),
            P(),
            P(),
        ),
        out_specs=(
            P(("batch", "head"), None),
            P(("batch", "head"), None),
            P(("batch", "head")),
            P(None, ("batch", "head")),
            P(None, ("batch", "head")),
            P(None, ("batch", "head")),
            P(None, ("batch", "head")),
            P(None, ("batch", "head")),
            P(None, ("batch", "head")),
            P(None, ("batch", "head")),
            P(None, ("batch", "head")),
            P(("batch", "head")),
            P(("batch", "head")),
        ),
        check_vma=False,
    )
```

```python
import functools

import jax
import jax.numpy as jnp
from jax import lax
from jax.experimental import pallas as pl
from jax.experimental.pallas import tpu as pltpu
from jax.sharding import PartitionSpec as P

D = 768
HEADS = 12
HEAD_DIM = 64
FF = 3072
CLASSES = 3
SLOT = 512
MESH = pl.DeviceIdType.MESH
LOW = jnp.bfloat16
F32 = jnp.float32


def layer_norm(hidden, gain, shift):
    center = hidden - jnp.mean(hidden, axis=-1, keepdims=True)
    spread = jnp.mean(center * center, axis=-1, keepdims=True)
    return center * lax.rsqrt(spread + 1e-12) * gain + shift


def exact_gelu(hidden):
    return jax.nn.gelu(hidden, approximate=False)


def inner(left, right):
    return lax.dot_general(
        left, right, (((0,), (0,)), ((), ())), preferred_element_type=jnp.float32
    )


def against(left, right):
    return lax.dot_general(
        left, right, (((1,), (1,)), ((), ())), preferred_element_type=jnp.float32
    )


def exact(left, right):
    return jnp.dot(left, right, precision=lax.Precision.HIGHEST, preferred_element_type=jnp.float32)


class Place:
    def __init__(self, rest):
        batch = lax.axis_index("batch")
        head = lax.axis_index("head")
        self.rest = rest
        self.z = batch // 2
        self.y = lax.rem(batch, 2)
        self.x = head // 2
        self.c = lax.rem(head, 2)

    def device(self, z, y, x, c):
        return (z * 2 + y, x * 2 + c)

    def core_peer(self):
        return self.device(self.z, self.y, self.x, 1 - self.c)

    def x_peer(self):
        return self.device(self.z, self.y, 1 - self.x, self.c)

    def y_peer(self):
        return self.device(self.z, 1 - self.y, self.x, self.c)

    def z_at(self, offset):
        return lax.rem(self.z + offset, self.rest)

    def z_peer(self, offset):
        return self.device(self.z_at(offset), self.y, self.x, self.c)

    def barrier(self):
        sem = pltpu.get_barrier_semaphore()
        for peer in (self.core_peer(), self.x_peer(), self.y_peer()):
            pl.semaphore_signal(sem, inc=1, device_id=peer, device_id_type=MESH)
        for offset in range(1, self.rest):
            pl.semaphore_signal(sem, inc=1, device_id=self.z_peer(offset), device_id_type=MESH)
        pl.semaphore_wait(sem, 3 + self.rest - 1)


def remote(src, dst, send, recv, peer):
    return pltpu.make_async_remote_copy(
        src_ref=src, dst_ref=dst, send_sem=send, recv_sem=recv, device_id=peer, device_id_type=MESH
    )


class Reduce:
    def __init__(self, place, part, bufs, sems, x_first):
        self.place, self.part, self.x_first = place, part, x_first
        self.r1, self.r2, self.r3, self.r4 = bufs
        send, recv, zsend, zrecv = sems
        p = place
        if x_first:
            far, near, second_far, second_near = (1 - p.x, p.x, 1 - p.y, p.y)
            peers = (p.x_peer(), p.y_peer())
            src2 = self.r1.at[far]
        else:
            far, near, second_far, second_near = (1 - p.y, p.y, 1 - p.x, p.x)
            peers = (p.y_peer(), p.x_peer())
            src2 = self.r1.at[:, far]
        self.near, self.second_near = near, second_near
        self.copies = [
            remote(part.at[1 - p.c], self.r1, send.at[0], recv.at[0], p.core_peer()),
            remote(src2, self.r2, send.at[1], recv.at[1], peers[0]),
            remote(self.r2.at[second_far], self.r3, send.at[2], recv.at[2], peers[1]),
        ]
        self.last = [
            remote(self.r3.at[p.z_at(k)], self.r4.at[k - 1], zsend.at[k - 1], zrecv.at[k - 1], p.z_peer(k))
            for k in range(1, p.rest)
        ]

    def start(self):
        self.copies[0].start()

    def step1(self):
        p = self.place
        self.copies[0].wait()
        for i in range(2):
            for j in range(2):
                def add(k, carry, i=i, j=j):
                    self.r1[i, j, k] = self.r1[i, j, k] + self.part[p.c, i, j, k]
                    return carry
                lax.fori_loop(0, p.rest, add, 0)
        self.copies[1].start()

    def step2(self):
        p = self.place
        self.copies[1].wait()
        for i in range(2):
            def add(k, carry, i=i):
                own = self.r1[self.near, i, k] if self.x_first else self.r1[i, self.near, k]
                self.r2[i, k] = self.r2[i, k] + own
                return carry
            lax.fori_loop(0, p.rest, add, 0)
        self.copies[2].start()

    def step3(self):
        p = self.place
        self.copies[2].wait()

        def add(k, carry):
            self.r3[k] = self.r3[k] + self.r2[self.second_near, k]
            return carry
        lax.fori_loop(0, p.rest, add, 0)
        for copy in self.last:
            copy.start()

    def total(self):
        p = self.place
        for copy in self.last:
            copy.wait()
        result = self.r3[p.z].astype(F32)
        for k in range(1, p.rest):
            result = result + self.r4[k - 1].astype(F32)
        return result


def chunk_scratch(rest, rows, width):
    return [
        pltpu.VMEM((2, 2, rest, rows, width), LOW),
        pltpu.VMEM((2, rest, rows, width), LOW),
        pltpu.VMEM((rest, rows, width), LOW),
        pltpu.VMEM((rest - 1, rows, width), LOW),
        pltpu.SemaphoreType.DMA((3,)),
        pltpu.SemaphoreType.DMA((3,)),
        pltpu.SemaphoreType.DMA((rest - 1,)),
        pltpu.SemaphoreType.DMA((rest - 1,)),
    ]


class Small:
    def __init__(self, place, small, lead, everyone, bufs):
        got, gotz, send, recv, zsend, zrecv, gsend, grecv, gzsend, gzrecv = bufs
        p = place
        self.place, self.small, self.got, self.gotz = p, small, got, gotz
        self.lead, self.everyone = lead, everyone
        peers = (p.core_peer(), p.x_peer(), p.y_peer())
        blocks = (
            everyone.at[p.z, p.y, p.x, p.c], everyone.at[p.z, p.y, p.x], everyone.at[p.z, p.y],
        )
        self.sums = [remote(small, got.at[i], send.at[i], recv.at[i], peers[i]) for i in range(3)]
        self.sum_last = [
            remote(small, gotz.at[k - 1], zsend.at[k - 1], zrecv.at[k - 1], p.z_peer(k)) for k in range(1, p.rest)
        ]
        self.gathers = [remote(blocks[i], blocks[i], gsend.at[i], grecv.at[i], peers[i]) for i in range(3)]
        self.gather_last = [
            remote(everyone.at[p.z], everyone.at[p.z], gzsend.at[k - 1], gzrecv.at[k - 1], p.z_peer(k))
            for k in range(1, p.rest)
        ]

    def gather_start(self):
        p = self.place
        self.everyone[p.z, p.y, p.x, p.c] = self.lead[...]
        self.gathers[0].start()

    def gather_step(self, i):
        self.gathers[i].wait()
        if i < 2:
            self.gathers[i + 1].start()
        else:
            for copy in self.gather_last:
                copy.start()

    def gather_end(self):
        for copy in self.gather_last:
            copy.wait()

    def sum_start(self):
        self.sums[0].start()

    def sum_step(self, i):
        self.sums[i].wait()
        self.small[...] = self.small[...] + self.got[i]
        if i < 2:
            self.sums[i + 1].start()
        else:
            for copy in self.sum_last:
                copy.start()

    def sum_end(self):
        for copy in self.sum_last:
            copy.wait()
        total = self.small[...]
        for k in range(1, self.place.rest):
            total = total + self.gotz[k - 1]
        return total


def small_scratch(rest):
    return [
        pltpu.VMEM((3, 16, D), F32),
        pltpu.VMEM((rest - 1, 16, D), F32),
    ] + [pltpu.SemaphoreType.DMA((3,)), pltpu.SemaphoreType.DMA((3,)),
         pltpu.SemaphoreType.DMA((rest - 1,)), pltpu.SemaphoreType.DMA((rest - 1,))] * 2


def reduce_kernel(rest, n_chunks, *refs):
    parts = refs[:n_chunks]
    small_in, lead = refs[n_chunks : n_chunks + 2]
    outs = refs[n_chunks + 2 : 2 * n_chunks + 2]
    small_out, everyone = refs[2 * n_chunks + 2 : 2 * n_chunks + 4]
    scratch = refs[2 * n_chunks + 4 :]
    place = Place(rest)
    chunks = []
    for i in range(n_chunks):
        own = scratch[8 * i : 8 * i + 8]
        chunks.append(Reduce(place, parts[i], own[:4], own[4:], i % 2 == 0))
    rest_scratch = scratch[8 * n_chunks :]
    small = Small(place, rest_scratch[0], lead, everyone, rest_scratch[1:])
    rest_scratch[0][...] = small_in[...]
    place.barrier()
    small.gather_start()
    small.sum_start()
    steps = [[c.step1, c.step2, c.step3] for c in chunks]
    for chunk in chunks:
        chunk.start()
    for i in range(3):
        small.gather_step(i)
        small.sum_step(i)
    for phase in range(n_chunks + 4):
        for i in range(n_chunks):
            k = phase - i
            if i % 2 == 1:
                k = phase - i + 1
            if 0 <= k < 3:
                steps[i][k]()
            if k == 3:
                outs[i][...] = chunks[i].total()
    small.gather_end()
    small_out[...] = small.sum_end()


def reduce_gradients(rest, parts, small, lead):
    vmem = pl.BlockSpec(memory_space=pltpu.VMEM)
    scratch = []
    for part in parts:
        scratch += chunk_scratch(rest, *part.shape[4:])
    scratch += [pltpu.VMEM((16, D), F32)] + small_scratch(rest)
    outs = [jax.ShapeDtypeStruct(part.shape[4:], F32) for part in parts]
    outs += [
        jax.ShapeDtypeStruct((16, D), F32),
        jax.ShapeDtypeStruct((rest, 2, 2, 2, 2, D), F32),
    ]
    return pl.pallas_call(
        functools.partial(reduce_kernel, rest, len(parts)),
        out_shape=tuple(outs),
        in_specs=[vmem] * (len(parts) + 2),
        out_specs=tuple([vmem] * len(outs)),
        scratch_shapes=scratch,
        compiler_params=pltpu.CompilerParams(
            collective_id=0, has_side_effects=True, vmem_limit_bytes=60 << 20
        ),
    )(*parts, small, lead)


def owner_blocks(grad_t, rest, width):
    rows = grad_t.shape[0] // (8 * rest)
    view = grad_t.astype(LOW).reshape(rest, 2, 2, 2, rows, width)
    return view.transpose(3, 2, 1, 0, 4, 5)


def attention(packed, length):
    heads = packed.reshape(SLOT, 3, HEADS, HEAD_DIM)
    queries, keys_all, values = heads[:, 0], heads[:, 1], heads[:, 2]
    scores = jnp.einsum("qhd,khd->hqk", queries, keys_all, preferred_element_type=F32) * HEAD_DIM ** (-0.5)
    scores = jnp.where((jnp.arange(SLOT) < length)[None, None, :], scores, -1e30)
    row_max = jnp.max(scores, axis=-1, keepdims=True)
    weights = jnp.exp(scores - row_max)
    weights = weights / jnp.sum(weights, axis=-1, keepdims=True)
    low = weights.astype(LOW)
    context = jnp.einsum("hqk,khd->qhd", low, values, preferred_element_type=F32)
    return context.astype(LOW).reshape(SLOT, D), low


def attention_back(packed, low, d_context):
    heads = packed.reshape(SLOT, 3, HEADS, HEAD_DIM)
    queries, keys_all, values = heads[:, 0], heads[:, 1], heads[:, 2]
    d_heads = d_context.reshape(SLOT, HEADS, HEAD_DIM)
    weights = low.astype(F32)
    d_weights = jnp.einsum("qhd,khd->hqk", d_heads, values, preferred_element_type=F32)
    d_values = jnp.einsum("hqk,qhd->khd", low, d_heads, preferred_element_type=F32)
    row_dot = jnp.sum(weights * d_weights, axis=-1, keepdims=True)
    d_scores = (weights * (d_weights - row_dot)).astype(LOW)
    scale = HEAD_DIM ** (-0.5)
    d_queries = jnp.einsum("hqk,khd->qhd", d_scores, keys_all, preferred_element_type=F32) * scale
    d_keys = jnp.einsum("hqk,qhd->khd", d_scores, queries, preferred_element_type=F32) * scale
    return jnp.stack([d_queries, d_keys, d_values], axis=1).astype(LOW).reshape(SLOT, 3 * D)


def nn(left, right):
    return jnp.dot(left, right, preferred_element_type=F32)


def aligned(index, step):
    return pl.ds(pl.multiple_of(index * step, step), step)


def column_sum(ones, array):
    return nn(ones, array)[0:1]


def normalized(hidden):
    center = hidden - jnp.mean(hidden, axis=-1, keepdims=True)
    spread = jnp.mean(center * center, axis=-1, keepdims=True)
    scale = lax.rsqrt(spread + 1e-12)
    return center * scale, scale


def normalized_back(normed, scale, d_normed):
    first = jnp.mean(d_normed, axis=-1, keepdims=True)
    second = jnp.mean(d_normed * normed, axis=-1, keepdims=True)
    return scale * (d_normed - first - normed * second)


class Unit:
    def __init__(self, place, order, part, bufs, send, recv, put):
        p = self.place = place
        self.put = put
        self.at = 0
        self.legs = []
        bufs = list(bufs)
        count = part.shape[0] // 2
        held = bufs.pop(0)
        copy = remote(part.at[pl.ds((1 - p.c) * count, count)], held, send.at[0], recv.at[0], p.core_peer())
        self.legs.append((copy.start, self.pair_end(copy, held, part, p.c * count, count, False)))
        base = 0
        slot = 1
        for i, axis in enumerate(order):
            last = i == len(order) - 1
            if axis == "z":
                count = count // 4
                self.line(held, base, count, bufs.pop(0), bufs.pop(0), send, recv, slot, last)
                base = base + p.z * count
                slot += 3
            else:
                count = count // 2
                mine, peer = (p.x, p.x_peer()) if axis == "x" else (p.y, p.y_peer())
                got = bufs.pop(0)
                copy = remote(held.at[pl.ds(base + (1 - mine) * count, count)], got, send.at[slot], recv.at[slot], peer)
                self.legs.append((copy.start, self.pair_end(copy, got, held, base + mine * count, count, last)))
                held, base = got, 0
                slot += 1

    def pair_end(self, copy, got, own, start, count, last):
        def end():
            copy.wait()
            if last:
                self.put(got[0].astype(F32) + own[start].astype(F32))
            elif count >= 8:
                def add(i, carry):
                    got[pl.ds(i * 4, 4)] = got[pl.ds(i * 4, 4)] + own[pl.ds(start + i * 4, 4)]
                    return carry
                lax.fori_loop(0, count // 4, add, 0)
            else:
                got[...] = got[...] + own[pl.ds(start, count)]
        return end

    def line(self, held, base, n, wide, single, send, recv, slot, last):
        p = self.place
        z = p.z
        outer = jnp.logical_or(z == 0, z == 3)
        inner = jnp.logical_not(outer)
        low = z < 2
        near = jnp.where(low, 1 - z, 5 - z)
        far = jnp.where(low, z + 2, z - 2)
        middle = 3 - z

        def at(block, count=n):
            return held.at[pl.ds(base + block * n, count)]

        def device(block):
            return p.device(block, p.y, p.x, p.c)

        outward = remote(at(jnp.where(z == 0, 1, 0), 3 * n), wide, send.at[slot], recv.at[slot], device(near))
        back = remote(at(near), wide.at[0:n], send.at[slot], recv.at[slot], device(near))
        across = remote(at(middle), single, send.at[slot + 1], recv.at[slot + 1], device(middle))
        beyond = remote(at(far), wide.at[n : 2 * n], send.at[slot + 2], recv.at[slot + 2], device(far))

        def begin_first():
            @pl.when(outer)
            def _():
                outward.start()

            @pl.when(inner)
            def _():
                back.start()

        def end_first():
            @pl.when(outer)
            def _():
                outward.wait_send()
                back.wait_recv()

            @pl.when(inner)
            def _():
                back.wait_send()
                outward.wait_recv()
                start = base + jnp.where(z == 1, n, 0)
                held[pl.ds(start, 3 * n)] = held[pl.ds(start, 3 * n)] + wide[...]

        def begin_second():
            @pl.when(inner)
            def _():
                across.start()
                beyond.start()

        def end_second():
            @pl.when(outer)
            def _():
                beyond.wait_recv()
                total = held[pl.ds(base + z * n, n)].astype(F32) + wide[0:n].astype(F32) + wide[n : 2 * n].astype(F32)
                if last:
                    self.put(total[0])
                else:
                    held[pl.ds(base + z * n, n)] = total.astype(LOW)

            @pl.when(inner)
            def _():
                across.wait()
                beyond.wait_send()
                total = held[pl.ds(base + z * n, n)].astype(F32) + single[...].astype(F32)
                if last:
                    self.put(total[0])
                else:
                    held[pl.ds(base + z * n, n)] = total.astype(LOW)

        self.legs.append((begin_first, end_first))
        self.legs.append((begin_second, end_second))

    def step(self):
        if self.at > 0:
            self.legs[self.at - 1][1]()
        if self.at < len(self.legs):
            self.legs[self.at][0]()
        self.at += 1


class Gather:
    def __init__(self, place, lead, everyone, send, recv):
        p = place
        peers = (p.core_peer(), p.x_peer(), p.y_peer())
        own = everyone.at[p.z, p.y, p.x, p.c]
        blocks = (own, everyone.at[p.z, p.y, p.x], everyone.at[p.z, p.y])
        groups = [[remote(blocks[i], blocks[i], send.at[i], recv.at[i], peers[i])] for i in range(3)]
        groups.append([
            remote(everyone.at[p.z], everyone.at[p.z], send.at[k + 2], recv.at[k + 2], p.z_peer(k)) for k in range(1, p.rest)
        ])
        self.groups, self.at, self.own, self.lead = groups, 0, own, lead

    def step(self):
        if self.at == 0:
            self.own[...] = self.lead[...]
        else:
            for copy in self.groups[self.at - 1]:
                copy.wait()
        if self.at < 4:
            for copy in self.groups[self.at]:
                copy.start()
        self.at += 1


class Total:
    def __init__(self, place, small, low, got, send, recv, put):
        p = place
        peers = (p.core_peer(), p.x_peer(), p.y_peer())
        groups = [[remote(low, got.at[i], send.at[i], recv.at[i], peers[i])] for i in range(3)]
        groups.append([
            remote(low, got.at[k + 2], send.at[k + 2], recv.at[k + 2], p.z_peer(k)) for k in range(1, p.rest)
        ])
        self.groups, self.at, self.small, self.low, self.got, self.put = groups, 0, small, low, got, put

    def step(self):
        total = self.small[...]
        if self.at > 0:
            first = self.at - 1
            for i, copy in enumerate(self.groups[first]):
                copy.wait()
                total = total + self.got[first + i].astype(F32)
        if self.at < 4:
            self.small[...] = total
            self.low[...] = total.astype(LOW)
            for copy in self.groups[self.at]:
                copy.start()
        else:
            self.put(total)
        self.at += 1


def block_index(order, rest, z, y, x, c):
    sizes = {"x": 2, "y": 2, "z": rest}
    at = {"x": x, "y": y, "z": z}
    index = c
    for axis in order:
        index = index * sizes[axis] + at[axis]
    return index


def owners(rest):
    return [(z, y, x, c) for z in range(rest) for y in range(2) for x in range(2) for c in range(2)]


def unit_scratch(order, rows, width):
    blocks = 16
    bufs = [pltpu.VMEM((blocks, rows, width), LOW)]
    for axis in order:
        if axis == "z":
            blocks = blocks // 4
            bufs += [pltpu.VMEM((3 * blocks, rows, width), LOW), pltpu.VMEM((blocks, rows, width), LOW)]
        else:
            blocks = blocks // 2
            bufs.append(pltpu.VMEM((blocks, rows, width), LOW))
    return bufs + [pltpu.SemaphoreType.DMA((6,)), pltpu.SemaphoreType.DMA((6,))]


UNITS = (("down", 4, 2), ("up", 4, 1), ("out", 1, 1), ("qkv", 3, 2))
ORDERS = (
    "zyx", "yzx", "xyz", "yxz", "yzx", "xzy", "zyx", "yzx", "xyz", "zyx", "yxz", "yxz", "xyz", "yxz", "xyz", "yxz", "xzy", "yxz", "xzy",
)
PLAN = (
    (),
    (),
    (),
    (),
    (),
    (19,),
    (0,),
    (1,),
    (3, 7, 6, 19, 5,),
    (1, 4, 2,),
    (5,),
    (3, 7, 6, 2, 19, 0, 8,),
    (1, 10, 9,),
    (2,),
    (12, 11, 3,),
    (8, 10,),
    (),
    (5, 4,),
    (11, 12, 9, 10, 6, 5,),
    (20, 8, 15, 16, 12, 18, 7, 3, 13, 11, 2, 5, 20, 8, 17, 14, 16,),
    (),
    (10, 0, 18, 11, 15, 13, 3, 6, 20, 4, 14, 16, 17, 15, 9, 7, 18, 13, 14, 12, 0, 20, 4, 16, 17, 1, 7, 11, 6, 15, 19, 9, 2, 13, 18, 14, 10, 16, 12, 4, 1, 17, 9, 0, 8, 13, 15, 18, 14, 17,),
)
N_IN = 13
N_OUT = 9


def layer_kernel(rest, *refs):
    (lengths, labels, biases, gains, bias_up, w_class, tokens_h, cot_h, wqkv_h, wout_h, wup_h, wdown_h, wpool_h) = refs[:N_IN]
    out_h, gtok_h, down_out, up_out, qkv_out, attn_out, small_out, everyone, loss_out = refs[N_IN : N_IN + N_OUT]
    scratch = list(refs[N_IN + N_OUT :])
    (
        tokens, w_qkv, w_out, w_up, w_down, packed, weights, inverse, context, normed_one, norm_low,
        activated, slope, d_hidden, d_low, d_packed, part0, part1, part2, part3, scale_one, small, lead, in_sem, out_sem,
    ) = scratch[:25]
    parts = [part0, part1, part2, part3]
    cot = d_low
    d_context = norm_low
    wide = SLOT
    pool_wide = d_packed.at[0:D]
    pool_rest = d_packed.at[D : 2 * D, 0 : D - wide]
    out_wide = d_packed.at[2 * D : 2 * D + SLOT]
    out_rest = d_packed.at[D : D + SLOT, wide // 2 : wide // 2 + D - wide]
    place = Place(rest)
    small_bufs = scratch[25:31]
    unit_bufs = scratch[31:]
    head_rank = lax.axis_index("head")
    length = lengths[head_rank]
    label = labels[head_rank]
    loads = [
        pltpu.make_async_copy(src, dst, in_sem.at[i])
        for i, (src, dst) in enumerate(
            [(tokens_h, tokens), (wqkv_h.at[:, 0:D], w_qkv.at[:, 0:D]), (wqkv_h.at[:, D : 2 * D], w_qkv.at[:, D : 2 * D]),
             (wqkv_h.at[:, 2 * D :], w_qkv.at[:, 2 * D :]), (wout_h, w_out), (wup_h, w_up),
             (wdown_h, w_down), (cot_h, cot), (wpool_h.at[:, 0:wide], pool_wide), (wpool_h.at[:, wide:D], pool_rest)]
        )
    ]
    for load in loads[:4]:
        load.start()
    sem = pltpu.get_barrier_semaphore()
    for peer in (place.core_peer(), place.x_peer(), place.y_peer()):
        pl.semaphore_signal(sem, inc=1, device_id=peer, device_id_type=MESH)
    for offset in range(1, rest):
        pl.semaphore_signal(sem, inc=1, device_id=place.z_peer(offset), device_id_type=MESH)

    height = D // 32
    order_of = owners(rest)

    targets = {"down": down_out, "up": up_out, "out": attn_out, "qkv": qkv_out}
    base_part = {"down": 0, "up": 0, "out": 0, "qkv": 1}

    def put_into(kind, i, columns):
        def put(total):
            if kind == "down":
                down_out[:, i * D + columns.start : i * D + columns.stop] = total
            else:
                targets[kind][i * height : (i + 1) * height, columns] = total
        return put

    units = []
    number = {}
    at = 0
    for kind, count, cut in UNITS:
        for i in range(count):
            for j in range(cut):
                columns = slice(j * D // cut, (j + 1) * D // cut)
                order = ORDERS[len(units)]
                size = len(unit_scratch(order, height, D // cut))
                own = unit_bufs[at : at + size]
                at += size
                part = parts[base_part[kind] + i]
                if cut > 1:
                    part = part.at[:, :, columns]
                number[kind, i, j] = len(units)
                units.append(Unit(place, order, part, own[:-2], own[-2], own[-1], put_into(kind, i, columns)))
    gather, totals = len(units), len(units) + 1

    def fill(kind, i, owner, columns, value):
        cut = {name: c for name, _, c in UNITS}[kind]
        width = D // cut
        part = parts[base_part[kind] + i]
        for j in range(cut):
            first, last = max(columns.start, j * width), min(columns.stop, (j + 1) * width)
            if first < last:
                index = block_index(ORDERS[number[kind, i, j]], rest, *owner)
                part[index, :, first:last] = value[:, first - columns.start : last - columns.start].astype(LOW)

    def go(kind, i, j):
        units[number[kind, i, j]].step()

    low_small, got_small, *small_sems = small_bufs
    units.append(Gather(place, lead, everyone, *small_sems[:2]))
    units.append(Total(place, small, low_small, got_small, *small_sems[2:], lambda total: small_out.__setitem__(Ellipsis, total)))
    plan = list(PLAN)

    def steps():
        for i in plan.pop(0):
            units[i].step()

    loads[0].wait()
    ones = jnp.ones((8, SLOT), LOW)
    for part in range(3):
        columns = slice(part * D, part * D + D)
        loads[part + 1].wait()
        if part == 0:
            for load in loads[4:]:
                load.start()
        result = nn(tokens[...], w_qkv[:, columns])
        if part == 0:
            result = (result + biases[0:1]).astype(LOW) * jnp.asarray(HEAD_DIM ** (-0.5), LOW)
        elif part == 2:
            result = (result + biases[1:2]).astype(LOW)
        else:
            result = result.astype(LOW)
        packed[:, columns] = result

    key_live = lax.broadcasted_iota(jnp.int32, (SLOT, 1), 0) < length
    lane = lax.broadcasted_iota(jnp.int32, (1, 2 * HEAD_DIM), 1)
    lane_of = [lane < HEAD_DIM, lane >= HEAD_DIM]

    def attend(pair):
        at = pair * 2 * HEAD_DIM
        queries = packed[:, at : at + 2 * HEAD_DIM]
        keys_all = packed[:, at + D : at + D + 2 * HEAD_DIM]
        values_t = packed[:, at + 2 * D : at + 2 * D + 2 * HEAD_DIM].T
        got = []
        for k in range(2):
            own_keys = jnp.where(lane_of[k], keys_all, jnp.zeros_like(keys_all))
            scores = jnp.where(key_live, against(own_keys, queries), -1e30)
            powers = jnp.exp(scores - jnp.max(scores, axis=0, keepdims=True))
            inv = 1.0 / jnp.sum(powers, axis=0, keepdims=True)
            powers = powers.astype(LOW)
            weights[2 * pair + k] = powers
            inverse[pair, k : k + 1] = inv
            got.append(nn(values_t[k * HEAD_DIM : (k + 1) * HEAD_DIM], powers) * inv)
        context[:, at : at + 2 * HEAD_DIM] = jnp.concatenate(got, axis=0).T.astype(LOW)

    for pair in range(HEADS // 2):
        attend(pair)

    blocks = [slice(0, SLOT // 2), slice(SLOT // 2, SLOT)]
    loads[4].wait()
    for rows in blocks:
        hidden = nn(context[rows], w_out[...]) + biases[2:3] + tokens[rows].astype(F32)
        normed, scale = normalized(hidden)
        normed_one[rows] = normed
        scale_one[rows] = scale
        norm_low[rows] = (normed * gains[0:1] + biases[3:4]).astype(LOW)

    loads[5].wait()

    def feed(tile):
        columns = slice(tile * D, (tile + 1) * D)
        hidden = nn(norm_low[...], w_up[:, columns]) + bias_up[0:1, columns]
        share = 0.5 + 0.5 * lax.erf(hidden * 0.7071067811865476)
        activated[:, columns] = (hidden * share).astype(LOW)
        slope[:, columns] = (share + hidden * (jnp.exp(-0.5 * hidden * hidden) * 0.3989422804014327)).astype(LOW)

    for tile in range(FF // D):
        feed(tile)

    for i in (6, 7, 8, 9):
        loads[i].wait()
    row = lax.broadcasted_iota(jnp.int32, (SLOT // 2, 1), 0)
    kept = []
    for k, rows in enumerate(blocks):
        hidden = nn(activated[rows], w_down[...]) + biases[4:5] + (normed_one[rows] * gains[0:1] + biases[3:4])
        normed, scale = normalized(hidden)
        result = normed * gains[1:2] + biases[5:6]
        low = result.astype(LOW)
        out_wide[rows] = low[:, 0:wide]
        out_rest[rows] = low[:, wide:D]
        d_hidden[rows] = normed
        kept.append(scale)
        if k == 0:
            leading = low[0:8]
    out_copies = [
        pltpu.make_async_copy(out_wide, out_h.at[:, 0:wide], out_sem.at[0]),
        pltpu.make_async_copy(out_rest, out_h.at[:, wide:D], out_sem.at[2]),
    ]
    for copy in out_copies:
        copy.start()

    pooled = jnp.concatenate([nn(leading, pool_wide[...]), nn(leading, pool_rest[...])], axis=1)
    pooled = jnp.tanh(pooled + biases[6:7])[0:1]
    pooled_low = pooled.astype(LOW).astype(F32)
    classes = w_class[...].astype(F32)
    logits = jnp.sum(pooled_low * classes, axis=-1, keepdims=True)
    top = jnp.max(logits, axis=0, keepdims=True)
    powers = jnp.exp(logits - top)
    total = jnp.sum(powers, axis=0, keepdims=True)
    onehot = (lax.broadcasted_iota(jnp.int32, (CLASSES, 1), 0) == label).astype(F32)
    loss_out[...] = jnp.broadcast_to(
        jnp.log(total) + top - jnp.sum(onehot * logits, axis=0, keepdims=True), loss_out.shape
    )
    d_logits = powers / total - onehot
    d_pre = jnp.sum(d_logits * classes, axis=0, keepdims=True) * (1.0 - pooled * pooled)
    high = d_pre.astype(LOW).astype(F32)
    middle = (d_pre - high).astype(LOW).astype(F32)
    low = d_pre - high - middle
    eight = lax.broadcasted_iota(jnp.int32, (8, 1), 0)
    split = jnp.where(eight == 0, high, jnp.where(eight == 1, middle, jnp.where(eight == 2, low, 0.0)))
    split = split.astype(LOW)
    d_leading = against(split[:, 0:wide], pool_wide[...]) + against(split[:, wide:D], pool_rest[...])
    d_leading = jnp.sum(d_leading, axis=0, keepdims=True)
    small[0:3] = d_logits * pooled_low
    small[15:16] = d_pre
    lead[0:1] = leading[0:1]
    lead[1:2] = d_pre.astype(LOW)

    shift_two = jnp.zeros((1, D), F32)
    gain_two = jnp.zeros((1, D), F32)
    for k in (1, 0):
        rows = blocks[k]
        normed, scale = d_hidden[rows], kept[k]
        d_out = jnp.where(row + k * (SLOT // 2) < length, cot[rows].astype(F32), 0.0)
        if k == 0:
            d_out = d_out + jnp.where(row == 0, d_leading, 0.0)
        shift_two = shift_two + jnp.sum(d_out, axis=0, keepdims=True)
        gain_two = gain_two + jnp.sum(d_out * normed, axis=0, keepdims=True)
        d_two = normalized_back(normed, scale, d_out * gains[1:2])
        d_hidden[rows] = d_two
        d_low[rows] = d_two.astype(LOW)
    small[8:9] = shift_two
    small[10:11] = gain_two
    small[7:8] = column_sum(ones, d_low[...])

    rows = height
    for copy in out_copies:
        copy.wait()
    pl.semaphore_wait(sem, 3 + rest - 1)
    units[gather].step()
    d_branch_t = d_low[...].T
    halves = (slice(0, D // 2), slice(D // 2, D))
    everything = slice(0, D)
    cuts = {name: cut for name, _, cut in UNITS}
    for i in range(4):
        for j, columns in enumerate(halves):
            result = nn(d_branch_t, activated[:, i * D + columns.start : i * D + columns.stop])
            for d, owner in enumerate(order_of):
                fill("down", i, owner, columns, result[d * rows : (d + 1) * rows])
            if cuts["down"] == 2:
                go("down", i, j)
            elif j == 1:
                go("down", i, 0)
            steps()

    def feed_back(tile, carry):
        columns = aligned(tile, D)
        d_up = (against(d_low[...], w_down[columns]) * slope[:, columns].astype(F32)).astype(LOW)
        slope[:, columns] = d_up
        small[pl.ds(11 + tile, 1)] = column_sum(ones, d_up)
        return carry

    for part in range(2):
        lax.fori_loop(2 * part, 2 * part + 2, feed_back, 0)
        steps()
    d_up = slope

    def up_gradient(tile, carry):
        for columns in halves:
            result = inner(d_up[:, aligned(tile, D)], norm_low[:, columns])
            for d in range(8):
                for i in range(4):
                    first = (d * 4 + i) * rows
                    fill("up", i, (tile, *order_of[d][1:]), columns, result[first : first + rows])
        return carry

    lax.fori_loop(0, FF // D, up_gradient, 0)
    for i in range(4):
        for j in range(cuts["up"]):
            go("up", i, j)
    steps()

    shift_one = jnp.zeros((1, D), F32)
    gain_one = jnp.zeros((1, D), F32)
    for block in blocks:
        d_norm = d_hidden[block] + against(d_up[block], w_up[...])
        normed = normed_one[block]
        shift_one = shift_one + jnp.sum(d_norm, axis=0, keepdims=True)
        gain_one = gain_one + jnp.sum(d_norm * normed, axis=0, keepdims=True)
        d_one = normalized_back(normed, scale_one[block], d_norm * gains[0:1])
        d_hidden[block] = d_one
        d_low[block] = d_one.astype(LOW)
        steps()
    small[6:7] = shift_one
    small[9:10] = gain_one
    small[5:6] = column_sum(ones, d_low[...])

    result = inner(d_low[...], context[...])
    for d, owner in enumerate(order_of):
        fill("out", 0, owner, everything, result[d * rows : (d + 1) * rows])
    for j in range(cuts["out"]):
        go("out", 0, j)
    d_context[...] = against(d_low[...], w_out[...]).astype(LOW)
    steps()

    def attend_back(pair, carry):
        at = pl.multiple_of(pair * 2 * HEAD_DIM, 2 * HEAD_DIM)
        queries_t = packed[:, pl.ds(at, 2 * HEAD_DIM)].T
        keys_t = packed[:, pl.ds(at + D, 2 * HEAD_DIM)].T
        values = packed[:, pl.ds(at + 2 * D, 2 * HEAD_DIM)]
        context_t = context[:, pl.ds(at, 2 * HEAD_DIM)].T
        d_context_t = d_context[:, pl.ds(at, 2 * HEAD_DIM)].T
        scaled = []
        dots = []
        for k in range(2):
            own_rows = slice(k * HEAD_DIM, (k + 1) * HEAD_DIM)
            own = d_context_t[own_rows].astype(F32) * inverse[pair, k : k + 1]
            dots.append(jnp.sum(own * context_t[own_rows].astype(F32), axis=0, keepdims=True))
            scaled.append(own.astype(LOW))
        both = jnp.concatenate(scaled, axis=0).T
        for k in range(2):
            own_rows = slice(k * HEAD_DIM, (k + 1) * HEAD_DIM)
            own_values = jnp.where(lane_of[k], values, jnp.zeros_like(values))
            powers = weights[2 * pair + k]
            d_scores = (powers.astype(F32) * (against(own_values, both) - dots[k])).astype(LOW)
            put = pl.multiple_of(at + k * HEAD_DIM, HEAD_DIM)
            d_packed[pl.ds(put, HEAD_DIM)] = (nn(keys_t[own_rows], d_scores) * HEAD_DIM ** (-0.5)).astype(LOW)
            d_packed[pl.ds(put + D, HEAD_DIM)] = against(queries_t[own_rows], d_scores).astype(LOW)
            d_packed[pl.ds(put + 2 * D, HEAD_DIM)] = against(scaled[k], powers).astype(LOW)
        return carry

    for part in range(3):
        lax.fori_loop(2 * part, 2 * part + 2, attend_back, 0)
        steps()

    small[3:4] = against(ones, d_packed[0:D])[0:1]
    small[4:5] = against(ones, d_packed[2 * D : 3 * D])[0:1]
    units[totals].step()
    steps()
    def qkv_gradient(tile, carry):
        result = nn(d_packed[aligned(tile, 24 * rows)], tokens[...])
        for d in range(8):
            for i in range(3):
                first = (d * 3 + i) * rows
                fill("qkv", i, (tile, *order_of[d][1:]), everything, result[first : first + rows])
        return carry

    lax.fori_loop(0, rest, qkv_gradient, 0)
    for i in range(3):
        for j in range(cuts["qkv"]):
            go("qkv", i, j)
    steps()

    for block in blocks:
        d_tokens = nn(w_qkv[...], d_packed[:, block]).T + d_hidden[block]
        d_low[block] = d_tokens.astype(LOW)
        steps()
    token_copy = pltpu.make_async_copy(d_low, gtok_h, out_sem.at[1])
    token_copy.start()
    steps()
    token_copy.wait()


def layer(rest, tokens, cotangent, lengths, labels, w_qkv, w_out, w_up, w_down, w_pool, w_class, biases, norm_gains, bias_up):
    rows = D // 32
    vmem = pl.BlockSpec(memory_space=pltpu.VMEM)
    smem = pl.BlockSpec(memory_space=pltpu.SMEM)
    anywhere = pl.BlockSpec(memory_space=pl.ANY)
    dma = pltpu.SemaphoreType.DMA
    scratch = [
        pltpu.VMEM((SLOT, D), LOW),
        pltpu.VMEM((D, 3 * D), LOW),
        pltpu.VMEM((D, D), LOW),
        pltpu.VMEM((D, FF), LOW),
        pltpu.VMEM((FF, D), LOW),
        pltpu.VMEM((SLOT, 3 * D), LOW),
        pltpu.VMEM((HEADS, SLOT, SLOT), LOW),
        pltpu.VMEM((HEADS // 2, 2, SLOT), F32),
        pltpu.VMEM((SLOT, D), LOW),
        pltpu.VMEM((SLOT, D), F32),
        pltpu.VMEM((SLOT, D), LOW),
        pltpu.VMEM((SLOT, FF), LOW),
        pltpu.VMEM((SLOT, FF), LOW),
        pltpu.VMEM((SLOT, D), F32),
        pltpu.VMEM((SLOT, D), LOW),
        pltpu.VMEM((3 * D, SLOT), LOW),
    ] + [pltpu.VMEM((32, rows, D), LOW)] * 4 + [
        pltpu.VMEM((SLOT, 1), F32),
        pltpu.VMEM((16, D), F32),
        pltpu.VMEM((2, D), LOW),
        dma((10,)),
        dma((3,)),
        pltpu.VMEM((16, D), LOW),
        pltpu.VMEM((6, 16, D), LOW),
        dma((6,)),
        dma((6,)),
        dma((6,)),
        dma((6,)),
    ]
    orders = list(ORDERS)
    for _, count, cut in UNITS:
        for _ in range(count * cut):
            scratch += unit_scratch(orders.pop(0), rows, D // cut)
    outs = [jax.ShapeDtypeStruct((SLOT, D), LOW)] * 2 + [
        jax.ShapeDtypeStruct((rows, FF), F32),
        jax.ShapeDtypeStruct((4 * rows, D), F32),
        jax.ShapeDtypeStruct((3 * rows, D), F32),
        jax.ShapeDtypeStruct((rows, D), F32),
        jax.ShapeDtypeStruct((16, D), F32),
        jax.ShapeDtypeStruct((rest, 2, 2, 2, 2, D), LOW),
        jax.ShapeDtypeStruct((1, 128), F32),
    ]
    return pl.pallas_call(
        functools.partial(layer_kernel, rest),
        out_shape=tuple(outs),
        in_specs=[smem, smem] + [vmem] * 4 + [anywhere] * 7,
        out_specs=tuple([anywhere] * 2 + [vmem] * 7),
        scratch_shapes=scratch,
        compiler_params=pltpu.CompilerParams(
            collective_id=0, has_side_effects=True, vmem_limit_bytes=61 << 20
        ),
    )(lengths, labels, biases, norm_gains, bias_up.reshape(1, FF), w_class, tokens, cotangent, w_qkv, w_out, w_up, w_down, w_pool)


def finish_kernel(rest, *refs):
    *moved, small, everyone, loss = refs[:9]
    targets = refs[9:15]
    losses, g_pool, g_class, g_biases, g_gains, g_bias_up, g_pool_bias = refs[15:22]
    *stages, sem_in, sem_out = refs[22:]
    arrive = [pltpu.make_async_copy(src, mid, sem_in.at[i]) for i, (src, mid) in enumerate(zip(moved, stages))]
    leave = [pltpu.make_async_copy(mid, dst, sem_out.at[i]) for i, (mid, dst) in enumerate(zip(stages, targets))]
    for copy in arrive:
        copy.start()
    for before, after in zip(arrive, leave):
        before.wait()
        after.start()
    rank = lax.axis_index("batch") * 4 + lax.axis_index("head")
    own = D // (8 * rest)
    own_up = 4 * own
    losses[...] = loss[0:1, 0:1]

    def window(array, start, size):
        at = lax.broadcasted_iota(jnp.int32, (D, size), 0)
        want = lax.broadcasted_iota(jnp.int32, (D, size), 1)
        return exact(array, (at == want + start).astype(F32))

    picked = window(small[...], rank * own, own)
    g_class[...] = picked[0:3]
    g_biases[...] = picked[3:9]
    g_gains[...] = picked[9:11]
    g_pool_bias[...] = picked[15:16]
    flat = rank * own_up
    part = flat // D
    pick = lax.broadcasted_iota(jnp.int32, (4, 1), 0) == part
    chosen = jnp.sum(jnp.where(pick, small[11:15], 0.0), axis=0, keepdims=True)
    g_bias_up[...] = window(jnp.broadcast_to(chosen, (8, D)), flat - part * D, own_up)[0:1]
    d_pre = window(everyone[:, 1].astype(F32), rank * own, own)
    g_pool[...] = lax.dot_general(
        d_pre, everyone[:, 0].astype(F32), (((0,), (0,)), ((), ())), precision=lax.Precision.HIGHEST, preferred_element_type=F32
    )
    for copy in leave:
        copy.wait()


def finish(rest, results):
    own = D // (8 * rest)
    vmem = pl.BlockSpec(memory_space=pltpu.VMEM)
    anywhere = pl.BlockSpec(memory_space=pl.ANY)
    shape = lambda *s: jax.ShapeDtypeStruct(s, F32)
    results = list(results)
    results[7] = results[7].reshape(8 * rest, 2, D)
    outs = [jax.ShapeDtypeStruct((SLOT, D), LOW)] * 2 + [
        shape(own, FF), shape(4 * own, D), shape(3 * own, D), shape(own, D),
        shape(1, 1), shape(own, D), shape(3, own), shape(6, own), shape(2, own), shape(1, 4 * own), shape(1, own),
    ]
    (out, gtok, down, up, qkv, attn, losses, pool, g_class, g_biases, g_gains, g_bias_up, g_pool_bias) = pl.pallas_call(
        functools.partial(finish_kernel, rest),
        out_shape=tuple(outs),
        in_specs=[anywhere] * 6 + [vmem] * 3,
        out_specs=tuple([anywhere] * 6 + [vmem] * 7),
        scratch_shapes=[pltpu.VMEM(o.shape, o.dtype) for o in outs[:6]] + [pltpu.SemaphoreType.DMA((6,))] * 2,
        compiler_params=pltpu.CompilerParams(vmem_limit_bytes=60 << 20),
    )(*results)
    return (
        out, gtok, losses.reshape(-1), qkv.T, attn.T, up.T, down.T, pool.T, g_class, g_biases, g_gains,
        g_bias_up.reshape(-1), g_pool_bias.reshape(-1),
    )


def per_device(
    tokens,
    cotangent,
    lengths,
    labels,
    w_qkv,
    w_out,
    w_up,
    w_down,
    w_pool,
    w_class,
    biases,
    norm_gains,
    bias_up,
):
    rest = lax.axis_size("batch") // 2
    if rest == 4:
        return finish(rest, layer(
            rest, tokens, cotangent, lengths, labels, w_qkv, w_out, w_up, w_down, w_pool, w_class, biases, norm_gains,
            bias_up,
        ))
    head_rank = lax.axis_index("head")
    rank = lax.axis_index("batch") * 4 + head_rank
    length = lax.dynamic_index_in_dim(lengths, head_rank, keepdims=False)
    label = lax.dynamic_index_in_dim(labels, head_rank, keepdims=False)
    slot_live = (jnp.arange(SLOT) < length).astype(F32)
    zeros_key = jnp.zeros((D,), F32)
    packed = jnp.dot(tokens, w_qkv, preferred_element_type=F32) + jnp.concatenate(
        [biases[0], zeros_key, biases[1]]
    )
    packed = packed.astype(LOW)
    context, probs = attention(packed, length)
    attn = jnp.dot(context, w_out, preferred_element_type=F32) + biases[2]
    first_sum = tokens.astype(F32) + attn
    norm_one, first_pull = jax.vjp(layer_norm, first_sum, norm_gains[0], biases[3])
    norm_low = norm_one.astype(LOW)
    hidden_up = jnp.dot(norm_low, w_up, preferred_element_type=F32) + bias_up
    activated_full, gelu_pull = jax.vjp(exact_gelu, hidden_up)
    activated = activated_full.astype(LOW)
    branch = jnp.dot(activated, w_down, preferred_element_type=F32) + biases[4]
    out_full, second_pull = jax.vjp(layer_norm, norm_one + branch, norm_gains[1], biases[5])
    leading = out_full[:1].astype(LOW)
    pooled = jnp.tanh(jnp.dot(leading, w_pool, preferred_element_type=F32) + biases[6])
    pooled_low = pooled.astype(LOW)
    logits = against(pooled_low, w_class)
    onehot = (jnp.arange(CLASSES)[None, :] == label).astype(F32)
    losses = jax.nn.logsumexp(logits, axis=-1) - jnp.sum(onehot * logits, axis=-1)
    d_logits = jax.nn.softmax(logits, axis=-1) - onehot
    g_class = exact(d_logits.T, pooled_low.astype(F32))
    d_pre = exact(d_logits, w_class.astype(F32)) * (1.0 - pooled * pooled)
    d_leading = exact(d_pre, w_pool.astype(F32).T)
    d_out = cotangent.astype(F32) * slot_live[:, None]
    d_out = d_out.at[0].add(d_leading[0])
    d_h2, g_gain_two, g_shift_two = second_pull(d_out)
    d_branch = d_h2.astype(LOW)
    g_bias_down = jnp.sum(d_branch.astype(F32), axis=0)
    g_down_t = inner(d_branch, activated)
    d_activated = against(d_branch, w_down)
    d_up = gelu_pull(d_activated)[0].astype(LOW)
    g_bias_up = jnp.sum(d_up.astype(F32), axis=0)
    g_up_t = inner(d_up, norm_low)
    d_norm_one = d_h2 + against(d_up, w_up)
    d_h1, g_gain_one, g_shift_one = first_pull(d_norm_one)
    d_attn = d_h1.astype(LOW)
    g_bias_out = jnp.sum(d_attn.astype(F32), axis=0)
    g_out_t = inner(d_attn, context)
    d_context = against(d_attn, w_out).astype(LOW)
    d_packed = attention_back(packed, probs, d_context)
    g_qkv_t = inner(d_packed, tokens)
    column_sums = jnp.sum(d_packed.astype(F32), axis=0)
    grad_tokens = (d_h1 + against(d_packed, w_qkv)).astype(LOW)
    small = jnp.concatenate(
        [
            g_class,
            jnp.stack([column_sums[:D], column_sums[2 * D :], g_bias_out, g_shift_one, g_bias_down, g_shift_two]),
            jnp.stack([g_gain_one, g_gain_two]),
            g_bias_up.reshape(FF // D, D),
            d_pre,
        ]
    )
    lead = jnp.concatenate([leading.astype(F32), d_pre])
    down = owner_blocks(g_down_t, rest, FF)
    up = owner_blocks(g_up_t, rest, D)
    last = jnp.concatenate([owner_blocks(g_qkv_t, rest, D), owner_blocks(g_out_t, rest, D)], axis=4)
    half = up.shape[4] // 2
    parts = [
        down[..., : FF // 2], down[..., FF // 2 :],
        up[..., :half, :], up[..., half:, :],
        last[..., :half, :], last[..., half:, :],
    ]
    *sums, small, everyone = reduce_gradients(rest, parts, small, lead)
    g_down = jnp.concatenate(sums[0:2], axis=1).T
    g_up = jnp.concatenate(sums[2:4], axis=0).T
    g_last = jnp.concatenate(sums[4:6], axis=0).T
    own_qkv = 3 * D // (8 * rest)
    own = D // (8 * rest)
    everyone = everyone.reshape(8 * rest, 2, D)
    window = lax.dynamic_slice_in_dim(small, rank * own, own, axis=1)
    pre_window = lax.dynamic_slice_in_dim(everyone[:, 1], rank * own, own, axis=1)
    g_pool = lax.dot_general(
        everyone[:, 0], pre_window, (((0,), (0,)), ((), ())),
        precision=lax.Precision.HIGHEST, preferred_element_type=F32,
    )
    own_up = FF // (8 * rest)
    g_bias_up = lax.dynamic_slice_in_dim(small[11:15].reshape(FF), rank * own_up, own_up)
    return (
        out_full.astype(LOW),
        grad_tokens,
        losses,
        g_last[:, :own_qkv],
        g_last[:, own_qkv:],
        g_up,
        g_down,
        g_pool,
        window[:3],
        window[3:9],
        window[9:11],
        g_bias_up,
        window[15],
    )


def solution(mesh):
    return jax.shard_map(
        per_device,
        mesh=mesh,
        in_specs=(
            P(("batch", "head"), None),
            P(("batch", "head"), None),
            P("batch"),
            P("batch"),
            P(),
            P(),
            P(),
            P(),
            P(),
            P(),
            P(),
            P(),
            P(),
        ),
        out_specs=(
            P(("batch", "head"), None),
            P(("batch", "head"), None),
            P(("batch", "head")),
            P(None, ("batch", "head")),
            P(None, ("batch", "head")),
            P(None, ("batch", "head")),
            P(None, ("batch", "head")),
            P(None, ("batch", "head")),
            P(None, ("batch", "head")),
            P(None, ("batch", "head")),
            P(None, ("batch", "head")),
            P(("batch", "head")),
            P(("batch", "head")),
        ),
        check_vma=False,
    )
```

```python
import functools

import jax
import jax.numpy as jnp
from jax import lax
from jax.experimental import pallas as pl
from jax.experimental.pallas import tpu as pltpu
from jax.sharding import PartitionSpec as P

D = 768
HEADS = 12
HEAD_DIM = 64
FF = 3072
CLASSES = 3
SLOT = 512
MESH = pl.DeviceIdType.MESH
LOW = jnp.bfloat16
F32 = jnp.float32


def layer_norm(hidden, gain, shift):
    center = hidden - jnp.mean(hidden, axis=-1, keepdims=True)
    spread = jnp.mean(center * center, axis=-1, keepdims=True)
    return center * lax.rsqrt(spread + 1e-12) * gain + shift


def exact_gelu(hidden):
    return jax.nn.gelu(hidden, approximate=False)


def inner(left, right):
    return lax.dot_general(
        left, right, (((0,), (0,)), ((), ())), preferred_element_type=jnp.float32
    )


def against(left, right):
    return lax.dot_general(
        left, right, (((1,), (1,)), ((), ())), preferred_element_type=jnp.float32
    )


def exact(left, right):
    return jnp.dot(left, right, precision=lax.Precision.HIGHEST, preferred_element_type=jnp.float32)


class Place:
    def __init__(self, rest):
        batch = lax.axis_index("batch")
        head = lax.axis_index("head")
        self.rest = rest
        self.z = batch // 2
        self.y = lax.rem(batch, 2)
        self.x = head // 2
        self.c = lax.rem(head, 2)

    def device(self, z, y, x, c):
        return (z * 2 + y, x * 2 + c)

    def core_peer(self):
        return self.device(self.z, self.y, self.x, 1 - self.c)

    def x_peer(self):
        return self.device(self.z, self.y, 1 - self.x, self.c)

    def y_peer(self):
        return self.device(self.z, 1 - self.y, self.x, self.c)

    def z_at(self, offset):
        return lax.rem(self.z + offset, self.rest)

    def z_peer(self, offset):
        return self.device(self.z_at(offset), self.y, self.x, self.c)

    def barrier(self):
        sem = pltpu.get_barrier_semaphore()
        for peer in (self.core_peer(), self.x_peer(), self.y_peer()):
            pl.semaphore_signal(sem, inc=1, device_id=peer, device_id_type=MESH)
        for offset in range(1, self.rest):
            pl.semaphore_signal(sem, inc=1, device_id=self.z_peer(offset), device_id_type=MESH)
        pl.semaphore_wait(sem, 3 + self.rest - 1)


def remote(src, dst, send, recv, peer):
    return pltpu.make_async_remote_copy(
        src_ref=src, dst_ref=dst, send_sem=send, recv_sem=recv, device_id=peer, device_id_type=MESH
    )


class Reduce:
    def __init__(self, place, part, bufs, sems, x_first):
        self.place, self.part, self.x_first = place, part, x_first
        self.r1, self.r2, self.r3, self.r4 = bufs
        send, recv, zsend, zrecv = sems
        p = place
        if x_first:
            far, near, second_far, second_near = (1 - p.x, p.x, 1 - p.y, p.y)
            peers = (p.x_peer(), p.y_peer())
            src2 = self.r1.at[far]
        else:
            far, near, second_far, second_near = (1 - p.y, p.y, 1 - p.x, p.x)
            peers = (p.y_peer(), p.x_peer())
            src2 = self.r1.at[:, far]
        self.near, self.second_near = near, second_near
        self.copies = [
            remote(part.at[1 - p.c], self.r1, send.at[0], recv.at[0], p.core_peer()),
            remote(src2, self.r2, send.at[1], recv.at[1], peers[0]),
            remote(self.r2.at[second_far], self.r3, send.at[2], recv.at[2], peers[1]),
        ]
        self.last = [
            remote(self.r3.at[p.z_at(k)], self.r4.at[k - 1], zsend.at[k - 1], zrecv.at[k - 1], p.z_peer(k))
            for k in range(1, p.rest)
        ]

    def start(self):
        self.copies[0].start()

    def step1(self):
        p = self.place
        self.copies[0].wait()
        for i in range(2):
            for j in range(2):
                def add(k, carry, i=i, j=j):
                    self.r1[i, j, k] = self.r1[i, j, k] + self.part[p.c, i, j, k]
                    return carry
                lax.fori_loop(0, p.rest, add, 0)
        self.copies[1].start()

    def step2(self):
        p = self.place
        self.copies[1].wait()
        for i in range(2):
            def add(k, carry, i=i):
                own = self.r1[self.near, i, k] if self.x_first else self.r1[i, self.near, k]
                self.r2[i, k] = self.r2[i, k] + own
                return carry
            lax.fori_loop(0, p.rest, add, 0)
        self.copies[2].start()

    def step3(self):
        p = self.place
        self.copies[2].wait()

        def add(k, carry):
            self.r3[k] = self.r3[k] + self.r2[self.second_near, k]
            return carry
        lax.fori_loop(0, p.rest, add, 0)
        for copy in self.last:
            copy.start()

    def total(self):
        p = self.place
        for copy in self.last:
            copy.wait()
        result = self.r3[p.z].astype(F32)
        for k in range(1, p.rest):
            result = result + self.r4[k - 1].astype(F32)
        return result


def chunk_scratch(rest, rows, width):
    return [
        pltpu.VMEM((2, 2, rest, rows, width), LOW),
        pltpu.VMEM((2, rest, rows, width), LOW),
        pltpu.VMEM((rest, rows, width), LOW),
        pltpu.VMEM((rest - 1, rows, width), LOW),
        pltpu.SemaphoreType.DMA((3,)),
        pltpu.SemaphoreType.DMA((3,)),
        pltpu.SemaphoreType.DMA((rest - 1,)),
        pltpu.SemaphoreType.DMA((rest - 1,)),
    ]


class Small:
    def __init__(self, place, small, lead, everyone, bufs):
        got, gotz, send, recv, zsend, zrecv, gsend, grecv, gzsend, gzrecv = bufs
        p = place
        self.place, self.small, self.got, self.gotz = p, small, got, gotz
        self.lead, self.everyone = lead, everyone
        peers = (p.core_peer(), p.x_peer(), p.y_peer())
        blocks = (
            everyone.at[p.z, p.y, p.x, p.c], everyone.at[p.z, p.y, p.x], everyone.at[p.z, p.y],
        )
        self.sums = [remote(small, got.at[i], send.at[i], recv.at[i], peers[i]) for i in range(3)]
        self.sum_last = [
            remote(small, gotz.at[k - 1], zsend.at[k - 1], zrecv.at[k - 1], p.z_peer(k)) for k in range(1, p.rest)
        ]
        self.gathers = [remote(blocks[i], blocks[i], gsend.at[i], grecv.at[i], peers[i]) for i in range(3)]
        self.gather_last = [
            remote(everyone.at[p.z], everyone.at[p.z], gzsend.at[k - 1], gzrecv.at[k - 1], p.z_peer(k))
            for k in range(1, p.rest)
        ]

    def gather_start(self):
        p = self.place
        self.everyone[p.z, p.y, p.x, p.c] = self.lead[...]
        self.gathers[0].start()

    def gather_step(self, i):
        self.gathers[i].wait()
        if i < 2:
            self.gathers[i + 1].start()
        else:
            for copy in self.gather_last:
                copy.start()

    def gather_end(self):
        for copy in self.gather_last:
            copy.wait()

    def sum_start(self):
        self.sums[0].start()

    def sum_step(self, i):
        self.sums[i].wait()
        self.small[...] = self.small[...] + self.got[i]
        if i < 2:
            self.sums[i + 1].start()
        else:
            for copy in self.sum_last:
                copy.start()

    def sum_end(self):
        for copy in self.sum_last:
            copy.wait()
        total = self.small[...]
        for k in range(1, self.place.rest):
            total = total + self.gotz[k - 1]
        return total


def small_scratch(rest):
    return [
        pltpu.VMEM((3, 16, D), F32),
        pltpu.VMEM((rest - 1, 16, D), F32),
    ] + [pltpu.SemaphoreType.DMA((3,)), pltpu.SemaphoreType.DMA((3,)),
         pltpu.SemaphoreType.DMA((rest - 1,)), pltpu.SemaphoreType.DMA((rest - 1,))] * 2


def reduce_kernel(rest, n_chunks, *refs):
    parts = refs[:n_chunks]
    small_in, lead = refs[n_chunks : n_chunks + 2]
    outs = refs[n_chunks + 2 : 2 * n_chunks + 2]
    small_out, everyone = refs[2 * n_chunks + 2 : 2 * n_chunks + 4]
    scratch = refs[2 * n_chunks + 4 :]
    place = Place(rest)
    chunks = []
    for i in range(n_chunks):
        own = scratch[8 * i : 8 * i + 8]
        chunks.append(Reduce(place, parts[i], own[:4], own[4:], i % 2 == 0))
    rest_scratch = scratch[8 * n_chunks :]
    small = Small(place, rest_scratch[0], lead, everyone, rest_scratch[1:])
    rest_scratch[0][...] = small_in[...]
    place.barrier()
    small.gather_start()
    small.sum_start()
    steps = [[c.step1, c.step2, c.step3] for c in chunks]
    for chunk in chunks:
        chunk.start()
    for i in range(3):
        small.gather_step(i)
        small.sum_step(i)
    for phase in range(n_chunks + 4):
        for i in range(n_chunks):
            k = phase - i
            if i % 2 == 1:
                k = phase - i + 1
            if 0 <= k < 3:
                steps[i][k]()
            if k == 3:
                outs[i][...] = chunks[i].total()
    small.gather_end()
    small_out[...] = small.sum_end()


def reduce_gradients(rest, parts, small, lead):
    vmem = pl.BlockSpec(memory_space=pltpu.VMEM)
    scratch = []
    for part in parts:
        scratch += chunk_scratch(rest, *part.shape[4:])
    scratch += [pltpu.VMEM((16, D), F32)] + small_scratch(rest)
    outs = [jax.ShapeDtypeStruct(part.shape[4:], F32) for part in parts]
    outs += [
        jax.ShapeDtypeStruct((16, D), F32),
        jax.ShapeDtypeStruct((rest, 2, 2, 2, 2, D), F32),
    ]
    return pl.pallas_call(
        functools.partial(reduce_kernel, rest, len(parts)),
        out_shape=tuple(outs),
        in_specs=[vmem] * (len(parts) + 2),
        out_specs=tuple([vmem] * len(outs)),
        scratch_shapes=scratch,
        compiler_params=pltpu.CompilerParams(
            collective_id=0, has_side_effects=True, vmem_limit_bytes=60 << 20
        ),
    )(*parts, small, lead)


def owner_blocks(grad_t, rest, width):
    rows = grad_t.shape[0] // (8 * rest)
    view = grad_t.astype(LOW).reshape(rest, 2, 2, 2, rows, width)
    return view.transpose(3, 2, 1, 0, 4, 5)


def attention(packed, length):
    heads = packed.reshape(SLOT, 3, HEADS, HEAD_DIM)
    queries, keys_all, values = heads[:, 0], heads[:, 1], heads[:, 2]
    scores = jnp.einsum("qhd,khd->hqk", queries, keys_all, preferred_element_type=F32) * HEAD_DIM ** (-0.5)
    scores = jnp.where((jnp.arange(SLOT) < length)[None, None, :], scores, -1e30)
    row_max = jnp.max(scores, axis=-1, keepdims=True)
    weights = jnp.exp(scores - row_max)
    weights = weights / jnp.sum(weights, axis=-1, keepdims=True)
    low = weights.astype(LOW)
    context = jnp.einsum("hqk,khd->qhd", low, values, preferred_element_type=F32)
    return context.astype(LOW).reshape(SLOT, D), low


def attention_back(packed, low, d_context):
    heads = packed.reshape(SLOT, 3, HEADS, HEAD_DIM)
    queries, keys_all, values = heads[:, 0], heads[:, 1], heads[:, 2]
    d_heads = d_context.reshape(SLOT, HEADS, HEAD_DIM)
    weights = low.astype(F32)
    d_weights = jnp.einsum("qhd,khd->hqk", d_heads, values, preferred_element_type=F32)
    d_values = jnp.einsum("hqk,qhd->khd", low, d_heads, preferred_element_type=F32)
    row_dot = jnp.sum(weights * d_weights, axis=-1, keepdims=True)
    d_scores = (weights * (d_weights - row_dot)).astype(LOW)
    scale = HEAD_DIM ** (-0.5)
    d_queries = jnp.einsum("hqk,khd->qhd", d_scores, keys_all, preferred_element_type=F32) * scale
    d_keys = jnp.einsum("hqk,qhd->khd", d_scores, queries, preferred_element_type=F32) * scale
    return jnp.stack([d_queries, d_keys, d_values], axis=1).astype(LOW).reshape(SLOT, 3 * D)


def nn(left, right):
    return jnp.dot(left, right, preferred_element_type=F32)


def aligned(index, step):
    return pl.ds(pl.multiple_of(index * step, step), step)


def normalized(hidden):
    center = hidden - jnp.mean(hidden, axis=-1, keepdims=True)
    spread = jnp.mean(center * center, axis=-1, keepdims=True)
    scale = lax.rsqrt(spread + 1e-12)
    return center * scale, scale


def normalized_back(normed, scale, d_normed):
    first = jnp.mean(d_normed, axis=-1, keepdims=True)
    second = jnp.mean(d_normed * normed, axis=-1, keepdims=True)
    return scale * (d_normed - first - normed * second)


class Unit:
    def __init__(self, place, order, part, bufs, send, recv, put, after):
        p = self.place = place
        self.put, self.after = put, after
        self.at = 0
        self.legs = []
        bufs = list(bufs)
        count = part.shape[0] // 2
        held = bufs.pop(0)
        copy = remote(part.at[pl.ds((1 - p.c) * count, count)], held, send.at[0], recv.at[0], p.core_peer())
        self.legs.append((copy.start, self.pair_end(copy, held, part, p.c * count, count, False)))
        base = 0
        slot = 1
        for i, axis in enumerate(order):
            last = i == len(order) - 1
            if axis == "z":
                count = count // 4
                self.line(held, base, count, bufs.pop(0), bufs.pop(0), send, recv, slot, last)
                base = base + p.z * count
                slot += 3
            else:
                count = count // 2
                mine, peer = (p.x, p.x_peer()) if axis == "x" else (p.y, p.y_peer())
                got = bufs.pop(0)
                copy = remote(held.at[pl.ds(base + (1 - mine) * count, count)], got, send.at[slot], recv.at[slot], peer)
                self.legs.append((copy.start, self.pair_end(copy, got, held, base + mine * count, count, last)))
                held, base = got, 0
                slot += 1

    def pair_end(self, copy, got, own, start, count, last):
        def end():
            copy.wait()
            if last:
                self.put(got[0].astype(F32) + own[start].astype(F32))
            elif count >= 8:
                def add(i, carry):
                    got[pl.ds(i * 4, 4)] = got[pl.ds(i * 4, 4)] + own[pl.ds(start + i * 4, 4)]
                    return carry
                lax.fori_loop(0, count // 4, add, 0)
            else:
                got[...] = got[...] + own[pl.ds(start, count)]
        return end

    def line(self, held, base, n, wide, single, send, recv, slot, last):
        p = self.place
        z = p.z
        outer = jnp.logical_or(z == 0, z == 3)
        inner = jnp.logical_not(outer)
        low = z < 2
        near = jnp.where(low, 1 - z, 5 - z)
        far = jnp.where(low, z + 2, z - 2)
        middle = 3 - z

        def at(block, count=n):
            return held.at[pl.ds(base + block * n, count)]

        def device(block):
            return p.device(block, p.y, p.x, p.c)

        outward = remote(at(jnp.where(z == 0, 1, 0), 3 * n), wide, send.at[slot], recv.at[slot], device(near))
        back = remote(at(near), wide.at[0:n], send.at[slot], recv.at[slot], device(near))
        across = remote(at(middle), single, send.at[slot + 1], recv.at[slot + 1], device(middle))
        beyond = remote(at(far), wide.at[n : 2 * n], send.at[slot + 2], recv.at[slot + 2], device(far))

        def begin_first():
            @pl.when(outer)
            def _():
                outward.start()

            @pl.when(inner)
            def _():
                back.start()

        def end_first():
            @pl.when(outer)
            def _():
                outward.wait_send()
                back.wait_recv()

            @pl.when(inner)
            def _():
                back.wait_send()
                outward.wait_recv()
                start = base + jnp.where(z == 1, n, 0)
                held[pl.ds(start, 3 * n)] = held[pl.ds(start, 3 * n)] + wide[...]

        def begin_second():
            @pl.when(inner)
            def _():
                across.start()
                beyond.start()

        def end_second():
            @pl.when(outer)
            def _():
                beyond.wait_recv()
                total = held[pl.ds(base + z * n, n)].astype(F32) + wide[0:n].astype(F32) + wide[n : 2 * n].astype(F32)
                if last:
                    self.put(total[0])
                else:
                    held[pl.ds(base + z * n, n)] = total.astype(LOW)

            @pl.when(inner)
            def _():
                across.wait()
                beyond.wait_send()
                total = held[pl.ds(base + z * n, n)].astype(F32) + single[...].astype(F32)
                if last:
                    self.put(total[0])
                else:
                    held[pl.ds(base + z * n, n)] = total.astype(LOW)

        self.legs.append((begin_first, end_first))
        self.legs.append((begin_second, end_second))

    def step(self):
        if self.at > 0:
            self.legs[self.at - 1][1]()
        if self.at < len(self.legs):
            self.legs[self.at][0]()
        else:
            self.after()
        self.at += 1


class Gather:
    def __init__(self, place, lead, everyone, send, recv, after):
        self.after = after
        p = place
        peers = (p.core_peer(), p.x_peer(), p.y_peer())
        own = everyone.at[p.z, p.y, p.x, p.c]
        blocks = (own, everyone.at[p.z, p.y, p.x], everyone.at[p.z, p.y])
        groups = [[remote(blocks[i], blocks[i], send.at[i], recv.at[i], peers[i])] for i in range(3)]
        groups.append([
            remote(everyone.at[p.z], everyone.at[p.z], send.at[k + 2], recv.at[k + 2], p.z_peer(k)) for k in range(1, p.rest)
        ])
        self.groups, self.at, self.own, self.lead = groups, 0, own, lead

    def step(self):
        if self.at == 0:
            self.own[...] = self.lead[...]
        else:
            for copy in self.groups[self.at - 1]:
                copy.wait()
        if self.at < 4:
            for copy in self.groups[self.at]:
                copy.start()
        else:
            self.after()
        self.at += 1


class Total:
    def __init__(self, place, small, low, got, send, recv, put):
        p = place
        peers = (p.core_peer(), p.x_peer(), p.y_peer())
        groups = [[remote(low, got.at[i], send.at[i], recv.at[i], peers[i])] for i in range(3)]
        groups.append([
            remote(low, got.at[k + 2], send.at[k + 2], recv.at[k + 2], p.z_peer(k)) for k in range(1, p.rest)
        ])
        self.groups, self.at, self.small, self.low, self.got, self.put = groups, 0, small, low, got, put

    def step(self):
        total = self.small[...]
        if self.at > 0:
            first = self.at - 1
            for i, copy in enumerate(self.groups[first]):
                copy.wait()
                total = total + self.got[first + i].astype(F32)
        if self.at < 4:
            self.small[...] = total
            self.low[...] = total.astype(LOW)
            for copy in self.groups[self.at]:
                copy.start()
        else:
            self.put(total)
        self.at += 1


def block_index(order, rest, z, y, x, c):
    sizes = {"x": 2, "y": 2, "z": rest}
    at = {"x": x, "y": y, "z": z}
    index = c
    for axis in order:
        index = index * sizes[axis] + at[axis]
    return index


def owners(rest):
    return [(z, y, x, c) for z in range(rest) for y in range(2) for x in range(2) for c in range(2)]


def unit_scratch(order, rows, width):
    blocks = 16
    bufs = [pltpu.VMEM((blocks, rows, width), LOW)]
    for axis in order:
        if axis == "z":
            blocks = blocks // 4
            bufs += [pltpu.VMEM((3 * blocks, rows, width), LOW), pltpu.VMEM((blocks, rows, width), LOW)]
        else:
            blocks = blocks // 2
            bufs.append(pltpu.VMEM((blocks, rows, width), LOW))
    return bufs + [pltpu.SemaphoreType.DMA((6,)), pltpu.SemaphoreType.DMA((6,))]


UNITS = (("down", 4, 1), ("up", 4, 1), ("out", 1, 1), ("qkv", 3, 3))
ORDERS = (
    "xyz", "zxy", "yzx", "xzy", "zxy", "yxz", "xyz", "yxz", "xyz", "yzx", "yxz", "xyz", "xyz", "xyz", "xyz", "yxz", "yxz", "yxz",
)
PLAN = (
    (),
    (),
    (),
    (),
    (),
    (),
    (),
    (),
    (1, 0, 2,),
    (3,),
    (),
    (0, 2,),
    (5, 4, 1, 6,),
    (7,),
    (8,),
    (),
    (3,),
    (5, 2, 6,),
    (8, 0, 7, 4, 9, 6, 18, 11,),
    (5, 10, 14, 0, 8, 12, 17, 3, 13, 6, 18, 9, 16, 7, 14, 15, 10,),
    (),
    (8, 17, 0, 18, 12, 11, 16, 9, 19, 4, 13, 10, 5, 14, 17, 15, 7, 1, 16, 12, 19, 2, 9, 11, 3, 8, 10, 13, 6, 17, 15, 4, 14, 16, 7, 19, 12, 1, 11, 5, 13, 9, 3, 15, 10, 18, 14, 17, 16, 2, 12, 4, 11, 1, 13, 19, 15,),
)
N_IN = 13
N_OUT = 9


def layer_kernel(rest, *refs):
    (lengths, labels, biases_h, gains_h, bias_up_h, w_class_h, tokens_h, cot_h, wqkv_h, wout_h, wup_h, wdown_h, wpool_h) = refs[:N_IN]
    out_h, gtok_h, down_out, up_out, qkv_out, attn_out, small_out, everyone_out, loss_out = refs[N_IN : N_IN + N_OUT]
    scratch = list(refs[N_IN + N_OUT :])
    (
        tokens, w_qkv, w_out, w_up, w_down, packed, weights, inverse, context, normed_one, norm_low,
        activated, slope, d_hidden, d_low, d_packed, part0, part1, part2, part3, scale_one, small, lead, in_sem, out_sem,
    ) = scratch[:25]
    parts = [part0, part1, part2, part3]
    cot = d_low
    d_context = norm_low
    wide = SLOT
    pool_wide = d_packed.at[0:D]
    pool_rest = d_packed.at[D : 2 * D, 0 : D - wide]
    out_wide = d_packed.at[2 * D : 2 * D + SLOT]
    out_rest = d_packed.at[D : D + SLOT, wide // 2 : wide // 2 + D - wide]
    place = Place(rest)
    small_bufs = scratch[25:31]
    biases, gains, bias_up, w_class = scratch[31:35]
    down_mid, up_mid, qkv_mid, attn_mid, small_mid, everyone, loss_mid = scratch[35:42]
    little_sem, done_sem = scratch[42:44]
    unit_bufs = scratch[44:]
    little = [
        pltpu.make_async_copy(src, dst, little_sem.at[i])
        for i, (src, dst) in enumerate([(biases_h, biases), (gains_h, gains), (bias_up_h, bias_up), (w_class_h, w_class)])
    ]
    head_rank = lax.axis_index("head")
    length = lengths[head_rank]
    label = labels[head_rank]
    loads = [
        pltpu.make_async_copy(src, dst, in_sem.at[i])
        for i, (src, dst) in enumerate(
            [(tokens_h, tokens), (wqkv_h.at[:, 0:D], w_qkv.at[:, 0:D]), (wqkv_h.at[:, D : 2 * D], w_qkv.at[:, D : 2 * D]),
             (wqkv_h.at[:, 2 * D :], w_qkv.at[:, 2 * D :]), (wout_h, w_out), (wup_h, w_up),
             (wdown_h, w_down), (cot_h, cot), (wpool_h.at[:, 0:wide], pool_wide), (wpool_h.at[:, wide:D], pool_rest)]
        )
    ]
    for load in loads[:4] + little:
        load.start()
    sem = pltpu.get_barrier_semaphore()
    for peer in (place.core_peer(), place.x_peer(), place.y_peer()):
        pl.semaphore_signal(sem, inc=1, device_id=peer, device_id_type=MESH)
    for offset in range(1, rest):
        pl.semaphore_signal(sem, inc=1, device_id=place.z_peer(offset), device_id_type=MESH)

    height = D // 32
    order_of = owners(rest)

    targets = {"down": (down_mid, down_out), "up": (up_mid, up_out), "out": (attn_mid, attn_out), "qkv": (qkv_mid, qkv_out)}
    leaving = []

    def leave(src, dst, i):
        copy = pltpu.make_async_copy(src, dst, done_sem.at[i])
        copy.start()
        leaving.append(copy)
    base_part = {"down": 0, "up": 0, "out": 0, "qkv": 1}

    def put_into(kind, i, columns, n):
        if kind == "down":
            place_of = (slice(None), slice(i * D + columns.start, i * D + columns.stop))
        else:
            place_of = (slice(i * height, (i + 1) * height), columns)
        mid, out = targets[kind]

        def put(total):
            mid[place_of] = total

        return put, lambda: leave(mid.at[place_of], out.at[place_of], n)

    units = []
    number = {}
    at = 0
    for kind, count, cut in UNITS:
        for i in range(count):
            for j in range(cut):
                columns = slice(j * D // cut, (j + 1) * D // cut)
                order = ORDERS[len(units)]
                size = len(unit_scratch(order, height, D // cut))
                own = unit_bufs[at : at + size]
                at += size
                part = parts[base_part[kind] + i]
                if cut > 1:
                    part = part.at[:, :, columns]
                number[kind, i, j] = len(units)
                put, after = put_into(kind, i, columns, len(units))
                units.append(Unit(place, order, part, own[:-2], own[-2], own[-1], put, after))
    def fill(kind, i, owner, columns, value):
        cut = {name: c for name, _, c in UNITS}[kind]
        width = D // cut
        part = parts[base_part[kind] + i]
        for j in range(cut):
            first, last = max(columns.start, j * width), min(columns.stop, (j + 1) * width)
            if first < last:
                index = block_index(ORDERS[number[kind, i, j]], rest, *owner)
                part[index, :, first:last] = value[:, first - columns.start : last - columns.start].astype(LOW)

    def go(kind, i, j):
        units[number[kind, i, j]].step()

    low_small, got_small, *small_sems = small_bufs
    gather, totals = len(units), len(units) + 1

    def put_small(total):
        small_mid[...] = total
        leave(small_mid, small_out, totals)

    units.append(Gather(place, lead, everyone, *small_sems[:2], lambda: leave(everyone, everyone_out, gather)))
    units.append(Total(place, small, low_small, got_small, *small_sems[2:], put_small))
    plan = list(PLAN)

    def steps():
        for i in plan.pop(0):
            units[i].step()

    loads[0].wait()
    for load in little:
        load.wait()
    ones = jnp.ones((8, SLOT), LOW)
    for part in range(3):
        columns = slice(part * D, part * D + D)
        loads[part + 1].wait()
        if part == 0:
            for load in loads[4:]:
                load.start()
        result = nn(tokens[...], w_qkv[:, columns])
        if part == 0:
            result = (result + biases[0:1]).astype(LOW) * jnp.asarray(HEAD_DIM ** (-0.5), LOW)
        elif part == 2:
            result = (result + biases[1:2]).astype(LOW)
        else:
            result = result.astype(LOW)
        packed[:, columns] = result

    key_live = lax.broadcasted_iota(jnp.int32, (SLOT, 1), 0) < length
    lane = lax.broadcasted_iota(jnp.int32, (1, 2 * HEAD_DIM), 1)
    lane_of = [lane < HEAD_DIM, lane >= HEAD_DIM]
    spare = [lane == HEAD_DIM, lane == 0]
    dead = [jnp.where(jnp.logical_and(spare[k], jnp.logical_not(key_live)), -1e30, 0.0).astype(LOW) for k in range(2)]

    def attend(pair):
        at = pair * 2 * HEAD_DIM
        queries = packed[:, at : at + 2 * HEAD_DIM]
        keys_all = packed[:, at + D : at + D + 2 * HEAD_DIM]
        values_t = packed[:, at + 2 * D : at + 2 * D + 2 * HEAD_DIM].T
        got = []
        for k in range(2):
            own_keys = jnp.where(lane_of[k], keys_all, dead[k])
            scores = against(own_keys, jnp.where(lane_of[k], queries, jnp.ones_like(queries)))
            powers = jnp.exp(scores - jnp.max(scores, axis=0, keepdims=True))
            inv = 1.0 / jnp.sum(powers, axis=0, keepdims=True)
            powers = powers.astype(LOW)
            weights[2 * pair + k] = powers
            inverse[pair, k : k + 1] = inv
            got.append(nn(values_t[k * HEAD_DIM : (k + 1) * HEAD_DIM], powers) * inv)
        context[:, at : at + 2 * HEAD_DIM] = jnp.concatenate(got, axis=0).T.astype(LOW)

    for pair in range(HEADS // 2):
        attend(pair)

    blocks = [slice(0, SLOT // 2), slice(SLOT // 2, SLOT)]
    loads[4].wait()
    for rows in blocks:
        hidden = nn(context[rows], w_out[...]) + biases[2:3] + tokens[rows].astype(F32)
        normed, scale = normalized(hidden)
        normed_one[rows] = normed
        scale_one[rows] = scale
        norm_low[rows] = (normed * gains[0:1] + biases[3:4]).astype(LOW)

    loads[5].wait()

    def feed(tile):
        columns = slice(tile * D, (tile + 1) * D)
        hidden = nn(norm_low[...], w_up[:, columns]) + bias_up[0:1, columns]
        share = 0.5 + 0.5 * lax.erf(hidden * 0.7071067811865476)
        activated[:, columns] = (hidden * share).astype(LOW)
        slope[:, columns] = (share + hidden * (jnp.exp(-0.5 * hidden * hidden) * 0.3989422804014327)).astype(LOW)

    for tile in range(FF // D):
        feed(tile)

    for i in (6, 7, 8, 9):
        loads[i].wait()
    row = lax.broadcasted_iota(jnp.int32, (SLOT // 2, 1), 0)
    kept = []
    for k, rows in enumerate(blocks):
        hidden = nn(activated[rows], w_down[...]) + biases[4:5] + (normed_one[rows] * gains[0:1] + biases[3:4])
        normed, scale = normalized(hidden)
        result = normed * gains[1:2] + biases[5:6]
        low = result.astype(LOW)
        out_wide[rows] = low[:, 0:wide]
        out_rest[rows] = low[:, wide:D]
        d_hidden[rows] = normed
        kept.append(scale)
        if k == 0:
            leading = low[0:8]
    out_copies = [
        pltpu.make_async_copy(out_wide, out_h.at[:, 0:wide], out_sem.at[0]),
        pltpu.make_async_copy(out_rest, out_h.at[:, wide:D], out_sem.at[2]),
    ]
    for copy in out_copies:
        copy.start()

    pooled = jnp.concatenate([nn(leading, pool_wide[...]), nn(leading, pool_rest[...])], axis=1)
    pooled = jnp.tanh(pooled + biases[6:7])[0:1]
    pooled_low = pooled.astype(LOW).astype(F32)
    classes = w_class[...].astype(F32)
    logits = jnp.sum(pooled_low * classes, axis=-1, keepdims=True)
    top = jnp.max(logits, axis=0, keepdims=True)
    powers = jnp.exp(logits - top)
    total = jnp.sum(powers, axis=0, keepdims=True)
    onehot = (lax.broadcasted_iota(jnp.int32, (CLASSES, 1), 0) == label).astype(F32)
    loss_mid[...] = jnp.broadcast_to(
        jnp.log(total) + top - jnp.sum(onehot * logits, axis=0, keepdims=True), loss_mid.shape
    )
    leave(loss_mid, loss_out, totals + 1)
    d_logits = powers / total - onehot
    d_pre = jnp.sum(d_logits * classes, axis=0, keepdims=True) * (1.0 - pooled * pooled)
    high = d_pre.astype(LOW).astype(F32)
    middle = (d_pre - high).astype(LOW).astype(F32)
    low = d_pre - high - middle
    eight = lax.broadcasted_iota(jnp.int32, (8, 1), 0)
    split = jnp.where(eight == 0, high, jnp.where(eight == 1, middle, jnp.where(eight == 2, low, 0.0)))
    split = split.astype(LOW)
    d_leading = against(split[:, 0:wide], pool_wide[...]) + against(split[:, wide:D], pool_rest[...])
    d_leading = jnp.sum(d_leading, axis=0, keepdims=True)
    small[0:3] = d_logits * pooled_low
    small[15:16] = d_pre
    lead[0:1] = leading[0:1]
    lead[1:2] = d_pre.astype(LOW)

    shift_two = jnp.zeros((1, D), F32)
    gain_two = jnp.zeros((1, D), F32)
    bias_down = jnp.zeros((1, D), F32)
    for k in (1, 0):
        rows = blocks[k]
        normed, scale = d_hidden[rows], kept[k]
        d_out = jnp.where(row + k * (SLOT // 2) < length, cot[rows].astype(F32), 0.0)
        if k == 0:
            d_out = d_out + jnp.where(row == 0, d_leading, 0.0)
        shift_two = shift_two + jnp.sum(d_out, axis=0, keepdims=True)
        gain_two = gain_two + jnp.sum(d_out * normed, axis=0, keepdims=True)
        d_two = normalized_back(normed, scale, d_out * gains[1:2])
        d_hidden[rows] = d_two
        d_two = d_two.astype(LOW)
        d_low[rows] = d_two
        bias_down = bias_down + jnp.sum(d_two.astype(F32), axis=0, keepdims=True)
    small[8:9] = shift_two
    small[10:11] = gain_two
    small[7:8] = bias_down

    rows = height
    for copy in out_copies:
        copy.wait()
    pl.semaphore_wait(sem, 3 + rest - 1)
    units[gather].step()
    d_branch_t = d_low[...].T
    halves = (slice(0, D // 2), slice(D // 2, D))
    everything = slice(0, D)
    cuts = {name: cut for name, _, cut in UNITS}
    for i in range(4):
        for j, columns in enumerate(halves):
            result = nn(d_branch_t, activated[:, i * D + columns.start : i * D + columns.stop])
            for d, owner in enumerate(order_of):
                fill("down", i, owner, columns, result[d * rows : (d + 1) * rows])
            if cuts["down"] == 2:
                go("down", i, j)
            elif j == 1:
                go("down", i, 0)
            steps()

    for tile in range(FF // D):
        columns = slice(tile * D, (tile + 1) * D)
        d_up = (against(d_low[...], w_down[columns]) * slope[:, columns].astype(F32)).astype(LOW)
        slope[:, columns] = d_up
        small[11 + tile : 12 + tile] = jnp.sum(d_up.astype(F32), axis=0, keepdims=True)
        if tile % 2 == 1:
            steps()
    d_up = slope

    def up_gradient(tile, carry):
        for columns in halves:
            result = inner(d_up[:, aligned(tile, D)], norm_low[:, columns])
            for d in range(8):
                for i in range(4):
                    first = (d * 4 + i) * rows
                    fill("up", i, (tile, *order_of[d][1:]), columns, result[first : first + rows])
        return carry

    lax.fori_loop(0, FF // D, up_gradient, 0)
    for i in range(4):
        for j in range(cuts["up"]):
            go("up", i, j)
    steps()

    shift_one = jnp.zeros((1, D), F32)
    gain_one = jnp.zeros((1, D), F32)
    bias_attn = jnp.zeros((1, D), F32)
    for block in blocks:
        d_norm = d_hidden[block] + against(d_up[block], w_up[...])
        normed = normed_one[block]
        shift_one = shift_one + jnp.sum(d_norm, axis=0, keepdims=True)
        gain_one = gain_one + jnp.sum(d_norm * normed, axis=0, keepdims=True)
        d_one = normalized_back(normed, scale_one[block], d_norm * gains[0:1])
        d_hidden[block] = d_one
        d_one = d_one.astype(LOW)
        d_low[block] = d_one
        bias_attn = bias_attn + jnp.sum(d_one.astype(F32), axis=0, keepdims=True)
        steps()
    small[6:7] = shift_one
    small[9:10] = gain_one
    small[5:6] = bias_attn

    result = inner(d_low[...], context[...])
    for d, owner in enumerate(order_of):
        fill("out", 0, owner, everything, result[d * rows : (d + 1) * rows])
    for j in range(cuts["out"]):
        go("out", 0, j)
    d_context[...] = against(d_low[...], w_out[...]).astype(LOW)
    steps()

    def attend_back(pair, carry):
        at = pl.multiple_of(pair * 2 * HEAD_DIM, 2 * HEAD_DIM)
        queries_t = packed[:, pl.ds(at, 2 * HEAD_DIM)].T
        keys_t = packed[:, pl.ds(at + D, 2 * HEAD_DIM)].T
        values = packed[:, pl.ds(at + 2 * D, 2 * HEAD_DIM)]
        context_t = context[:, pl.ds(at, 2 * HEAD_DIM)].T
        d_context_t = d_context[:, pl.ds(at, 2 * HEAD_DIM)].T
        scaled = []
        dots = []
        for k in range(2):
            own_rows = slice(k * HEAD_DIM, (k + 1) * HEAD_DIM)
            own = d_context_t[own_rows].astype(F32) * inverse[pair, k : k + 1]
            dots.append(jnp.sum(own * context_t[own_rows].astype(F32), axis=0, keepdims=True))
            scaled.append(own.astype(LOW))
        both = jnp.concatenate(scaled, axis=0).T
        for k in range(2):
            own_rows = slice(k * HEAD_DIM, (k + 1) * HEAD_DIM)
            own_values = jnp.where(lane_of[k], values, jnp.zeros_like(values))
            powers = weights[2 * pair + k]
            d_scores = (powers.astype(F32) * (against(own_values, both) - dots[k])).astype(LOW)
            put = pl.multiple_of(at + k * HEAD_DIM, HEAD_DIM)
            d_packed[pl.ds(put, HEAD_DIM)] = (nn(keys_t[own_rows], d_scores) * HEAD_DIM ** (-0.5)).astype(LOW)
            d_packed[pl.ds(put + D, HEAD_DIM)] = against(queries_t[own_rows], d_scores).astype(LOW)
            d_packed[pl.ds(put + 2 * D, HEAD_DIM)] = against(scaled[k], powers).astype(LOW)
        return carry

    for part in range(3):
        lax.fori_loop(2 * part, 2 * part + 2, attend_back, 0)
        steps()

    small[3:4] = against(ones, d_packed[0:D])[0:1]
    small[4:5] = against(ones, d_packed[2 * D : 3 * D])[0:1]
    units[totals].step()
    steps()
    def qkv_gradient(tile, carry):
        result = nn(d_packed[aligned(tile, 24 * rows)], tokens[...])
        for d in range(8):
            for i in range(3):
                first = (d * 3 + i) * rows
                fill("qkv", i, (tile, *order_of[d][1:]), everything, result[first : first + rows])
        return carry

    lax.fori_loop(0, rest, qkv_gradient, 0)
    for i in range(3):
        for j in range(cuts["qkv"]):
            go("qkv", i, j)
    steps()

    for block in blocks:
        d_tokens = nn(w_qkv[...], d_packed[:, block]).T + d_hidden[block]
        d_low[block] = d_tokens.astype(LOW)
        steps()
    token_copy = pltpu.make_async_copy(d_low, gtok_h, out_sem.at[1])
    token_copy.start()
    steps()
    token_copy.wait()
    for copy in leaving:
        copy.wait()


def layer(rest, tokens, cotangent, lengths, labels, w_qkv, w_out, w_up, w_down, w_pool, w_class, biases, norm_gains, bias_up):
    rows = D // 32
    vmem = pl.BlockSpec(memory_space=pltpu.VMEM)
    smem = pl.BlockSpec(memory_space=pltpu.SMEM)
    anywhere = pl.BlockSpec(memory_space=pl.ANY)
    dma = pltpu.SemaphoreType.DMA
    scratch = [
        pltpu.VMEM((SLOT, D), LOW),
        pltpu.VMEM((D, 3 * D), LOW),
        pltpu.VMEM((D, D), LOW),
        pltpu.VMEM((D, FF), LOW),
        pltpu.VMEM((FF, D), LOW),
        pltpu.VMEM((SLOT, 3 * D), LOW),
        pltpu.VMEM((HEADS, SLOT, SLOT), LOW),
        pltpu.VMEM((HEADS // 2, 2, SLOT), F32),
        pltpu.VMEM((SLOT, D), LOW),
        pltpu.VMEM((SLOT, D), F32),
        pltpu.VMEM((SLOT, D), LOW),
        pltpu.VMEM((SLOT, FF), LOW),
        pltpu.VMEM((SLOT, FF), LOW),
        pltpu.VMEM((SLOT, D), F32),
        pltpu.VMEM((SLOT, D), LOW),
        pltpu.VMEM((3 * D, SLOT), LOW),
    ] + [pltpu.VMEM((32, rows, D), LOW)] * 4 + [
        pltpu.VMEM((SLOT, 1), F32),
        pltpu.VMEM((16, D), F32),
        pltpu.VMEM((2, D), LOW),
        dma((10,)),
        dma((3,)),
        pltpu.VMEM((16, D), LOW),
        pltpu.VMEM((6, 16, D), LOW),
        dma((6,)),
        dma((6,)),
        dma((6,)),
        dma((6,)),
        pltpu.VMEM(biases.shape, F32),
        pltpu.VMEM(norm_gains.shape, F32),
        pltpu.VMEM((1, FF), F32),
        pltpu.VMEM(w_class.shape, LOW),
    ]
    outs = [jax.ShapeDtypeStruct((SLOT, D), LOW)] * 2 + [
        jax.ShapeDtypeStruct((rows, FF), F32),
        jax.ShapeDtypeStruct((4 * rows, D), F32),
        jax.ShapeDtypeStruct((3 * rows, D), F32),
        jax.ShapeDtypeStruct((rows, D), F32),
        jax.ShapeDtypeStruct((16, D), F32),
        jax.ShapeDtypeStruct((rest, 2, 2, 2, 2, D), LOW),
        jax.ShapeDtypeStruct((1, 128), F32),
    ]
    scratch += [pltpu.VMEM(o.shape, o.dtype) for o in outs[2:]]
    scratch += [dma((4,)), dma((len(ORDERS) + 3,))]
    orders = list(ORDERS)
    for _, count, cut in UNITS:
        for _ in range(count * cut):
            scratch += unit_scratch(orders.pop(0), rows, D // cut)
    return pl.pallas_call(
        functools.partial(layer_kernel, rest),
        out_shape=tuple(outs),
        in_specs=[smem, smem] + [anywhere] * 11,
        out_specs=tuple([anywhere] * 9),
        scratch_shapes=scratch,
        compiler_params=pltpu.CompilerParams(
            collective_id=0, has_side_effects=True, vmem_limit_bytes=61 << 20
        ),
    )(lengths, labels, biases, norm_gains, bias_up.reshape(1, FF), w_class, tokens, cotangent, w_qkv, w_out, w_up, w_down, w_pool)


def finish_kernel(rest, *refs):
    moved, tables = refs[:6], refs[6:9]
    targets, rest_out = refs[9:15], refs[15:22]
    stages, tables_in, results = refs[22:28], refs[28:31], refs[31:38]
    sem_in, sem_out = refs[38:]
    arrive = [pltpu.make_async_copy(src, mid, sem_in.at[i]) for i, (src, mid) in enumerate(zip(tables + moved, tables_in + stages))]
    leave = [pltpu.make_async_copy(mid, dst, sem_out.at[i]) for i, (mid, dst) in enumerate(zip(stages + results, targets + rest_out))]
    for copy in arrive:
        copy.start()
    small, everyone, loss = tables_in
    losses, g_pool, g_class, g_biases, g_gains, g_bias_up, g_pool_bias = results
    rank = lax.axis_index("batch") * 4 + lax.axis_index("head")
    own = D // (8 * rest)
    own_up = 4 * own
    for copy in arrive[:3]:
        copy.wait()
    losses[...] = loss[0:1, 0:1]

    def window(array, start, size):
        at = lax.broadcasted_iota(jnp.int32, (D, size), 0)
        want = lax.broadcasted_iota(jnp.int32, (D, size), 1)
        return exact(array, (at == want + start).astype(F32))

    leading = everyone[:, 0].astype(F32)
    d_pre = everyone[:, 1].astype(F32)
    both = window(jnp.concatenate([small[...], d_pre], axis=0), rank * own, own)
    picked = both[0:16]
    g_class[...] = picked[0:3]
    g_biases[...] = picked[3:9]
    g_gains[...] = picked[9:11]
    g_pool_bias[...] = picked[15:16]
    flat = rank * own_up
    part = flat // D
    pick = lax.broadcasted_iota(jnp.int32, (4, 1), 0) == part
    chosen = jnp.sum(jnp.where(pick, small[11:15], 0.0), axis=0, keepdims=True)
    g_bias_up[...] = window(jnp.broadcast_to(chosen, (8, D)), flat - part * D, own_up)[0:1]
    g_pool[...] = lax.dot_general(
        both[16:], leading, (((0,), (0,)), ((), ())), precision=lax.Precision.HIGHEST, preferred_element_type=F32
    )
    for before, after in zip(arrive[3:], leave):
        before.wait()
        after.start()
    for copy in leave[6:]:
        copy.start()
    for copy in leave:
        copy.wait()


def finish(rest, results):
    own = D // (8 * rest)
    anywhere = pl.BlockSpec(memory_space=pl.ANY)
    shape = lambda *s: jax.ShapeDtypeStruct(s, F32)
    results = list(results)
    results[7] = results[7].reshape(8 * rest, 2, D)
    outs = [jax.ShapeDtypeStruct((SLOT, D), LOW)] * 2 + [
        shape(own, FF), shape(4 * own, D), shape(3 * own, D), shape(own, D),
        shape(1, 1), shape(own, D), shape(3, own), shape(6, own), shape(2, own), shape(1, 4 * own), shape(1, own),
    ]
    held = lambda arrays: [pltpu.VMEM(o.shape, o.dtype) for o in arrays]
    (out, gtok, down, up, qkv, attn, losses, pool, g_class, g_biases, g_gains, g_bias_up, g_pool_bias) = pl.pallas_call(
        functools.partial(finish_kernel, rest),
        out_shape=tuple(outs),
        in_specs=[anywhere] * 9,
        out_specs=tuple([anywhere] * 13),
        scratch_shapes=held(outs[:6]) + held(results[6:]) + held(outs[6:])
        + [pltpu.SemaphoreType.DMA((9,)), pltpu.SemaphoreType.DMA((13,))],
        compiler_params=pltpu.CompilerParams(vmem_limit_bytes=60 << 20),
    )(*results)
    return (
        out, gtok, losses.reshape(-1), qkv.T, attn.T, up.T, down.T, pool.T, g_class, g_biases, g_gains,
        g_bias_up.reshape(-1), g_pool_bias.reshape(-1),
    )


def per_device(
    tokens,
    cotangent,
    lengths,
    labels,
    w_qkv,
    w_out,
    w_up,
    w_down,
    w_pool,
    w_class,
    biases,
    norm_gains,
    bias_up,
):
    rest = lax.axis_size("batch") // 2
    if rest == 4:
        return finish(rest, layer(
            rest, tokens, cotangent, lengths, labels, w_qkv, w_out, w_up, w_down, w_pool, w_class, biases, norm_gains,
            bias_up,
        ))
    head_rank = lax.axis_index("head")
    rank = lax.axis_index("batch") * 4 + head_rank
    length = lax.dynamic_index_in_dim(lengths, head_rank, keepdims=False)
    label = lax.dynamic_index_in_dim(labels, head_rank, keepdims=False)
    slot_live = (jnp.arange(SLOT) < length).astype(F32)
    zeros_key = jnp.zeros((D,), F32)
    packed = jnp.dot(tokens, w_qkv, preferred_element_type=F32) + jnp.concatenate(
        [biases[0], zeros_key, biases[1]]
    )
    packed = packed.astype(LOW)
    context, probs = attention(packed, length)
    attn = jnp.dot(context, w_out, preferred_element_type=F32) + biases[2]
    first_sum = tokens.astype(F32) + attn
    norm_one, first_pull = jax.vjp(layer_norm, first_sum, norm_gains[0], biases[3])
    norm_low = norm_one.astype(LOW)
    hidden_up = jnp.dot(norm_low, w_up, preferred_element_type=F32) + bias_up
    activated_full, gelu_pull = jax.vjp(exact_gelu, hidden_up)
    activated = activated_full.astype(LOW)
    branch = jnp.dot(activated, w_down, preferred_element_type=F32) + biases[4]
    out_full, second_pull = jax.vjp(layer_norm, norm_one + branch, norm_gains[1], biases[5])
    leading = out_full[:1].astype(LOW)
    pooled = jnp.tanh(jnp.dot(leading, w_pool, preferred_element_type=F32) + biases[6])
    pooled_low = pooled.astype(LOW)
    logits = against(pooled_low, w_class)
    onehot = (jnp.arange(CLASSES)[None, :] == label).astype(F32)
    losses = jax.nn.logsumexp(logits, axis=-1) - jnp.sum(onehot * logits, axis=-1)
    d_logits = jax.nn.softmax(logits, axis=-1) - onehot
    g_class = exact(d_logits.T, pooled_low.astype(F32))
    d_pre = exact(d_logits, w_class.astype(F32)) * (1.0 - pooled * pooled)
    d_leading = exact(d_pre, w_pool.astype(F32).T)
    d_out = cotangent.astype(F32) * slot_live[:, None]
    d_out = d_out.at[0].add(d_leading[0])
    d_h2, g_gain_two, g_shift_two = second_pull(d_out)
    d_branch = d_h2.astype(LOW)
    g_bias_down = jnp.sum(d_branch.astype(F32), axis=0)
    g_down_t = inner(d_branch, activated)
    d_activated = against(d_branch, w_down)
    d_up = gelu_pull(d_activated)[0].astype(LOW)
    g_bias_up = jnp.sum(d_up.astype(F32), axis=0)
    g_up_t = inner(d_up, norm_low)
    d_norm_one = d_h2 + against(d_up, w_up)
    d_h1, g_gain_one, g_shift_one = first_pull(d_norm_one)
    d_attn = d_h1.astype(LOW)
    g_bias_out = jnp.sum(d_attn.astype(F32), axis=0)
    g_out_t = inner(d_attn, context)
    d_context = against(d_attn, w_out).astype(LOW)
    d_packed = attention_back(packed, probs, d_context)
    g_qkv_t = inner(d_packed, tokens)
    column_sums = jnp.sum(d_packed.astype(F32), axis=0)
    grad_tokens = (d_h1 + against(d_packed, w_qkv)).astype(LOW)
    small = jnp.concatenate(
        [
            g_class,
            jnp.stack([column_sums[:D], column_sums[2 * D :], g_bias_out, g_shift_one, g_bias_down, g_shift_two]),
            jnp.stack([g_gain_one, g_gain_two]),
            g_bias_up.reshape(FF // D, D),
            d_pre,
        ]
    )
    lead = jnp.concatenate([leading.astype(F32), d_pre])
    down = owner_blocks(g_down_t, rest, FF)
    up = owner_blocks(g_up_t, rest, D)
    last = jnp.concatenate([owner_blocks(g_qkv_t, rest, D), owner_blocks(g_out_t, rest, D)], axis=4)
    half = up.shape[4] // 2
    parts = [
        down[..., : FF // 2], down[..., FF // 2 :],
        up[..., :half, :], up[..., half:, :],
        last[..., :half, :], last[..., half:, :],
    ]
    *sums, small, everyone = reduce_gradients(rest, parts, small, lead)
    g_down = jnp.concatenate(sums[0:2], axis=1).T
    g_up = jnp.concatenate(sums[2:4], axis=0).T
    g_last = jnp.concatenate(sums[4:6], axis=0).T
    own_qkv = 3 * D // (8 * rest)
    own = D // (8 * rest)
    everyone = everyone.reshape(8 * rest, 2, D)
    window = lax.dynamic_slice_in_dim(small, rank * own, own, axis=1)
    pre_window = lax.dynamic_slice_in_dim(everyone[:, 1], rank * own, own, axis=1)
    g_pool = lax.dot_general(
        everyone[:, 0], pre_window, (((0,), (0,)), ((), ())),
        precision=lax.Precision.HIGHEST, preferred_element_type=F32,
    )
    own_up = FF // (8 * rest)
    g_bias_up = lax.dynamic_slice_in_dim(small[11:15].reshape(FF), rank * own_up, own_up)
    return (
        out_full.astype(LOW),
        grad_tokens,
        losses,
        g_last[:, :own_qkv],
        g_last[:, own_qkv:],
        g_up,
        g_down,
        g_pool,
        window[:3],
        window[3:9],
        window[9:11],
        g_bias_up,
        window[15],
    )


def solution(mesh):
    return jax.shard_map(
        per_device,
        mesh=mesh,
        in_specs=(
            P(("batch", "head"), None),
            P(("batch", "head"), None),
            P("batch"),
            P("batch"),
            P(),
            P(),
            P(),
            P(),
            P(),
            P(),
            P(),
            P(),
            P(),
        ),
        out_specs=(
            P(("batch", "head"), None),
            P(("batch", "head"), None),
            P(("batch", "head")),
            P(None, ("batch", "head")),
            P(None, ("batch", "head")),
            P(None, ("batch", "head")),
            P(None, ("batch", "head")),
            P(None, ("batch", "head")),
            P(None, ("batch", "head")),
            P(None, ("batch", "head")),
            P(None, ("batch", "head")),
            P(("batch", "head")),
            P(("batch", "head")),
        ),
        check_vma=False,
    )
```

```python
import functools

import jax
import jax.numpy as jnp
from jax import lax
from jax.experimental import pallas as pl
from jax.experimental.pallas import tpu as pltpu
from jax.sharding import PartitionSpec as P

D = 768
HEADS = 12
HEAD_DIM = 64
FF = 3072
CLASSES = 3
SLOT = 512
MESH = pl.DeviceIdType.MESH
LOW = jnp.bfloat16
F32 = jnp.float32


def layer_norm(hidden, gain, shift):
    center = hidden - jnp.mean(hidden, axis=-1, keepdims=True)
    spread = jnp.mean(center * center, axis=-1, keepdims=True)
    return center * lax.rsqrt(spread + 1e-12) * gain + shift


def exact_gelu(hidden):
    return jax.nn.gelu(hidden, approximate=False)


def inner(left, right):
    return lax.dot_general(
        left, right, (((0,), (0,)), ((), ())), preferred_element_type=jnp.float32
    )


def against(left, right):
    return lax.dot_general(
        left, right, (((1,), (1,)), ((), ())), preferred_element_type=jnp.float32
    )


def exact(left, right):
    return jnp.dot(left, right, precision=lax.Precision.HIGHEST, preferred_element_type=jnp.float32)


class Place:
    def __init__(self, rest):
        batch = lax.axis_index("batch")
        head = lax.axis_index("head")
        self.rest = rest
        self.z = batch // 2
        self.y = lax.rem(batch, 2)
        self.x = head // 2
        self.c = lax.rem(head, 2)

    def device(self, z, y, x, c):
        return (z * 2 + y, x * 2 + c)

    def core_peer(self):
        return self.device(self.z, self.y, self.x, 1 - self.c)

    def x_peer(self):
        return self.device(self.z, self.y, 1 - self.x, self.c)

    def y_peer(self):
        return self.device(self.z, 1 - self.y, self.x, self.c)

    def z_at(self, offset):
        return lax.rem(self.z + offset, self.rest)

    def z_peer(self, offset):
        return self.device(self.z_at(offset), self.y, self.x, self.c)

    def barrier(self):
        sem = pltpu.get_barrier_semaphore()
        for peer in (self.core_peer(), self.x_peer(), self.y_peer()):
            pl.semaphore_signal(sem, inc=1, device_id=peer, device_id_type=MESH)
        for offset in range(1, self.rest):
            pl.semaphore_signal(sem, inc=1, device_id=self.z_peer(offset), device_id_type=MESH)
        pl.semaphore_wait(sem, 3 + self.rest - 1)


def remote(src, dst, send, recv, peer):
    return pltpu.make_async_remote_copy(
        src_ref=src, dst_ref=dst, send_sem=send, recv_sem=recv, device_id=peer, device_id_type=MESH
    )


class Reduce:
    def __init__(self, place, part, bufs, sems, x_first):
        self.place, self.part, self.x_first = place, part, x_first
        self.r1, self.r2, self.r3, self.r4 = bufs
        send, recv, zsend, zrecv = sems
        p = place
        if x_first:
            far, near, second_far, second_near = (1 - p.x, p.x, 1 - p.y, p.y)
            peers = (p.x_peer(), p.y_peer())
            src2 = self.r1.at[far]
        else:
            far, near, second_far, second_near = (1 - p.y, p.y, 1 - p.x, p.x)
            peers = (p.y_peer(), p.x_peer())
            src2 = self.r1.at[:, far]
        self.near, self.second_near = near, second_near
        self.copies = [
            remote(part.at[1 - p.c], self.r1, send.at[0], recv.at[0], p.core_peer()),
            remote(src2, self.r2, send.at[1], recv.at[1], peers[0]),
            remote(self.r2.at[second_far], self.r3, send.at[2], recv.at[2], peers[1]),
        ]
        self.last = [
            remote(self.r3.at[p.z_at(k)], self.r4.at[k - 1], zsend.at[k - 1], zrecv.at[k - 1], p.z_peer(k))
            for k in range(1, p.rest)
        ]

    def start(self):
        self.copies[0].start()

    def step1(self):
        p = self.place
        self.copies[0].wait()
        for i in range(2):
            for j in range(2):
                def add(k, carry, i=i, j=j):
                    self.r1[i, j, k] = self.r1[i, j, k] + self.part[p.c, i, j, k]
                    return carry
                lax.fori_loop(0, p.rest, add, 0)
        self.copies[1].start()

    def step2(self):
        p = self.place
        self.copies[1].wait()
        for i in range(2):
            def add(k, carry, i=i):
                own = self.r1[self.near, i, k] if self.x_first else self.r1[i, self.near, k]
                self.r2[i, k] = self.r2[i, k] + own
                return carry
            lax.fori_loop(0, p.rest, add, 0)
        self.copies[2].start()

    def step3(self):
        p = self.place
        self.copies[2].wait()

        def add(k, carry):
            self.r3[k] = self.r3[k] + self.r2[self.second_near, k]
            return carry
        lax.fori_loop(0, p.rest, add, 0)
        for copy in self.last:
            copy.start()

    def total(self):
        p = self.place
        for copy in self.last:
            copy.wait()
        result = self.r3[p.z].astype(F32)
        for k in range(1, p.rest):
            result = result + self.r4[k - 1].astype(F32)
        return result


def chunk_scratch(rest, rows, width):
    return [
        pltpu.VMEM((2, 2, rest, rows, width), LOW),
        pltpu.VMEM((2, rest, rows, width), LOW),
        pltpu.VMEM((rest, rows, width), LOW),
        pltpu.VMEM((rest - 1, rows, width), LOW),
        pltpu.SemaphoreType.DMA((3,)),
        pltpu.SemaphoreType.DMA((3,)),
        pltpu.SemaphoreType.DMA((rest - 1,)),
        pltpu.SemaphoreType.DMA((rest - 1,)),
    ]


class Small:
    def __init__(self, place, small, lead, everyone, bufs):
        got, gotz, send, recv, zsend, zrecv, gsend, grecv, gzsend, gzrecv = bufs
        p = place
        self.place, self.small, self.got, self.gotz = p, small, got, gotz
        self.lead, self.everyone = lead, everyone
        peers = (p.core_peer(), p.x_peer(), p.y_peer())
        blocks = (
            everyone.at[p.z, p.y, p.x, p.c], everyone.at[p.z, p.y, p.x], everyone.at[p.z, p.y],
        )
        self.sums = [remote(small, got.at[i], send.at[i], recv.at[i], peers[i]) for i in range(3)]
        self.sum_last = [
            remote(small, gotz.at[k - 1], zsend.at[k - 1], zrecv.at[k - 1], p.z_peer(k)) for k in range(1, p.rest)
        ]
        self.gathers = [remote(blocks[i], blocks[i], gsend.at[i], grecv.at[i], peers[i]) for i in range(3)]
        self.gather_last = [
            remote(everyone.at[p.z], everyone.at[p.z], gzsend.at[k - 1], gzrecv.at[k - 1], p.z_peer(k))
            for k in range(1, p.rest)
        ]

    def gather_start(self):
        p = self.place
        self.everyone[p.z, p.y, p.x, p.c] = self.lead[...]
        self.gathers[0].start()

    def gather_step(self, i):
        self.gathers[i].wait()
        if i < 2:
            self.gathers[i + 1].start()
        else:
            for copy in self.gather_last:
                copy.start()

    def gather_end(self):
        for copy in self.gather_last:
            copy.wait()

    def sum_start(self):
        self.sums[0].start()

    def sum_step(self, i):
        self.sums[i].wait()
        self.small[...] = self.small[...] + self.got[i]
        if i < 2:
            self.sums[i + 1].start()
        else:
            for copy in self.sum_last:
                copy.start()

    def sum_end(self):
        for copy in self.sum_last:
            copy.wait()
        total = self.small[...]
        for k in range(1, self.place.rest):
            total = total + self.gotz[k - 1]
        return total


def small_scratch(rest):
    return [
        pltpu.VMEM((3, 16, D), F32),
        pltpu.VMEM((rest - 1, 16, D), F32),
    ] + [pltpu.SemaphoreType.DMA((3,)), pltpu.SemaphoreType.DMA((3,)),
         pltpu.SemaphoreType.DMA((rest - 1,)), pltpu.SemaphoreType.DMA((rest - 1,))] * 2


def reduce_kernel(rest, n_chunks, *refs):
    parts = refs[:n_chunks]
    small_in, lead = refs[n_chunks : n_chunks + 2]
    outs = refs[n_chunks + 2 : 2 * n_chunks + 2]
    small_out, everyone = refs[2 * n_chunks + 2 : 2 * n_chunks + 4]
    scratch = refs[2 * n_chunks + 4 :]
    place = Place(rest)
    chunks = []
    for i in range(n_chunks):
        own = scratch[8 * i : 8 * i + 8]
        chunks.append(Reduce(place, parts[i], own[:4], own[4:], i % 2 == 0))
    rest_scratch = scratch[8 * n_chunks :]
    small = Small(place, rest_scratch[0], lead, everyone, rest_scratch[1:])
    rest_scratch[0][...] = small_in[...]
    place.barrier()
    small.gather_start()
    small.sum_start()
    steps = [[c.step1, c.step2, c.step3] for c in chunks]
    for chunk in chunks:
        chunk.start()
    for i in range(3):
        small.gather_step(i)
        small.sum_step(i)
    for phase in range(n_chunks + 4):
        for i in range(n_chunks):
            k = phase - i
            if i % 2 == 1:
                k = phase - i + 1
            if 0 <= k < 3:
                steps[i][k]()
            if k == 3:
                outs[i][...] = chunks[i].total()
    small.gather_end()
    small_out[...] = small.sum_end()


def reduce_gradients(rest, parts, small, lead):
    vmem = pl.BlockSpec(memory_space=pltpu.VMEM)
    scratch = []
    for part in parts:
        scratch += chunk_scratch(rest, *part.shape[4:])
    scratch += [pltpu.VMEM((16, D), F32)] + small_scratch(rest)
    outs = [jax.ShapeDtypeStruct(part.shape[4:], F32) for part in parts]
    outs += [
        jax.ShapeDtypeStruct((16, D), F32),
        jax.ShapeDtypeStruct((rest, 2, 2, 2, 2, D), F32),
    ]
    return pl.pallas_call(
        functools.partial(reduce_kernel, rest, len(parts)),
        out_shape=tuple(outs),
        in_specs=[vmem] * (len(parts) + 2),
        out_specs=tuple([vmem] * len(outs)),
        scratch_shapes=scratch,
        compiler_params=pltpu.CompilerParams(
            collective_id=0, has_side_effects=True, vmem_limit_bytes=60 << 20
        ),
    )(*parts, small, lead)


def owner_blocks(grad_t, rest, width):
    rows = grad_t.shape[0] // (8 * rest)
    view = grad_t.astype(LOW).reshape(rest, 2, 2, 2, rows, width)
    return view.transpose(3, 2, 1, 0, 4, 5)


def attention(packed, length):
    heads = packed.reshape(SLOT, 3, HEADS, HEAD_DIM)
    queries, keys_all, values = heads[:, 0], heads[:, 1], heads[:, 2]
    scores = jnp.einsum("qhd,khd->hqk", queries, keys_all, preferred_element_type=F32) * HEAD_DIM ** (-0.5)
    scores = jnp.where((jnp.arange(SLOT) < length)[None, None, :], scores, -1e30)
    row_max = jnp.max(scores, axis=-1, keepdims=True)
    weights = jnp.exp(scores - row_max)
    weights = weights / jnp.sum(weights, axis=-1, keepdims=True)
    low = weights.astype(LOW)
    context = jnp.einsum("hqk,khd->qhd", low, values, preferred_element_type=F32)
    return context.astype(LOW).reshape(SLOT, D), low


def attention_back(packed, low, d_context):
    heads = packed.reshape(SLOT, 3, HEADS, HEAD_DIM)
    queries, keys_all, values = heads[:, 0], heads[:, 1], heads[:, 2]
    d_heads = d_context.reshape(SLOT, HEADS, HEAD_DIM)
    weights = low.astype(F32)
    d_weights = jnp.einsum("qhd,khd->hqk", d_heads, values, preferred_element_type=F32)
    d_values = jnp.einsum("hqk,qhd->khd", low, d_heads, preferred_element_type=F32)
    row_dot = jnp.sum(weights * d_weights, axis=-1, keepdims=True)
    d_scores = (weights * (d_weights - row_dot)).astype(LOW)
    scale = HEAD_DIM ** (-0.5)
    d_queries = jnp.einsum("hqk,khd->qhd", d_scores, keys_all, preferred_element_type=F32) * scale
    d_keys = jnp.einsum("hqk,qhd->khd", d_scores, queries, preferred_element_type=F32) * scale
    return jnp.stack([d_queries, d_keys, d_values], axis=1).astype(LOW).reshape(SLOT, 3 * D)


def nn(left, right):
    return jnp.dot(left, right, preferred_element_type=F32)


def aligned(index, step):
    return pl.ds(pl.multiple_of(index * step, step), step)


def normalized(hidden):
    center = hidden - jnp.mean(hidden, axis=-1, keepdims=True)
    spread = jnp.mean(center * center, axis=-1, keepdims=True)
    scale = lax.rsqrt(spread + 1e-12)
    return center * scale, scale


def normalized_back(normed, scale, d_normed):
    first = jnp.mean(d_normed, axis=-1, keepdims=True)
    second = jnp.mean(d_normed * normed, axis=-1, keepdims=True)
    return scale * (d_normed - first - normed * second)


class Unit:
    def __init__(self, place, order, part, bufs, send, recv, put, after):
        p = self.place = place
        self.put, self.after = put, after
        self.at = 0
        self.legs = []
        bufs = list(bufs)
        count = part.shape[0] // 2
        held = bufs.pop(0)
        copy = remote(part.at[pl.ds((1 - p.c) * count, count)], held, send.at[0], recv.at[0], p.core_peer())
        self.legs.append((copy.start, self.pair_end(copy, held, part, p.c * count, count, False)))
        base = 0
        slot = 1
        for i, axis in enumerate(order):
            last = i == len(order) - 1
            if axis == "z":
                count = count // 4
                self.line(held, base, count, bufs.pop(0), bufs.pop(0), send, recv, slot, last)
                base = base + p.z * count
                slot += 3
            else:
                count = count // 2
                mine, peer = (p.x, p.x_peer()) if axis == "x" else (p.y, p.y_peer())
                got = bufs.pop(0)
                copy = remote(held.at[pl.ds(base + (1 - mine) * count, count)], got, send.at[slot], recv.at[slot], peer)
                self.legs.append((copy.start, self.pair_end(copy, got, held, base + mine * count, count, last)))
                held, base = got, 0
                slot += 1

    def pair_end(self, copy, got, own, start, count, last):
        def end():
            copy.wait()
            if last:
                self.put(got[0].astype(F32) + own[start].astype(F32))
            elif count >= 8:
                def add(i, carry):
                    got[pl.ds(i * 4, 4)] = got[pl.ds(i * 4, 4)] + own[pl.ds(start + i * 4, 4)]
                    return carry
                lax.fori_loop(0, count // 4, add, 0)
            else:
                got[...] = got[...] + own[pl.ds(start, count)]
        return end

    def line(self, held, base, n, wide, single, send, recv, slot, last):
        p = self.place
        z = p.z
        outer = jnp.logical_or(z == 0, z == 3)
        inner = jnp.logical_not(outer)
        low = z < 2
        near = jnp.where(low, 1 - z, 5 - z)
        far = jnp.where(low, z + 2, z - 2)
        middle = 3 - z

        def at(block, count=n):
            return held.at[pl.ds(base + block * n, count)]

        def device(block):
            return p.device(block, p.y, p.x, p.c)

        outward = remote(at(jnp.where(z == 0, 1, 0), 3 * n), wide, send.at[slot], recv.at[slot], device(near))
        back = remote(at(near), wide.at[0:n], send.at[slot], recv.at[slot], device(near))
        across = remote(at(middle), single, send.at[slot + 1], recv.at[slot + 1], device(middle))
        beyond = remote(at(far), wide.at[n : 2 * n], send.at[slot + 2], recv.at[slot + 2], device(far))

        def begin_first():
            @pl.when(outer)
            def _():
                outward.start()

            @pl.when(inner)
            def _():
                back.start()

        def end_first():
            @pl.when(outer)
            def _():
                outward.wait_send()
                back.wait_recv()

            @pl.when(inner)
            def _():
                back.wait_send()
                outward.wait_recv()
                start = base + jnp.where(z == 1, n, 0)
                held[pl.ds(start, 3 * n)] = held[pl.ds(start, 3 * n)] + wide[...]

        def begin_second():
            @pl.when(inner)
            def _():
                across.start()
                beyond.start()

        def end_second():
            @pl.when(outer)
            def _():
                beyond.wait_recv()
                total = held[pl.ds(base + z * n, n)].astype(F32) + wide[0:n].astype(F32) + wide[n : 2 * n].astype(F32)
                if last:
                    self.put(total[0])
                else:
                    held[pl.ds(base + z * n, n)] = total.astype(LOW)

            @pl.when(inner)
            def _():
                across.wait()
                beyond.wait_send()
                total = held[pl.ds(base + z * n, n)].astype(F32) + single[...].astype(F32)
                if last:
                    self.put(total[0])
                else:
                    held[pl.ds(base + z * n, n)] = total.astype(LOW)

        self.legs.append((begin_first, end_first))
        self.legs.append((begin_second, end_second))

    def step(self):
        if self.at > 0:
            self.legs[self.at - 1][1]()
        if self.at < len(self.legs):
            self.legs[self.at][0]()
        else:
            self.after()
        self.at += 1


class Gather:
    def __init__(self, place, lead, everyone, send, recv, after):
        self.after = after
        p = place
        peers = (p.core_peer(), p.x_peer(), p.y_peer())
        own = everyone.at[p.z, p.y, p.x, p.c]
        blocks = (own, everyone.at[p.z, p.y, p.x], everyone.at[p.z, p.y])
        groups = [[remote(blocks[i], blocks[i], send.at[i], recv.at[i], peers[i])] for i in range(3)]
        groups.append([
            remote(everyone.at[p.z], everyone.at[p.z], send.at[k + 2], recv.at[k + 2], p.z_peer(k)) for k in range(1, p.rest)
        ])
        self.groups, self.at, self.own, self.lead = groups, 0, own, lead

    def step(self):
        if self.at == 0:
            self.own[...] = self.lead[...]
        else:
            for copy in self.groups[self.at - 1]:
                copy.wait()
        if self.at < 4:
            for copy in self.groups[self.at]:
                copy.start()
        else:
            self.after()
        self.at += 1


class Total:
    def __init__(self, place, small, low, got, send, recv, put):
        p = place
        peers = (p.core_peer(), p.x_peer(), p.y_peer())
        groups = [[remote(low, got.at[i], send.at[i], recv.at[i], peers[i])] for i in range(3)]
        groups.append([
            remote(low, got.at[k + 2], send.at[k + 2], recv.at[k + 2], p.z_peer(k)) for k in range(1, p.rest)
        ])
        self.groups, self.at, self.small, self.low, self.got, self.put = groups, 0, small, low, got, put

    def step(self):
        total = self.small[...]
        if self.at > 0:
            first = self.at - 1
            for i, copy in enumerate(self.groups[first]):
                copy.wait()
                total = total + self.got[first + i].astype(F32)
        if self.at < 4:
            self.small[...] = total
            self.low[...] = total.astype(LOW)
            for copy in self.groups[self.at]:
                copy.start()
        else:
            self.put(total)
        self.at += 1


def block_index(order, rest, z, y, x, c):
    sizes = {"x": 2, "y": 2, "z": rest}
    at = {"x": x, "y": y, "z": z}
    index = c
    for axis in order:
        index = index * sizes[axis] + at[axis]
    return index


def owners(rest):
    return [(z, y, x, c) for z in range(rest) for y in range(2) for x in range(2) for c in range(2)]


def unit_scratch(order, rows, width):
    blocks = 16
    bufs = [pltpu.VMEM((blocks, rows, width), LOW)]
    for axis in order:
        if axis == "z":
            blocks = blocks // 4
            bufs += [pltpu.VMEM((3 * blocks, rows, width), LOW), pltpu.VMEM((blocks, rows, width), LOW)]
        else:
            blocks = blocks // 2
            bufs.append(pltpu.VMEM((blocks, rows, width), LOW))
    return bufs + [pltpu.SemaphoreType.DMA((6,)), pltpu.SemaphoreType.DMA((6,))]


UNITS = (("down", 4, 1), ("up", 4, 1), ("out", 1, 1), ("qkv", 3, 3))
ORDERS = (
    "zxy", "xyz", "yzx", "xyz", "yxz", "zyx", "xzy", "yxz", "xyz", "yxz", "xyz", "xzy", "yxz", "yxz", "yxz", "yxz", "xyz", "xyz",
)
PLAN = (
    (),
    (),
    (),
    (),
    (),
    (),
    (),
    (),
    (0, 1, 2,),
    (3,),
    (),
    (1, 2,),
    (4,),
    (6, 5, 0,),
    (7, 8,),
    (),
    (6,),
    (4, 3, 2,),
    (8, 1, 7, 5, 3, 18, 9, 11, 4, 14,),
    (16, 17, 7, 10, 18, 15, 1, 6, 11, 13, 9, 14, 16, 8, 4, 12,),
    (),
    (15, 17, 18, 19, 11, 1, 3, 10, 16, 13, 5, 9, 7, 14, 6, 12, 8, 15, 0, 19, 17, 2, 13, 10, 9, 3, 11, 14, 5, 12, 18, 15, 16, 19, 17, 0, 13, 7, 11, 10, 2, 5, 12, 15, 8, 14, 9, 6, 16, 4, 17, 0, 13, 10, 19, 12,),
)
N_IN = 13
N_OUT = 9


def layer_kernel(rest, *refs):
    (lengths, labels, biases_h, gains_h, bias_up_h, w_class_h, tokens_h, cot_h, wqkv_h, wout_h, wup_h, wdown_h, wpool_h) = refs[:N_IN]
    out_h, gtok_h, down_out, up_out, qkv_out, attn_out, small_out, everyone_out, loss_out = refs[N_IN : N_IN + N_OUT]
    scratch = list(refs[N_IN + N_OUT :])
    (
        tokens, w_qkv, w_out, w_up, w_down, packed, weights, inverse, context, normed_one, norm_low,
        activated, slope, d_hidden, d_low, d_packed, part0, part1, part2, part3, scale_one, small, lead, in_sem, out_sem,
    ) = scratch[:25]
    parts = [part0, part1, part2, part3]
    cot = d_low
    d_context = norm_low
    wide = SLOT
    pool_wide = d_packed.at[0:D]
    pool_rest = d_packed.at[D : 2 * D, 0 : D - wide]
    out_wide = d_packed.at[2 * D : 2 * D + SLOT]
    out_rest = d_packed.at[D : D + SLOT, wide // 2 : wide // 2 + D - wide]
    place = Place(rest)
    small_bufs = scratch[25:31]
    biases, gains, bias_up, w_class = scratch[31:35]
    down_mid, up_mid, qkv_mid, attn_mid, small_mid, everyone, loss_mid = scratch[35:42]
    little_sem, done_sem = scratch[42:44]
    unit_bufs = scratch[44:]
    little = [
        pltpu.make_async_copy(src, dst, little_sem.at[i])
        for i, (src, dst) in enumerate([(biases_h, biases), (gains_h, gains), (bias_up_h, bias_up), (w_class_h, w_class)])
    ]
    head_rank = lax.axis_index("head")
    length = lengths[head_rank]
    label = labels[head_rank]
    loads = [
        pltpu.make_async_copy(src, dst, in_sem.at[i])
        for i, (src, dst) in enumerate(
            [(tokens_h, tokens), (wqkv_h.at[:, 0:D], w_qkv.at[:, 0:D]), (wqkv_h.at[:, D : 2 * D], w_qkv.at[:, D : 2 * D]),
             (wqkv_h.at[:, 2 * D :], w_qkv.at[:, 2 * D :]), (wout_h, w_out), (wup_h, w_up),
             (wdown_h, w_down), (cot_h, cot), (wpool_h.at[:, 0:wide], pool_wide), (wpool_h.at[:, wide:D], pool_rest)]
        )
    ]
    for load in loads[:4] + little:
        load.start()
    sem = pltpu.get_barrier_semaphore()
    for peer in (place.core_peer(), place.x_peer(), place.y_peer()):
        pl.semaphore_signal(sem, inc=1, device_id=peer, device_id_type=MESH)
    for offset in range(1, rest):
        pl.semaphore_signal(sem, inc=1, device_id=place.z_peer(offset), device_id_type=MESH)

    height = D // 32
    order_of = owners(rest)

    targets = {"down": (down_mid, down_out), "up": (up_mid, up_out), "out": (attn_mid, attn_out), "qkv": (qkv_mid, qkv_out)}
    leaving = []

    def leave(src, dst, i):
        copy = pltpu.make_async_copy(src, dst, done_sem.at[i])
        copy.start()
        leaving.append(copy)
    base_part = {"down": 0, "up": 0, "out": 0, "qkv": 1}

    def put_into(kind, i, columns, n):
        if kind == "down":
            place_of = (slice(None), slice(i * D + columns.start, i * D + columns.stop))
        else:
            place_of = (slice(i * height, (i + 1) * height), columns)
        mid, out = targets[kind]

        def put(total):
            mid[place_of] = total

        return put, lambda: leave(mid.at[place_of], out.at[place_of], n)

    units = []
    number = {}
    at = 0
    for kind, count, cut in UNITS:
        for i in range(count):
            for j in range(cut):
                columns = slice(j * D // cut, (j + 1) * D // cut)
                order = ORDERS[len(units)]
                size = len(unit_scratch(order, height, D // cut))
                own = unit_bufs[at : at + size]
                at += size
                part = parts[base_part[kind] + i]
                if cut > 1:
                    part = part.at[:, :, columns]
                number[kind, i, j] = len(units)
                put, after = put_into(kind, i, columns, len(units))
                units.append(Unit(place, order, part, own[:-2], own[-2], own[-1], put, after))
    def fill(kind, i, owner, columns, value):
        cut = {name: c for name, _, c in UNITS}[kind]
        width = D // cut
        part = parts[base_part[kind] + i]
        for j in range(cut):
            first, last = max(columns.start, j * width), min(columns.stop, (j + 1) * width)
            if first < last:
                index = block_index(ORDERS[number[kind, i, j]], rest, *owner)
                part[index, :, first:last] = value[:, first - columns.start : last - columns.start].astype(LOW)

    def go(kind, i, j):
        units[number[kind, i, j]].step()

    low_small, got_small, *small_sems = small_bufs
    gather, totals = len(units), len(units) + 1

    def put_small(total):
        small_mid[...] = total
        leave(small_mid, small_out, totals)

    units.append(Gather(place, lead, everyone, *small_sems[:2], lambda: leave(everyone, everyone_out, gather)))
    units.append(Total(place, small, low_small, got_small, *small_sems[2:], put_small))
    plan = list(PLAN)

    def steps():
        for i in plan.pop(0):
            units[i].step()

    loads[0].wait()
    for load in little:
        load.wait()
    ones = jnp.ones((8, SLOT), LOW)
    for part in range(3):
        columns = slice(part * D, part * D + D)
        loads[part + 1].wait()
        if part == 0:
            for load in loads[4:]:
                load.start()
        result = nn(tokens[...], w_qkv[:, columns])
        if part == 0:
            result = (result + biases[0:1]).astype(LOW) * jnp.asarray(HEAD_DIM ** (-0.5), LOW)
        elif part == 2:
            result = (result + biases[1:2]).astype(LOW)
        else:
            result = result.astype(LOW)
        packed[:, columns] = result

    key_live = lax.broadcasted_iota(jnp.int32, (SLOT, 1), 0) < length
    lane = lax.broadcasted_iota(jnp.int32, (1, 2 * HEAD_DIM), 1)
    lane_of = [lane < HEAD_DIM, lane >= HEAD_DIM]
    spare = [lane == HEAD_DIM, lane == 0]
    dead = [jnp.where(jnp.logical_and(spare[k], jnp.logical_not(key_live)), -1e30, 0.0).astype(LOW) for k in range(2)]

    def attend(pair):
        at = pair * 2 * HEAD_DIM
        queries = packed[:, at : at + 2 * HEAD_DIM]
        keys_all = packed[:, at + D : at + D + 2 * HEAD_DIM]
        values_t = packed[:, at + 2 * D : at + 2 * D + 2 * HEAD_DIM].T
        got = []
        for k in range(2):
            own_keys = jnp.where(lane_of[k], keys_all, dead[k])
            scores = against(own_keys, jnp.where(lane_of[k], queries, jnp.ones_like(queries)))
            powers = jnp.exp(scores - jnp.max(scores, axis=0, keepdims=True))
            inv = 1.0 / jnp.sum(powers, axis=0, keepdims=True)
            powers = powers.astype(LOW)
            weights[2 * pair + k] = powers
            inverse[pair, k : k + 1] = inv
            got.append(nn(values_t[k * HEAD_DIM : (k + 1) * HEAD_DIM], powers) * inv)
        context[:, at : at + 2 * HEAD_DIM] = jnp.concatenate(got, axis=0).T.astype(LOW)

    for pair in range(HEADS // 2):
        attend(pair)

    blocks = [slice(0, SLOT // 2), slice(SLOT // 2, SLOT)]
    loads[4].wait()
    for rows in blocks:
        hidden = nn(context[rows], w_out[...]) + biases[2:3] + tokens[rows].astype(F32)
        normed, scale = normalized(hidden)
        normed_one[rows] = normed
        scale_one[rows] = scale
        norm_low[rows] = (normed * gains[0:1] + biases[3:4]).astype(LOW)

    loads[5].wait()

    def feed(tile):
        columns = slice(tile * D, (tile + 1) * D)
        hidden = nn(norm_low[...], w_up[:, columns]) + bias_up[0:1, columns]
        share = 0.5 + 0.5 * lax.erf(hidden * 0.7071067811865476)
        activated[:, columns] = (hidden * share).astype(LOW)
        slope[:, columns] = (share + hidden * (jnp.exp(-0.5 * hidden * hidden) * 0.3989422804014327)).astype(LOW)

    for tile in range(FF // D):
        feed(tile)

    for i in (6, 7, 8, 9):
        loads[i].wait()
    row = lax.broadcasted_iota(jnp.int32, (SLOT // 2, 1), 0)
    kept = []
    for k, rows in enumerate(blocks):
        hidden = nn(activated[rows], w_down[...]) + biases[4:5] + (normed_one[rows] * gains[0:1] + biases[3:4])
        normed, scale = normalized(hidden)
        result = normed * gains[1:2] + biases[5:6]
        low = result.astype(LOW)
        out_wide[rows] = low[:, 0:wide]
        out_rest[rows] = low[:, wide:D]
        d_hidden[rows] = normed
        kept.append(scale)
        if k == 0:
            leading = low[0:8]
    out_copies = [
        pltpu.make_async_copy(out_wide, out_h.at[:, 0:wide], out_sem.at[0]),
        pltpu.make_async_copy(out_rest, out_h.at[:, wide:D], out_sem.at[2]),
    ]
    for copy in out_copies:
        copy.start()

    pooled = jnp.concatenate([nn(leading, pool_wide[...]), nn(leading, pool_rest[...])], axis=1)
    pooled = jnp.tanh(pooled + biases[6:7])[0:1]
    pooled_low = pooled.astype(LOW).astype(F32)
    classes = w_class[...].astype(F32)
    logits = jnp.sum(pooled_low * classes, axis=-1, keepdims=True)
    top = jnp.max(logits, axis=0, keepdims=True)
    powers = jnp.exp(logits - top)
    total = jnp.sum(powers, axis=0, keepdims=True)
    onehot = (lax.broadcasted_iota(jnp.int32, (CLASSES, 1), 0) == label).astype(F32)
    loss_mid[...] = jnp.broadcast_to(
        jnp.log(total) + top - jnp.sum(onehot * logits, axis=0, keepdims=True), loss_mid.shape
    )
    leave(loss_mid, loss_out, totals + 1)
    d_logits = powers / total - onehot
    d_pre = jnp.sum(d_logits * classes, axis=0, keepdims=True) * (1.0 - pooled * pooled)
    high = d_pre.astype(LOW).astype(F32)
    middle = (d_pre - high).astype(LOW).astype(F32)
    low = d_pre - high - middle
    eight = lax.broadcasted_iota(jnp.int32, (8, 1), 0)
    split = jnp.where(eight == 0, high, jnp.where(eight == 1, middle, jnp.where(eight == 2, low, 0.0)))
    split = split.astype(LOW)
    d_leading = against(split[:, 0:wide], pool_wide[...]) + against(split[:, wide:D], pool_rest[...])
    d_leading = jnp.sum(d_leading, axis=0, keepdims=True)
    small[0:3] = d_logits * pooled_low
    small[15:16] = d_pre
    lead[0:1] = leading[0:1]
    lead[1:2] = d_pre.astype(LOW)

    shift_two = jnp.zeros((1, D), F32)
    gain_two = jnp.zeros((1, D), F32)
    bias_down = jnp.zeros((1, D), F32)
    for k in (1, 0):
        rows = blocks[k]
        normed, scale = d_hidden[rows], kept[k]
        d_out = jnp.where(row + k * (SLOT // 2) < length, cot[rows].astype(F32), 0.0)
        if k == 0:
            d_out = d_out + jnp.where(row == 0, d_leading, 0.0)
        shift_two = shift_two + jnp.sum(d_out, axis=0, keepdims=True)
        gain_two = gain_two + jnp.sum(d_out * normed, axis=0, keepdims=True)
        d_two = normalized_back(normed, scale, d_out * gains[1:2])
        d_hidden[rows] = d_two
        d_two = d_two.astype(LOW)
        d_low[rows] = d_two
        bias_down = bias_down + jnp.sum(d_two.astype(F32), axis=0, keepdims=True)
    small[8:9] = shift_two
    small[10:11] = gain_two
    small[7:8] = bias_down

    rows = height
    pl.semaphore_wait(sem, 3 + rest - 1)
    units[gather].step()
    d_branch_t = d_low[...].T
    halves = (slice(0, D // 2), slice(D // 2, D))
    everything = slice(0, D)
    cuts = {name: cut for name, _, cut in UNITS}
    for i in range(4):
        for j, columns in enumerate(halves):
            result = nn(d_branch_t, activated[:, i * D + columns.start : i * D + columns.stop])
            for d, owner in enumerate(order_of):
                fill("down", i, owner, columns, result[d * rows : (d + 1) * rows])
            if cuts["down"] == 2:
                go("down", i, j)
            elif j == 1:
                go("down", i, 0)
            steps()

    for tile in range(FF // D):
        columns = slice(tile * D, (tile + 1) * D)
        d_up = (against(d_low[...], w_down[columns]) * slope[:, columns].astype(F32)).astype(LOW)
        slope[:, columns] = d_up
        small[11 + tile : 12 + tile] = jnp.sum(d_up.astype(F32), axis=0, keepdims=True)
        if tile % 2 == 1:
            steps()
    d_up = slope

    def up_gradient(tile, carry):
        for columns in halves:
            result = inner(d_up[:, aligned(tile, D)], norm_low[:, columns])
            for d in range(8):
                for i in range(4):
                    first = (d * 4 + i) * rows
                    fill("up", i, (tile, *order_of[d][1:]), columns, result[first : first + rows])
        return carry

    lax.fori_loop(0, FF // D, up_gradient, 0)
    for i in range(4):
        for j in range(cuts["up"]):
            go("up", i, j)
    steps()

    shift_one = jnp.zeros((1, D), F32)
    gain_one = jnp.zeros((1, D), F32)
    bias_attn = jnp.zeros((1, D), F32)
    for block in blocks:
        d_norm = d_hidden[block] + against(d_up[block], w_up[...])
        normed = normed_one[block]
        shift_one = shift_one + jnp.sum(d_norm, axis=0, keepdims=True)
        gain_one = gain_one + jnp.sum(d_norm * normed, axis=0, keepdims=True)
        d_one = normalized_back(normed, scale_one[block], d_norm * gains[0:1])
        d_hidden[block] = d_one
        d_one = d_one.astype(LOW)
        d_low[block] = d_one
        bias_attn = bias_attn + jnp.sum(d_one.astype(F32), axis=0, keepdims=True)
        steps()
    small[6:7] = shift_one
    small[9:10] = gain_one
    small[5:6] = bias_attn

    result = inner(d_low[...], context[...])
    for d, owner in enumerate(order_of):
        fill("out", 0, owner, everything, result[d * rows : (d + 1) * rows])
    for j in range(cuts["out"]):
        go("out", 0, j)
    d_context[...] = against(d_low[...], w_out[...]).astype(LOW)
    steps()

    def attend_back(pair, carry):
        at = pl.multiple_of(pair * 2 * HEAD_DIM, 2 * HEAD_DIM)
        queries_t = packed[:, pl.ds(at, 2 * HEAD_DIM)].T
        keys_t = packed[:, pl.ds(at + D, 2 * HEAD_DIM)].T
        values = packed[:, pl.ds(at + 2 * D, 2 * HEAD_DIM)]
        context_t = context[:, pl.ds(at, 2 * HEAD_DIM)].T
        d_context_t = d_context[:, pl.ds(at, 2 * HEAD_DIM)].T
        scaled = []
        dots = []
        for k in range(2):
            own_rows = slice(k * HEAD_DIM, (k + 1) * HEAD_DIM)
            own = d_context_t[own_rows].astype(F32) * inverse[pair, k : k + 1]
            dots.append(jnp.sum(own * context_t[own_rows].astype(F32), axis=0, keepdims=True))
            scaled.append(own.astype(LOW))
        both = jnp.concatenate(scaled, axis=0).T
        for k in range(2):
            own_rows = slice(k * HEAD_DIM, (k + 1) * HEAD_DIM)
            own_values = jnp.where(lane_of[k], values, jnp.zeros_like(values))
            powers = weights[2 * pair + k]
            d_scores = (powers.astype(F32) * (against(own_values, both) - dots[k])).astype(LOW)
            put = pl.multiple_of(at + k * HEAD_DIM, HEAD_DIM)
            d_packed[pl.ds(put, HEAD_DIM)] = (nn(keys_t[own_rows], d_scores) * HEAD_DIM ** (-0.5)).astype(LOW)
            d_packed[pl.ds(put + D, HEAD_DIM)] = against(queries_t[own_rows], d_scores).astype(LOW)
            d_packed[pl.ds(put + 2 * D, HEAD_DIM)] = against(scaled[k], powers).astype(LOW)
        return carry

    for copy in out_copies:
        copy.wait()
    for part in range(3):
        lax.fori_loop(2 * part, 2 * part + 2, attend_back, 0)
        steps()

    small[3:4] = against(ones, d_packed[0:D])[0:1]
    small[4:5] = against(ones, d_packed[2 * D : 3 * D])[0:1]
    units[totals].step()
    steps()
    def qkv_gradient(tile, carry):
        result = nn(d_packed[aligned(tile, 24 * rows)], tokens[...])
        for d in range(8):
            for i in range(3):
                first = (d * 3 + i) * rows
                fill("qkv", i, (tile, *order_of[d][1:]), everything, result[first : first + rows])
        return carry

    lax.fori_loop(0, rest, qkv_gradient, 0)
    for i in range(3):
        for j in range(cuts["qkv"]):
            go("qkv", i, j)
    steps()

    for block in blocks:
        d_tokens = nn(w_qkv[...], d_packed[:, block]).T + d_hidden[block]
        d_low[block] = d_tokens.astype(LOW)
        steps()
    token_copy = pltpu.make_async_copy(d_low, gtok_h, out_sem.at[1])
    token_copy.start()
    steps()
    token_copy.wait()
    for copy in leaving:
        copy.wait()


def layer(rest, tokens, cotangent, lengths, labels, w_qkv, w_out, w_up, w_down, w_pool, w_class, biases, norm_gains, bias_up):
    rows = D // 32
    vmem = pl.BlockSpec(memory_space=pltpu.VMEM)
    smem = pl.BlockSpec(memory_space=pltpu.SMEM)
    anywhere = pl.BlockSpec(memory_space=pl.ANY)
    dma = pltpu.SemaphoreType.DMA
    scratch = [
        pltpu.VMEM((SLOT, D), LOW),
        pltpu.VMEM((D, 3 * D), LOW),
        pltpu.VMEM((D, D), LOW),
        pltpu.VMEM((D, FF), LOW),
        pltpu.VMEM((FF, D), LOW),
        pltpu.VMEM((SLOT, 3 * D), LOW),
        pltpu.VMEM((HEADS, SLOT, SLOT), LOW),
        pltpu.VMEM((HEADS // 2, 2, SLOT), F32),
        pltpu.VMEM((SLOT, D), LOW),
        pltpu.VMEM((SLOT, D), F32),
        pltpu.VMEM((SLOT, D), LOW),
        pltpu.VMEM((SLOT, FF), LOW),
        pltpu.VMEM((SLOT, FF), LOW),
        pltpu.VMEM((SLOT, D), F32),
        pltpu.VMEM((SLOT, D), LOW),
        pltpu.VMEM((3 * D, SLOT), LOW),
    ] + [pltpu.VMEM((32, rows, D), LOW)] * 4 + [
        pltpu.VMEM((SLOT, 1), F32),
        pltpu.VMEM((16, D), F32),
        pltpu.VMEM((2, D), LOW),
        dma((10,)),
        dma((3,)),
        pltpu.VMEM((16, D), LOW),
        pltpu.VMEM((6, 16, D), LOW),
        dma((6,)),
        dma((6,)),
        dma((6,)),
        dma((6,)),
        pltpu.VMEM(biases.shape, F32),
        pltpu.VMEM(norm_gains.shape, F32),
        pltpu.VMEM((1, FF), F32),
        pltpu.VMEM(w_class.shape, LOW),
    ]
    outs = [jax.ShapeDtypeStruct((SLOT, D), LOW)] * 2 + [
        jax.ShapeDtypeStruct((rows, FF), F32),
        jax.ShapeDtypeStruct((4 * rows, D), F32),
        jax.ShapeDtypeStruct((3 * rows, D), F32),
        jax.ShapeDtypeStruct((rows, D), F32),
        jax.ShapeDtypeStruct((16, D), F32),
        jax.ShapeDtypeStruct((rest, 2, 2, 2, 2, D), LOW),
        jax.ShapeDtypeStruct((1, 128), F32),
    ]
    scratch += [pltpu.VMEM(o.shape, o.dtype) for o in outs[2:]]
    scratch += [dma((4,)), dma((len(ORDERS) + 3,))]
    orders = list(ORDERS)
    for _, count, cut in UNITS:
        for _ in range(count * cut):
            scratch += unit_scratch(orders.pop(0), rows, D // cut)
    return pl.pallas_call(
        functools.partial(layer_kernel, rest),
        out_shape=tuple(outs),
        in_specs=[smem, smem] + [anywhere] * 11,
        out_specs=tuple([anywhere] * 9),
        scratch_shapes=scratch,
        compiler_params=pltpu.CompilerParams(
            collective_id=0, has_side_effects=True, vmem_limit_bytes=61 << 20
        ),
    )(lengths, labels, biases, norm_gains, bias_up.reshape(1, FF), w_class, tokens, cotangent, w_qkv, w_out, w_up, w_down, w_pool)


def finish_kernel(rest, *refs):
    moved, tables = refs[:6], refs[6:9]
    targets, rest_out = refs[9:15], refs[15:22]
    stages, tables_in, results = refs[22:28], refs[28:31], refs[31:38]
    sem_in, sem_out = refs[38:]
    arrive = [pltpu.make_async_copy(src, mid, sem_in.at[i]) for i, (src, mid) in enumerate(zip(tables + moved, tables_in + stages))]
    leave = [pltpu.make_async_copy(mid, dst, sem_out.at[i]) for i, (mid, dst) in enumerate(zip(stages + results, targets + rest_out))]
    for copy in arrive:
        copy.start()
    small, everyone, loss = tables_in
    losses, g_pool, g_class, g_biases, g_gains, g_bias_up, g_pool_bias = results
    rank = lax.axis_index("batch") * 4 + lax.axis_index("head")
    own = D // (8 * rest)
    own_up = 4 * own
    for before, after in zip(arrive[3:], leave):
        before.wait()
        after.start()
    for copy in arrive[:3]:
        copy.wait()
    losses[...] = loss[0:1, 0:1]

    def window(array, start, size):
        at = lax.broadcasted_iota(jnp.int32, (D, size), 0)
        want = lax.broadcasted_iota(jnp.int32, (D, size), 1)
        return exact(array, (at == want + start).astype(F32))

    leading = everyone[:, 0].astype(F32)
    d_pre = everyone[:, 1].astype(F32)
    both = window(jnp.concatenate([small[...], d_pre], axis=0), rank * own, own)
    picked = both[0:16]
    g_class[...] = picked[0:3]
    g_biases[...] = picked[3:9]
    g_gains[...] = picked[9:11]
    g_pool_bias[...] = picked[15:16]
    flat = rank * own_up
    part = flat // D
    pick = lax.broadcasted_iota(jnp.int32, (4, 1), 0) == part
    chosen = jnp.sum(jnp.where(pick, small[11:15], 0.0), axis=0, keepdims=True)
    g_bias_up[...] = window(jnp.broadcast_to(chosen, (8, D)), flat - part * D, own_up)[0:1]
    g_pool[...] = lax.dot_general(
        both[16:], leading, (((0,), (0,)), ((), ())), precision=lax.Precision.HIGHEST, preferred_element_type=F32
    )
    for copy in leave[6:]:
        copy.start()
    for copy in leave:
        copy.wait()


def finish(rest, results):
    own = D // (8 * rest)
    anywhere = pl.BlockSpec(memory_space=pl.ANY)
    shape = lambda *s: jax.ShapeDtypeStruct(s, F32)
    results = list(results)
    results[7] = results[7].reshape(8 * rest, 2, D)
    outs = [jax.ShapeDtypeStruct((SLOT, D), LOW)] * 2 + [
        shape(own, FF), shape(4 * own, D), shape(3 * own, D), shape(own, D),
        shape(1, 1), shape(own, D), shape(3, own), shape(6, own), shape(2, own), shape(1, 4 * own), shape(1, own),
    ]
    held = lambda arrays: [pltpu.VMEM(o.shape, o.dtype) for o in arrays]
    (out, gtok, down, up, qkv, attn, losses, pool, g_class, g_biases, g_gains, g_bias_up, g_pool_bias) = pl.pallas_call(
        functools.partial(finish_kernel, rest),
        out_shape=tuple(outs),
        in_specs=[anywhere] * 9,
        out_specs=tuple([anywhere] * 13),
        scratch_shapes=held(outs[:6]) + held(results[6:]) + held(outs[6:])
        + [pltpu.SemaphoreType.DMA((9,)), pltpu.SemaphoreType.DMA((13,))],
        compiler_params=pltpu.CompilerParams(vmem_limit_bytes=60 << 20),
    )(*results)
    return (
        out, gtok, losses.reshape(-1), qkv.T, attn.T, up.T, down.T, pool.T, g_class, g_biases, g_gains,
        g_bias_up.reshape(-1), g_pool_bias.reshape(-1),
    )


def per_device(
    tokens,
    cotangent,
    lengths,
    labels,
    w_qkv,
    w_out,
    w_up,
    w_down,
    w_pool,
    w_class,
    biases,
    norm_gains,
    bias_up,
):
    rest = lax.axis_size("batch") // 2
    if rest == 4:
        return finish(rest, layer(
            rest, tokens, cotangent, lengths, labels, w_qkv, w_out, w_up, w_down, w_pool, w_class, biases, norm_gains,
            bias_up,
        ))
    head_rank = lax.axis_index("head")
    rank = lax.axis_index("batch") * 4 + head_rank
    length = lax.dynamic_index_in_dim(lengths, head_rank, keepdims=False)
    label = lax.dynamic_index_in_dim(labels, head_rank, keepdims=False)
    slot_live = (jnp.arange(SLOT) < length).astype(F32)
    zeros_key = jnp.zeros((D,), F32)
    packed = jnp.dot(tokens, w_qkv, preferred_element_type=F32) + jnp.concatenate(
        [biases[0], zeros_key, biases[1]]
    )
    packed = packed.astype(LOW)
    context, probs = attention(packed, length)
    attn = jnp.dot(context, w_out, preferred_element_type=F32) + biases[2]
    first_sum = tokens.astype(F32) + attn
    norm_one, first_pull = jax.vjp(layer_norm, first_sum, norm_gains[0], biases[3])
    norm_low = norm_one.astype(LOW)
    hidden_up = jnp.dot(norm_low, w_up, preferred_element_type=F32) + bias_up
    activated_full, gelu_pull = jax.vjp(exact_gelu, hidden_up)
    activated = activated_full.astype(LOW)
    branch = jnp.dot(activated, w_down, preferred_element_type=F32) + biases[4]
    out_full, second_pull = jax.vjp(layer_norm, norm_one + branch, norm_gains[1], biases[5])
    leading = out_full[:1].astype(LOW)
    pooled = jnp.tanh(jnp.dot(leading, w_pool, preferred_element_type=F32) + biases[6])
    pooled_low = pooled.astype(LOW)
    logits = against(pooled_low, w_class)
    onehot = (jnp.arange(CLASSES)[None, :] == label).astype(F32)
    losses = jax.nn.logsumexp(logits, axis=-1) - jnp.sum(onehot * logits, axis=-1)
    d_logits = jax.nn.softmax(logits, axis=-1) - onehot
    g_class = exact(d_logits.T, pooled_low.astype(F32))
    d_pre = exact(d_logits, w_class.astype(F32)) * (1.0 - pooled * pooled)
    d_leading = exact(d_pre, w_pool.astype(F32).T)
    d_out = cotangent.astype(F32) * slot_live[:, None]
    d_out = d_out.at[0].add(d_leading[0])
    d_h2, g_gain_two, g_shift_two = second_pull(d_out)
    d_branch = d_h2.astype(LOW)
    g_bias_down = jnp.sum(d_branch.astype(F32), axis=0)
    g_down_t = inner(d_branch, activated)
    d_activated = against(d_branch, w_down)
    d_up = gelu_pull(d_activated)[0].astype(LOW)
    g_bias_up = jnp.sum(d_up.astype(F32), axis=0)
    g_up_t = inner(d_up, norm_low)
    d_norm_one = d_h2 + against(d_up, w_up)
    d_h1, g_gain_one, g_shift_one = first_pull(d_norm_one)
    d_attn = d_h1.astype(LOW)
    g_bias_out = jnp.sum(d_attn.astype(F32), axis=0)
    g_out_t = inner(d_attn, context)
    d_context = against(d_attn, w_out).astype(LOW)
    d_packed = attention_back(packed, probs, d_context)
    g_qkv_t = inner(d_packed, tokens)
    column_sums = jnp.sum(d_packed.astype(F32), axis=0)
    grad_tokens = (d_h1 + against(d_packed, w_qkv)).astype(LOW)
    small = jnp.concatenate(
        [
            g_class,
            jnp.stack([column_sums[:D], column_sums[2 * D :], g_bias_out, g_shift_one, g_bias_down, g_shift_two]),
            jnp.stack([g_gain_one, g_gain_two]),
            g_bias_up.reshape(FF // D, D),
            d_pre,
        ]
    )
    lead = jnp.concatenate([leading.astype(F32), d_pre])
    down = owner_blocks(g_down_t, rest, FF)
    up = owner_blocks(g_up_t, rest, D)
    last = jnp.concatenate([owner_blocks(g_qkv_t, rest, D), owner_blocks(g_out_t, rest, D)], axis=4)
    half = up.shape[4] // 2
    parts = [
        down[..., : FF // 2], down[..., FF // 2 :],
        up[..., :half, :], up[..., half:, :],
        last[..., :half, :], last[..., half:, :],
    ]
    *sums, small, everyone = reduce_gradients(rest, parts, small, lead)
    g_down = jnp.concatenate(sums[0:2], axis=1).T
    g_up = jnp.concatenate(sums[2:4], axis=0).T
    g_last = jnp.concatenate(sums[4:6], axis=0).T
    own_qkv = 3 * D // (8 * rest)
    own = D // (8 * rest)
    everyone = everyone.reshape(8 * rest, 2, D)
    window = lax.dynamic_slice_in_dim(small, rank * own, own, axis=1)
    pre_window = lax.dynamic_slice_in_dim(everyone[:, 1], rank * own, own, axis=1)
    g_pool = lax.dot_general(
        everyone[:, 0], pre_window, (((0,), (0,)), ((), ())),
        precision=lax.Precision.HIGHEST, preferred_element_type=F32,
    )
    own_up = FF // (8 * rest)
    g_bias_up = lax.dynamic_slice_in_dim(small[11:15].reshape(FF), rank * own_up, own_up)
    return (
        out_full.astype(LOW),
        grad_tokens,
        losses,
        g_last[:, :own_qkv],
        g_last[:, own_qkv:],
        g_up,
        g_down,
        g_pool,
        window[:3],
        window[3:9],
        window[9:11],
        g_bias_up,
        window[15],
    )


def solution(mesh):
    return jax.shard_map(
        per_device,
        mesh=mesh,
        in_specs=(
            P(("batch", "head"), None),
            P(("batch", "head"), None),
            P("batch"),
            P("batch"),
            P(),
            P(),
            P(),
            P(),
            P(),
            P(),
            P(),
            P(),
            P(),
        ),
        out_specs=(
            P(("batch", "head"), None),
            P(("batch", "head"), None),
            P(("batch", "head")),
            P(None, ("batch", "head")),
            P(None, ("batch", "head")),
            P(None, ("batch", "head")),
            P(None, ("batch", "head")),
            P(None, ("batch", "head")),
            P(None, ("batch", "head")),
            P(None, ("batch", "head")),
            P(None, ("batch", "head")),
            P(("batch", "head")),
            P(("batch", "head")),
        ),
        check_vma=False,
    )
```
